128 devices in a mesh: gx: 32 (over x, y, core), gy: 4 (over z).
Axes of the slice: x: 4, y: 4, z: 4, core: 2. Of those that a mesh axis runs over, the one named last changes fastest.
Arguments:
- fluid_state: float32 [512, 32, 768], P('gx', 'gy'), may hold values from -4 to 4, as said below
- cell_counts: int32 [512, 32], P('gx', 'gy'), may hold values from 24 to 64
- wall_blocks: float32 [32768, 512], P(('gx', 'gy')), may hold values from -2.5 to 4, as said below
- readers: int32 [32768, 2], P(('gx', 'gy')), may hold values from 0 to 127, all different within a row; in each aligned block of 256 rows (0 to 255, 256 to 511, ...) at most 8 rows name the same one
- targets: int32 [32768, 2], P(('gx', 'gy')), may hold values from 0 to 127
Outputs:
- fluid_rates: float32 [512, 32, 256], P('gx', 'gy')
- density_rate: float32 [512, 2048], P('gx', 'gy')
The draws below stay inside these ranges and needn't reach their ends.
Inputs may be any that keep to these rules, and one draw needn't show every extreme that they name: The two readers of a wall block are different devices; among the wall blocks of one device at most 8 name the same reader. `fluid_state`: offsets x, y in [0, 1), depth in [0, 4), density in [0.97, 1.03], smoothing length in [0.3, 0.5], sound speed in [1, 2], mass in [0.04, 0.08], viscosity in [0.01, 0.04]. `wall_blocks`: wall positions x, y in [-0.2, 1.2], depth in [0, 4), Shepard correction in [0.5, 1].
All inputs are finite; a program needn't handle non-finite values.
Results may differ from the reference program's by a relative error of at most 0.0001.
Values sent between devices are 32-bit elements; how exact they have to be, the bound alone decides.
A program may use at most 64 MiB of HBM per device.

```python
import math
import jax
import jax.numpy as jnp
import numpy as np
from jax import lax

CX = 16
CY = 8
WALL_DEV = 256
MOST = 8
NCX = 512
NCY = 32
WALLS = 32768
N_GX = 32
N_GY = 4


def draw_fluid_state(key, part):
    keys = jax.random.split(key, 12)
    shape = (NCX, NCY, 64)
    offset_x = jax.random.uniform(keys[0], shape, jnp.float32, 0.0, 1.0)
    offset_y = jax.random.uniform(keys[1], shape, jnp.float32, 0.0, 1.0)
    depth = jax.random.uniform(keys[2], shape, jnp.float32, 0.0, 4.0)
    speeds = [0.5 * jnp.clip(jax.random.normal(keys[3 + k], shape, jnp.float32), -4.0, 4.0) for k in range(3)]
    warmth = jnp.clip(jax.random.normal(keys[11], shape, jnp.float32), -4.0, 4.0)
    mass = jax.random.uniform(keys[6], shape, jnp.float32, 0.04, 0.08)
    density = jax.random.uniform(keys[7], shape, jnp.float32, 0.97, 1.03)
    smooth = jax.random.uniform(keys[8], shape, jnp.float32, 0.3, 0.5)
    sound = jax.random.uniform(keys[9], shape, jnp.float32, 1.0, 2.0)
    viscous = jnp.exp(jax.random.uniform(keys[10], shape, jnp.float32, math.log(0.01), math.log(0.04)))
    fields = [offset_x, offset_y, depth] + speeds + [mass, density, smooth, sound, viscous, warmth]
    return jnp.stack(fields, axis=2).reshape(NCX, NCY, 768)


def draw_cell_counts(key, part):
    return jnp.minimum(jax.random.randint(key, (NCX, NCY), 24, 80), 64).astype(jnp.int32)


def draw_wall_blocks(key, part):
    keys = jax.random.split(key, 8)
    shape = (WALLS, 64)
    spot_x = jax.random.uniform(keys[0], shape, jnp.float32, -0.2, 1.2)
    spot_y = jax.random.uniform(keys[1], shape, jnp.float32, -0.2, 1.2)
    depth = jax.random.uniform(keys[2], shape, jnp.float32, 0.0, 4.0)
    normals = [jax.random.uniform(keys[3 + k], shape, jnp.float32, -1.0, 1.0) for k in range(3)]
    shepard = jax.random.uniform(keys[6], shape, jnp.float32, 0.5, 1.0)
    heat = jnp.clip(jax.random.normal(keys[7], shape, jnp.float32), -2.5, 2.5)
    fields = [spot_x, spot_y, depth] + normals + [shepard, heat]
    return jnp.stack(fields, axis=1).reshape(WALLS, 512)


def plant(drawn, rng, smallest, high):
    place = [jax.random.randint(jax.random.fold_in(rng, axis), (), 0, length) for axis, length in enumerate(drawn.shape)]
    widest = drawn.shape.index(max(drawn.shape))
    beside = place[:widest] + [(place[widest] + 1) % drawn.shape[widest]] + place[widest + 1:]
    return drawn.at[tuple(place)].set(smallest).at[tuple(beside)].set(high)


def routed_block(own_key, own, number, rows, number_of, top, limit, skew):
    ranking = jax.random.permutation(own_key, number_of)
    packed, common = shares(number_of, rows * top, limit, skew, True), shares(number_of, rows * top, limit, skew, False)
    places = jnp.arange(number_of)

    def named(tallies, turn):
        used = int((tallies > 0).sum())
        fixed = max(1, used // 4)
        moved = fixed + (places - fixed + turn * (used - fixed)) % max(1, number_of - fixed)
        return jnp.zeros((number_of,), jnp.int32).at[ranking[jnp.where(places < fixed, places, moved)]].set(jnp.asarray(tallies, jnp.int32))

    tallies = jnp.where(number % 4 == 0, named(packed, number // 4), named(common, number - number // 4 - 1))
    mixed = jax.random.permutation(jax.random.fold_in(own, 3), number_of)
    donor, receiver = mixed[0:number_of // 2 * 2:2], mixed[1:number_of // 2 * 2:2]
    room = jnp.minimum(tallies[donor] - 1, limit - tallies[receiver]) // 2
    room = jnp.where((donor == ranking[0]) | (receiver == ranking[0]) | (tallies[receiver] == 0), 0, jnp.maximum(room, 0))
    moved = jax.random.randint(jax.random.fold_in(own, 4), (number_of // 2,), 0, 1 << 20) % (room + 1)
    tallies = tallies.at[donor].add(-moved).at[receiver].add(moved)
    members = jnp.searchsorted(jnp.cumsum(tallies), jnp.arange(rows * top), side="right").astype(jnp.int32)
    listing = members.reshape(top, rows).T
    listing = listing[jax.random.permutation(jax.random.fold_in(own, 1), rows)]
    turn = jax.random.randint(jax.random.fold_in(own, 2), (rows, 1), 0, top)
    return jnp.take_along_axis(listing, (jnp.arange(top)[None, :] + turn) % top, axis=1)


def shares(number_of, total, most, slope, full):
    loads = [(1 << 20) // math.isqrt(grade ** slope) + 1 for grade in range(1, number_of + 1)]
    largest = most if full else min(most, max(-(-total // number_of), total * loads[0] // sum(loads)))
    least = 1 if total - largest >= number_of - 1 else 0
    given, spare = [largest] + [least] * (number_of - 1), total - largest - least * (number_of - 1)
    while spare > 0:
        free = [i for i in range(1, number_of) if given[i] < largest] or [i for i in range(1, number_of) if given[i] < most]
        whole, budget = sum([loads[i] for i in free]), spare
        for i in free:
            extra = min(most - given[i], max(1, budget * loads[i] // whole), spare)
            given[i] = given[i] + extra
            spare = spare - extra
    return np.array(given)


def setup_inputs(seed: int = 0) -> dict:
    key_list = jax.random.split(jax.random.key(seed), 6)
    fluid_state = draw_fluid_state(jax.random.fold_in(key_list[5], 71), 0)
    cell_counts = draw_cell_counts(jax.random.fold_in(key_list[5], 71), 0)
    wall_blocks = draw_wall_blocks(jax.random.fold_in(key_list[5], 71), 0)
    readers_keys = jax.random.split(jax.random.fold_in(key_list[3], 1), WALLS // WALL_DEV)
    readers_turns = jax.random.permutation(jax.random.fold_in(key_list[3], 3), WALLS // WALL_DEV)
    readers = jax.vmap(lambda own, number: routed_block(jax.random.fold_in(key_list[3], 2), own, number, WALL_DEV, N_GX * N_GY, 2, MOST, 2))(readers_keys, readers_turns).reshape((WALLS, 2))
    targets = plant(jax.random.randint(key_list[4], (WALLS, 2), 0, CX * CY), jax.random.fold_in(key_list[4], 1), 0, (CX * CY) - 1).astype(jnp.int32)
    return dict(fluid_state=fluid_state, cell_counts=cell_counts, wall_blocks=wall_blocks, readers=readers, targets=targets)


KERN_W = 21.0 / (16.0 * math.pi)
KERN_F = 105.0 / (16.0 * math.pi)
KAPPA = 0.02
WALL_PUSH = 0.03
WALL_HEAT = 0.02
EPS_R = 0.01

def pair_records(fluid_state, cell_counts):
    comps = fluid_state.reshape(fluid_state.shape[:-1] + (12, 64))
    alive = (jnp.arange(64, dtype=jnp.int32) < cell_counts[..., None]).astype(fluid_state.dtype)
    density = comps[..., 7, :]
    inverse = 1.0 / density
    sound = comps[..., 9, :]
    pressure = sound * sound / 7.0 * (density ** 7 - 1.0)
    fields = [comps[..., k, :] for k in range(6)]
    fields = fields + [comps[..., 6, :] * alive, pressure * inverse * inverse, comps[..., 10, :] * inverse, inverse, comps[..., 8, :], comps[..., 11, :]]
    return jnp.stack(fields, axis=-2).reshape(fluid_state.shape)

def pair_sums(center, neighbour, shift_x, shift_y):
    near = [center[..., k, :, None] for k in range(12)]
    far = [neighbour[..., k, None, :] for k in range(12)]
    delta_x = near[0] - far[0] - shift_x
    delta_y = near[1] - far[1] - shift_y
    delta_z = near[2] - far[2]
    dist_sq = delta_x * delta_x + delta_y * delta_y + delta_z * delta_z
    smooth = 0.5 * (near[10] + far[10])
    ratio = jnp.sqrt(dist_sq) / smooth
    shell = jnp.maximum(1.0 - 0.5 * ratio, 0.0)
    weighted = far[6] * -KERN_F * shell * shell * shell / smooth ** 5
    damping = dist_sq / (dist_sq + EPS_R * smooth * smooth)
    diff_u = near[3] - far[3]
    diff_v = near[4] - far[4]
    diff_w = near[5] - far[5]
    density_rate = lax.optimization_barrier(jnp.sum(weighted * (diff_u * delta_x + diff_v * delta_y + diff_w * delta_z), axis=-1))
    pressure = near[7] + far[7]
    viscous = (near[8] * far[9] + far[8] * near[9]) * damping
    accel_x = lax.optimization_barrier(jnp.sum(weighted * (viscous * diff_u - pressure * delta_x), axis=-1))
    accel_y = lax.optimization_barrier(jnp.sum(weighted * (viscous * diff_v - pressure * delta_y), axis=-1))
    accel_z = lax.optimization_barrier(jnp.sum(weighted * (viscous * diff_w - pressure * delta_z), axis=-1))
    heating = lax.optimization_barrier(jnp.sum(weighted * (2.0 * KAPPA) * near[9] * far[9] * damping * (near[11] - far[11]), axis=-1))
    return jnp.stack([density_rate, accel_x, accel_y, accel_z, heating], axis=-2)

def neighbour_terms(center, extended):
    rows_a = center.shape[0]
    rows_b = center.shape[1]
    middle = center.reshape(rows_a, rows_b, 12, 64)
    totals = jnp.zeros((rows_a, rows_b, 5, 64), jnp.float32)
    for shift_x in (-1, 0, 1):
        for shift_y in (-1, 0, 1):
            beside = extended[1 + shift_x:1 + shift_x + rows_a, 1 + shift_y:1 + shift_y + rows_b]
            totals = totals + pair_sums(middle, beside.reshape(rows_a, rows_b, 12, 64), float(shift_x), float(shift_y))
    return totals

def wall_terms(cell_rows, wall_rows):
    count = cell_rows.shape[0]
    fluid_part = cell_rows.reshape(count, 12, 64)
    wall_part = wall_rows.reshape(count, 8, 64)
    delta_x = fluid_part[:, 0, :, None] - wall_part[:, 0, None, :]
    delta_y = fluid_part[:, 1, :, None] - wall_part[:, 1, None, :]
    delta_z = fluid_part[:, 2, :, None] - wall_part[:, 2, None, :]
    smooth = fluid_part[:, 8, :, None]
    ratio = jnp.sqrt(delta_x * delta_x + delta_y * delta_y + delta_z * delta_z) / smooth
    shell = jnp.maximum(1.0 - 0.5 * ratio, 0.0)
    kernel = KERN_W * shell ** 4 * (2.0 * ratio + 1.0) / (smooth * smooth * smooth)
    corrected = wall_part[:, 6, None, :] * kernel
    sound = fluid_part[:, 9, :]
    push = WALL_PUSH * sound * sound
    force_x = push * lax.optimization_barrier(jnp.sum(corrected * wall_part[:, 3, None, :], axis=-1))
    force_y = push * lax.optimization_barrier(jnp.sum(corrected * wall_part[:, 4, None, :], axis=-1))
    force_z = push * lax.optimization_barrier(jnp.sum(corrected * wall_part[:, 5, None, :], axis=-1))
    heating = WALL_HEAT * lax.optimization_barrier(jnp.sum(corrected * (wall_part[:, 7, None, :] - fluid_part[:, 11, :, None]), axis=-1))
    return jnp.stack([force_x, force_y, force_z, heating], axis=1).reshape(count, 256)

def finish(fluid_terms, wall_sum):
    rows_a = fluid_terms.shape[0]
    rows_b = fluid_terms.shape[1]
    walled = wall_sum.reshape(rows_a, rows_b, 4, 64)
    rates = (fluid_terms[:, :, 1:, :] + walled).reshape(rows_a, rows_b, 256)
    density = fluid_terms[:, :, 0, :].reshape(rows_a, rows_b * 64)
    return (rates, density)

def reference(fluid_state, cell_counts, wall_blocks, readers, targets):
    records = pair_records(fluid_state, cell_counts)
    padded = jnp.pad(records, ((1, 1), (1, 1), (0, 0)))

    def one_row(row_index):
        extended = lax.dynamic_slice_in_dim(padded, row_index, 3, 0)
        return neighbour_terms(extended[1:2, 1:-1], extended)[0]
    fluid_terms = lax.map(one_row, jnp.arange(NCX, dtype=jnp.int32))
    device = readers.reshape(-1)
    local_cell = targets.reshape(-1)
    row = device // N_GY * CX + local_cell // CY
    column = device % N_GY * CY + local_cell % CY
    flat = (row * NCY + column).astype(jnp.int32)
    flat_fluid = fluid_state.reshape(NCX * NCY, 768)
    copies = jnp.repeat(wall_blocks, 2, axis=0)

    def one_block(pieces):
        return wall_terms(flat_fluid[pieces[0]], pieces[1])
    contrib = lax.map(one_block, (flat.reshape(-1, 512), copies.reshape(-1, 512, 512)))
    wall_sum = jnp.zeros((NCX * NCY, 256), jnp.float32).at[flat].add(contrib.reshape(-1, 256))
    rates, density = finish(fluid_terms, wall_sum)
    return (rates, density)
```

```python
import math

import jax
import jax.numpy as jnp
from jax import lax
from jax.experimental import pallas as pl
from jax.experimental.pallas import tpu as pltpu
from jax.sharding import PartitionSpec as P

CA = 16
CB = 8
PAIRS = 4
SLOTS = 8
KERN_W = 21.0 / (16.0 * math.pi)
KERN_F = 105.0 / (16.0 * math.pi)
KAPPA = 0.02
WALL_PUSH = 0.03
WALL_HEAT = 0.02
EPS_R = 0.01
F32 = jnp.float32
BF16 = jnp.bfloat16


def iota(shape, axis):
    return lax.broadcasted_iota(jnp.int32, shape, axis)


def split2(value):
    high = value.astype(BF16)
    low = (value - high.astype(F32)).astype(BF16)
    return high, low


def split3(value):
    high = value.astype(BF16).astype(F32)
    rest = value - high
    middle = rest.astype(BF16).astype(F32)
    return high, middle, rest - middle


def pack_kernel(counts_ref, fluid_ref, out_ref):
    lane = iota((8, 128), 1)
    left = lane < 64
    slot = lane - jnp.where(left, 0, 64)

    def row(a, carry):
        comps = []
        for v in range(6):
            x = fluid_ref[a, :, v * 128 : (v + 1) * 128]
            turned = pltpu.roll(x, 64, 1)
            comps.append(jnp.where(left, x, pltpu.roll(turned, 7, 0)))
            comps.append(jnp.where(left, turned, pltpu.roll(x, 7, 0)))
        density, smooth, sound = comps[7], comps[8], comps[9]
        inverse = 1.0 / density
        d2 = density * density
        d4 = d2 * d2
        pressure = sound * sound / 7.0 * (d4 * d2 * density - 1.0)
        fields = comps[:6] + [
            comps[6],
            pressure * inverse * inverse,
            comps[10] * inverse,
            inverse,
            smooth,
            comps[11],
            sound,
        ]
        for p in range(PAIRS):
            count = jnp.where(left[:1], counts_ref[2 * p, a], counts_ref[2 * p + 1, a])
            for c, field in enumerate(fields):
                line = field[2 * p : 2 * p + 1]
                if c == 6:
                    line = jnp.where(slot[:1] < count, line, 0.0)
                out_ref[a, p, c : c + 1, :] = line
            out_ref[a, p, 13:16, :] = jnp.zeros((3, 128), F32)
        return carry

    lax.fori_loop(0, CA, row, 0)


def pack_records(fluid_state, counts_t):
    return pl.pallas_call(
        pack_kernel,
        out_shape=jax.ShapeDtypeStruct((CA, PAIRS, 16, 128), F32),
        in_specs=[
            pl.BlockSpec(memory_space=pltpu.SMEM),
            pl.BlockSpec(memory_space=pltpu.VMEM),
        ],
        out_specs=pl.BlockSpec(memory_space=pltpu.VMEM),
        name="pack_records",
    )(counts_t, fluid_state)


def route_kernel(devices, wall_ref, readers_ref, targets_ref, out_ref, sel_ref, rhs_ref):
    rows = wall_ref.shape[0]
    lane = iota((rows, 128), 1)
    left = lane < 64
    later = (iota((rows, rows), 0) < iota((rows, rows), 1)).astype(BF16)
    device = iota((devices, rows), 0)
    before = jnp.zeros((devices, 1), F32)
    slots = []
    cells = jnp.zeros((devices, 128), F32)
    slot_row = iota((128, rows), 0).astype(F32)
    for r in range(2):
        reader = readers_ref[r : r + 1, :]
        hot = (device == reader).astype(F32)
        earlier = jnp.dot(hot.astype(BF16), later, preferred_element_type=F32) + before
        position = jnp.sum(hot * earlier, axis=0, keepdims=True)
        before = before + jnp.sum(hot, axis=1, keepdims=True)
        slots.append(reader * SLOTS + position.astype(jnp.int32))
        named = jnp.where(slot_row == position, targets_ref[r : r + 1, :].astype(F32), 0.0)
        named = jnp.where(slot_row == SLOTS, 1.0, named)
        cells = cells + lax.dot_general(
            hot.astype(BF16),
            named.astype(BF16),
            (((1,), (1,)), ((), ())),
            preferred_element_type=F32,
        )
    chunk = devices * SLOTS // 2
    pair = iota((chunk, rows), 0) * 2
    for half in range(2):
        chosen = (pair + half == slots[0]) | (pair + half == slots[1])
        sel_ref[:, half * rows : (half + 1) * rows] = jnp.where(chosen, 1.0, 0.0).astype(BF16)
    gamma = wall_ref[:, 384:512]
    gamma = jnp.where(left, gamma, pltpu.roll(gamma, 64, 1))
    for v in range(4):
        x = wall_ref[:, v * 128 : (v + 1) * 128]
        if v == 1:
            x = jnp.where(left, x, x * gamma)
        elif v == 2:
            x = x * gamma
        elif v == 3:
            x = jnp.where(left, x, x * gamma)
        turned = pltpu.roll(x, 64, 1)
        for odd in range(2):
            even_half = jnp.where(left, turned if odd else x, 0.0)
            odd_half = jnp.where(left, 0.0, x if odd else turned)
            for part, (e, o) in enumerate(zip(split3(even_half), split3(odd_half))):
                rhs_ref[0:rows, part * 128 : (part + 1) * 128] = e.astype(BF16)
                rhs_ref[rows : 2 * rows, part * 128 : (part + 1) * 128] = o.astype(BF16)
            got = jnp.dot(sel_ref[...], rhs_ref[...], preferred_element_type=F32)
            got = got[:, 0:128] + got[:, 128:256] + got[:, 256:384]
            got = got.reshape(devices, SLOTS // 2, 128)
            for q in range(SLOTS // 2):
                out_ref[:, q * 8 + 2 * v + odd, :] = got[:, q, :]
    for k in range(8):
        out_ref[:, 32 + k, :] = cells


def route_walls(devices, wall_blocks, readers_t, targets_t):
    rows = wall_blocks.shape[0]
    return pl.pallas_call(
        lambda *refs: route_kernel(devices, *refs),
        out_shape=jax.ShapeDtypeStruct((devices, 40, 128), F32),
        in_specs=[pl.BlockSpec(memory_space=pltpu.VMEM)] * 3,
        out_specs=pl.BlockSpec(memory_space=pltpu.VMEM),
        scratch_shapes=[
            pltpu.VMEM((devices * SLOTS // 2, 2 * rows), BF16),
            pltpu.VMEM((2 * rows, 384), BF16),
        ],
        compiler_params=pltpu.CompilerParams(vmem_limit_bytes=40 << 20),
        name="route_walls",
    )(wall_blocks, readers_t, targets_t)


def features(tile, left):
    x = tile[0:1] - 0.5
    y = tile[1:2] + jnp.where(left, -1.0, 0.0)
    z = tile[2:3] - 2.0
    u, v, w = tile[3:4], tile[4:5], tile[5:6]
    mass = tile[6:7] * (-32.0 * KERN_F)
    mp = mass * tile[7:8]
    mv = mass * tile[8:9]
    mi = mass * tile[9:10]
    heat = tile[11:12]
    mu, mvv, mw = mass * u, mass * v, mass * w
    first = [mass, mp, mu, mass, mp, mvv, mw, mass * z]
    second = [mass * x, mp * x, mu * x, mass * y, mp * y, mvv * y, mp * z, mw * z]
    third = [mi, mi * u, mi * v, mi * w, mi * heat, mv, mv * u, mv * v]
    fourth = [mv * w] + [jnp.zeros_like(x)] * 7
    return (
        jnp.concatenate(first + second, axis=0),
        jnp.concatenate(third + fourth, axis=0),
        jnp.concatenate([x, y, z, tile[10:11]] + [jnp.zeros_like(x)] * 4, axis=0),
    )


def near_kernel(ext_ref, out_ref, feat_ref, turn_ref, am_ref, bm_ref, ax_ref, bx_ref):
    left1 = iota((1, 128), 1) < 64
    left16 = iota((16, 128), 1) < 64

    def prepare(k, carry):
        a = k // 6
        p = k - a * 6
        fa, fb, pos = features(ext_ref[a, p], left1)
        for variant in range(3):
            if variant == 0:
                va, vb = fa, fb
            else:
                ta, tb = pltpu.roll(fa, 64, 1), pltpu.roll(fb, 64, 1)
                keep = left16 if variant == 1 else jnp.logical_not(left16)
                va, vb = jnp.where(keep, fa, ta), jnp.where(keep, fb, tb)
            ha, la = split2(va)
            hb, lb = split2(vb)
            feat_ref[a, p, variant, 0:16, :] = ha
            feat_ref[a, p, variant, 16:32, :] = la
            feat_ref[a, p, variant, 32:48, :] = hb
            feat_ref[a, p, variant, 48:64, :] = lb
        turn_ref[a, p] = pos.T
        return carry

    lax.fori_loop(0, 18 * 6, prepare, 0)

    rows8 = iota((8, 128), 0)

    def kernel_rows(xi, yi, zi, hi, xj, yj, zj, hj):
        dx = xi - xj
        dy = yi - yj
        dz = zi - zj
        s = dx * dx + dy * dy + dz * dz
        wide = hi + hj
        w2 = wide * wide
        e = s + (0.25 * EPS_R) * w2
        w4 = w2 * w2
        den = w4 * w4 * e
        r = s * lax.rsqrt(jnp.maximum(s, 1e-30))
        shell = jnp.maximum(wide - r, 0.0)
        base = shell * shell * shell / den
        return split2(base * e), split2(base * s)

    def pair(k, carry):
        a = k // PAIRS
        p = k - a * PAIRS
        tile = ext_ref[a + 1, p + 1]
        x0 = tile[0:1] - 0.5
        yi = tile[1:2] + jnp.where(left1, -1.0, 0.0)
        zi = tile[2:3] - 2.0
        hi = tile[10:11]
        y_mixed = yi + jnp.where(left1, 2.0, -2.0)
        sums = [jnp.zeros((8, 128), F32) for _ in range(4)]
        for sx in (-1, 0, 1):
            r = a + 1 + sx
            xi = x0 - float(sx)
            for c in range(8):
                rows = pl.ds(c * 16, 16)
                t = turn_ref[r, p + 1, rows, :]
                (ah, al), (bh, bl) = kernel_rows(
                    xi, yi, zi, hi, t[:, 0:1], t[:, 1:2], t[:, 2:3], t[:, 3:4]
                )
                am_ref[sx + 1, c * 16 : c * 16 + 16, :] = ah
                am_ref[sx + 1, 128 + c * 16 : 144 + c * 16, :] = al
                bm_ref[sx + 1, c * 16 : c * 16 + 16, :] = bh
                bm_ref[sx + 1, 128 + c * 16 : 144 + c * 16, :] = bl
            for c in range(4):
                tl = turn_ref[r, p, pl.ds(64 + c * 16, 16), :]
                tr = turn_ref[r, p + 2, pl.ds(c * 16, 16), :]
                mixed = [jnp.where(left16, tl[:, n : n + 1], tr[:, n : n + 1]) for n in range(4)]
                (ah, al), (bh, bl) = kernel_rows(xi, y_mixed, zi, hi, *mixed)
                ax_ref[sx + 1, c * 16 : c * 16 + 16, :] = ah
                ax_ref[sx + 1, 64 + c * 16 : 80 + c * 16, :] = al
                bx_ref[sx + 1, c * 16 : c * 16 + 16, :] = bh
                bx_ref[sx + 1, 64 + c * 16 : 80 + c * 16, :] = bl
            mid = feat_ref[r, p + 1, 0]
            fa = jnp.concatenate([mid[0:32], mid[0:32]], axis=1)
            fb = jnp.concatenate([mid[32:64], mid[32:64]], axis=1)
            ga = jnp.dot(fa, am_ref[sx + 1], preferred_element_type=F32)
            gb = jnp.dot(fb, bm_ref[sx + 1], preferred_element_type=F32)
            side_l = feat_ref[r, p, 2]
            side_r = feat_ref[r, p + 2, 1]
            xa = jnp.dot(
                jnp.concatenate([side_l[0:32], side_r[0:32]], axis=0),
                ax_ref[sx + 1],
                preferred_element_type=F32,
            )
            xb = jnp.dot(
                jnp.concatenate([side_l[32:64], side_r[32:64]], axis=0),
                bx_ref[sx + 1],
                preferred_element_type=F32,
            )
            ga = ga[0:16] + ga[16:32]
            gb = gb[0:16] + gb[16:32]
            xa = jnp.where(left16, xa[0:16] + xa[16:32], xa[32:48] + xa[48:64])
            xb = jnp.where(left16, xb[0:16] + xb[16:32], xb[32:48] + xb[48:64])
            by_x = jnp.where(rows8 < 3, float(sx), 0.0)
            by_y = jnp.where((rows8 >= 3) & (rows8 < 6), jnp.where(left1, -2.0, 2.0), 0.0)
            sums[0] = sums[0] + (ga[0:8] + xa[0:8])
            sums[1] = sums[1] + (ga[8:16] + xa[8:16] + by_y * xa[0:8])
            if sx:
                sums[1] = sums[1] + by_x * (ga[0:8] + xa[0:8])
            sums[2] = sums[2] + (gb[0:8] + xb[0:8])
            sums[3] = sums[3] + (gb[8:16] + xb[8:16])
        v0, v1, v2, v3 = sums
        u, v, w = tile[3:4], tile[4:5], tile[5:6]
        sm, smp = v0[0:1], v0[1:2]
        gx = x0 * sm - v1[0:1]
        gy = yi * sm - v1[3:4]
        gz = zi * sm - v0[7:8]
        density = (
            u * gx
            - (x0 * v0[2:3] - v1[2:3])
            + v * gy
            - (yi * v0[5:6] - v1[5:6])
            + w * gz
            - (zi * v0[6:7] - v1[7:8])
        )
        pi, visc, inv = tile[7:8], tile[8:9], tile[9:10]
        smi, smv = v2[0:1], v2[5:6]
        ax = visc * (u * smi - v2[1:2]) + inv * (u * smv - v2[6:7])
        ay = visc * (v * smi - v2[2:3]) + inv * (v * smv - v2[7:8])
        az = visc * (w * smi - v2[3:4]) + inv * (w * smv - v3[0:1])
        ax = ax - (pi * gx + (x0 * smp - v1[1:2]))
        ay = ay - (pi * gy + (yi * smp - v1[4:5]))
        az = az - (pi * gz + (zi * smp - v1[6:7]))
        heat = (2.0 * KAPPA) * inv * (tile[11:12] * smi - v2[4:5])
        out_ref[a, p, 0:1, :] = density
        out_ref[a, p, 1:2, :] = ax
        out_ref[a, p, 2:3, :] = ay
        out_ref[a, p, 3:4, :] = az
        out_ref[a, p, 4:5, :] = heat
        out_ref[a, p, 5:8, :] = jnp.zeros((3, 128), F32)
        return carry

    lax.fori_loop(0, CA * PAIRS, pair, 0)


def near_terms(ext):
    return pl.pallas_call(
        near_kernel,
        out_shape=jax.ShapeDtypeStruct((CA, PAIRS, 8, 128), F32),
        in_specs=[pl.BlockSpec(memory_space=pltpu.VMEM)],
        out_specs=pl.BlockSpec(memory_space=pltpu.VMEM),
        scratch_shapes=[
            pltpu.VMEM((18, 6, 3, 64, 128), BF16),
            pltpu.VMEM((18, 6, 128, 8), F32),
            pltpu.VMEM((3, 256, 128), BF16),
            pltpu.VMEM((3, 256, 128), BF16),
            pltpu.VMEM((3, 128, 128), BF16),
            pltpu.VMEM((3, 128, 128), BF16),
        ],
        compiler_params=pltpu.CompilerParams(vmem_limit_bytes=48 << 20),
        name="near_terms",
    )(ext)


def wall_kernel(cells_ref, recv_ref, rec_ref, near_ref, rates_ref, dens_ref, lhs_ref, acc_ref):
    lane1 = iota((1, 128), 1)
    left1 = lane1 < 64
    row8 = iota((8, 128), 0)
    left8 = iota((8, 128), 1) < 64
    left16 = iota((16, 128), 1) < 64

    def cell_features(k, carry):
        a = k // PAIRS
        p = k - a * PAIRS
        tile = rec_ref[a, p]
        x = tile[0:1] - 0.5
        y = tile[1:2] - 0.5
        z = tile[2:3] - 2.0
        h = tile[10:11]
        s = 0.25 / (h * h)
        zero = jnp.zeros_like(x)
        rows = jnp.concatenate(
            [-2.0 * s * x, -2.0 * s * y, -2.0 * s * z, s, s * (x * x + y * y + z * z)] + [zero] * 3,
            axis=0,
        )
        hi, mid, lo = split3(rows)
        pad = jnp.zeros((16, 128), F32)
        stack = jnp.concatenate([hi, hi, mid, hi, mid, lo, pad], axis=0)
        both = jnp.concatenate([stack, stack], axis=0).T
        first = iota((128, 128), 1) < 64
        lhs_ref[2 * k, 0] = jnp.where(first[:64], both[:64], 0.0).astype(BF16)
        lhs_ref[2 * k, 1] = jnp.where(first[:64], 0.0, both[:64]).astype(BF16)
        lhs_ref[2 * k + 1, 0] = jnp.where(first[64:], both[64:], 0.0).astype(BF16)
        lhs_ref[2 * k + 1, 1] = jnp.where(first[64:], 0.0, both[64:]).astype(BF16)
        acc_ref[2 * k] = jnp.zeros((8, 128), F32)
        acc_ref[2 * k + 1] = jnp.zeros((8, 128), F32)
        return carry

    lax.fori_loop(0, CA * PAIRS, cell_features, 0)

    center = jnp.where(row8 == 2, 2.0, 0.5)

    def slot_pair(src, q):
        ca = cells_ref[src * 16 + 2 * q]
        cb = cells_ref[src * 16 + 2 * q + 1]
        tile = recv_ref[src, q * 8 : q * 8 + 8, :]
        c = tile - center
        sq = c * c
        norm = pltpu.roll(sq, 1, 0) + pltpu.roll(sq, 2, 0) + pltpu.roll(sq, 3, 0)
        rows = jnp.where(
            row8 < 3, c, jnp.where(row8 == 3, norm, jnp.where(row8 == 4, 1.0, 0.0))
        )
        hi, mid, lo = split3(rows)
        blocks = []
        for side in range(2):
            keep = left8 if side == 0 else jnp.logical_not(left8)
            h1, m1, l1 = [jnp.where(keep, t, 0.0) for t in (hi, mid, lo)]
            for top, bottom in ((h1, m1), (h1, l1), (m1, h1)):
                blocks.append(jnp.concatenate([top, bottom], axis=0).astype(BF16))
            blocks.append(jnp.zeros((16, 128), BF16))
        right = jnp.concatenate(blocks, axis=0)
        lhs = lhs_ref[ca, 0] + lhs_ref[cb, 1]
        q2 = jnp.maximum(jnp.dot(lhs, right, preferred_element_type=F32), 1e-30)
        t = q2 * lax.rsqrt(q2)
        shell = jnp.maximum(1.0 - t, 0.0)
        shell = shell * shell
        kernel = shell * shell * (4.0 * t + 1.0)
        kh, kl = split2(kernel)
        give = jnp.where(row8 < 3, 0.0, tile)
        gh, gl = split2(give)
        gh, gl = gh.astype(F32), gl.astype(F32)
        zero = jnp.zeros_like(gh)
        feats = jnp.concatenate(
            [
                jnp.concatenate([jnp.where(left8, gh, zero), jnp.where(left8, gl, zero)], axis=0),
                jnp.concatenate([jnp.where(left8, zero, gh), jnp.where(left8, zero, gl)], axis=0),
            ],
            axis=0,
        ).astype(BF16)
        got = lax.dot_general(
            feats,
            jnp.concatenate([kh, kl], axis=0),
            (((1,), (1,)), ((), ())),
            preferred_element_type=F32,
        )
        acc_ref[ca] = acc_ref[ca] + (got[0:8] + got[8:16])
        acc_ref[cb] = acc_ref[cb] + (got[16:24] + got[24:32])

    def source(src, carry):
        for q in range(SLOTS // 2):
            slot_pair(src, q)
        return carry

    lax.fori_loop(0, recv_ref.shape[0], source, 0)

    def finish(a, carry):
        for p in range(PAIRS):
            ta = acc_ref[a * CB + 2 * p]
            tb = acc_ref[a * CB + 2 * p + 1]
            total = jnp.where(left8, ta + pltpu.roll(ta, 64, 1), tb + pltpu.roll(tb, 64, 1))
            tile = rec_ref[a, p]
            near = near_ref[a, p]
            h, sound = tile[10:11], tile[12:13]
            scale = KERN_W / (h * h * h)
            push = WALL_PUSH * sound * sound * scale
            heat = WALL_HEAT * scale * (total[7:8] - tile[11:12] * total[6:7])
            r = [near[1 + n : 2 + n] + push * total[3 + n : 4 + n] for n in range(3)]
            r.append(near[4:5] + heat)
            t = [pltpu.roll(line, 64, 1) for line in r]
            for v in range(2):
                lo, hi = 2 * v, 2 * v + 1
                span = slice(v * 128, (v + 1) * 128)
                rates_ref[a, 2 * p : 2 * p + 1, span] = jnp.where(left1, r[lo], t[hi])
                rates_ref[a, 2 * p + 1 : 2 * p + 2, span] = jnp.where(left1, t[lo], r[hi])
            dens_ref[a, p : p + 1, :] = near[0:1]
        return carry

    lax.fori_loop(0, CA, finish, 0)


def wall_terms(cells, recv, records, near):
    return pl.pallas_call(
        wall_kernel,
        out_shape=(
            jax.ShapeDtypeStruct((CA, CB, 256), F32),
            jax.ShapeDtypeStruct((CA, PAIRS, 128), F32),
        ),
        in_specs=[pl.BlockSpec(memory_space=pltpu.SMEM)]
        + [pl.BlockSpec(memory_space=pltpu.VMEM)] * 3,
        out_specs=[pl.BlockSpec(memory_space=pltpu.VMEM)] * 2,
        scratch_shapes=[
            pltpu.VMEM((CA * CB, 2, 64, 128), BF16),
            pltpu.VMEM((CA * CB, 8, 128), F32),
        ],
        compiler_params=pltpu.CompilerParams(vmem_limit_bytes=48 << 20),
        name="wall_terms",
    )(cells, recv, records, near)


def shift_from(array, axis, step):
    peers = lax.axis_size(axis)
    up = [(i, i + 1) for i in range(peers - 1)]
    pairs = up if step > 0 else [(j, i) for i, j in up]
    return lax.ppermute(array, axis, pairs)


def local(fluid_state, cell_counts, wall_blocks, readers, targets):
    devices = lax.axis_size("gx") * lax.axis_size("gy")
    records = pack_records(fluid_state, cell_counts.T)
    send = route_walls(devices, wall_blocks, readers.T, targets.T)
    before = shift_from(records[:, PAIRS - 1 :], "gy", 1)
    after = shift_from(records[:, :1], "gy", -1)
    wide = jnp.concatenate([before, records, after], axis=1)
    above = shift_from(wide[CA - 1 :], "gx", 1)
    below = shift_from(wide[:1], "gx", -1)
    ext = jnp.concatenate([above, wide, below], axis=0)
    recv = lax.all_to_all(send, ("gx", "gy"), split_axis=0, concat_axis=0, tiled=True)
    cells = recv[:, 32, :16].astype(jnp.int32).reshape(-1)
    near = near_terms(ext)
    rates, density = wall_terms(cells, recv, records, near)
    return (rates, density.reshape(CA, CB * 64))


def solution(mesh):
    placed = (
        P("gx", "gy", None),
        P("gx", "gy"),
        P(("gx", "gy"), None),
        P(("gx", "gy"), None),
        P(("gx", "gy"), None),
    )
    return jax.shard_map(
        local,
        mesh=mesh,
        in_specs=placed,
        out_specs=(P("gx", "gy", None), P("gx", "gy")),
        check_vma=False,
    )
```

```python
import math

import jax
import jax.numpy as jnp
from jax import lax
from jax.experimental import pallas as pl
from jax.experimental.pallas import tpu as pltpu
from jax.sharding import PartitionSpec as P

CA = 16
CB = 8
PAIRS = 4
SLOTS = 8
KERN_W = 21.0 / (16.0 * math.pi)
KERN_F = 105.0 / (16.0 * math.pi)
KAPPA = 0.02
WALL_PUSH = 0.03
WALL_HEAT = 0.02
EPS_R = 0.01
F32 = jnp.float32
BF16 = jnp.bfloat16


def iota(shape, axis):
    return lax.broadcasted_iota(jnp.int32, shape, axis)


def split2(value):
    high = value.astype(BF16)
    low = (value - high.astype(F32)).astype(BF16)
    return high, low


def split3(value):
    high = value.astype(BF16).astype(F32)
    rest = value - high
    middle = rest.astype(BF16).astype(F32)
    return high, middle, rest - middle


def pack_kernel(counts_ref, fluid_ref, out_ref):
    lane = iota((8, 128), 1)
    left = lane < 64
    slot = lane - jnp.where(left, 0, 64)

    def row(a, carry):
        comps = []
        for v in range(6):
            x = fluid_ref[a, :, v * 128 : (v + 1) * 128]
            turned = pltpu.roll(x, 64, 1)
            comps.append(jnp.where(left, x, pltpu.roll(turned, 7, 0)))
            comps.append(jnp.where(left, turned, pltpu.roll(x, 7, 0)))
        density, smooth, sound = comps[7], comps[8], comps[9]
        inverse = 1.0 / density
        d2 = density * density
        d4 = d2 * d2
        pressure = sound * sound / 7.0 * (d4 * d2 * density - 1.0)
        fields = comps[:6] + [
            comps[6],
            pressure * inverse * inverse,
            comps[10] * inverse,
            inverse,
            smooth,
            comps[11],
            sound,
        ]
        for p in range(PAIRS):
            count = jnp.where(left[:1], counts_ref[2 * p, a], counts_ref[2 * p + 1, a])
            for c, field in enumerate(fields):
                line = field[2 * p : 2 * p + 1]
                if c == 6:
                    line = jnp.where(slot[:1] < count, line, 0.0)
                out_ref[a, p, c : c + 1, :] = line
            out_ref[a, p, 13:16, :] = jnp.zeros((3, 128), F32)
        return carry

    lax.fori_loop(0, CA, row, 0)


def pack_records(fluid_state, counts_t):
    return pl.pallas_call(
        pack_kernel,
        out_shape=jax.ShapeDtypeStruct((CA, PAIRS, 16, 128), F32),
        in_specs=[
            pl.BlockSpec(memory_space=pltpu.SMEM),
            pl.BlockSpec(memory_space=pltpu.VMEM),
        ],
        out_specs=pl.BlockSpec(memory_space=pltpu.VMEM),
        name="pack_records",
    )(counts_t, fluid_state)


def route_kernel(devices, wall_ref, readers_ref, targets_ref, out_ref, sel_ref, rhs_ref):
    rows = wall_ref.shape[0]
    lane = iota((rows, 128), 1)
    left = lane < 64
    later = (iota((rows, rows), 0) < iota((rows, rows), 1)).astype(BF16)
    device = iota((devices, rows), 0)
    before = jnp.zeros((devices, 1), F32)
    slots = []
    cells = jnp.zeros((devices, 128), F32)
    slot_row = iota((128, rows), 0).astype(F32)
    for r in range(2):
        reader = readers_ref[r : r + 1, :]
        hot = (device == reader).astype(F32)
        earlier = jnp.dot(hot.astype(BF16), later, preferred_element_type=F32) + before
        position = jnp.sum(hot * earlier, axis=0, keepdims=True)
        before = before + jnp.sum(hot, axis=1, keepdims=True)
        slots.append(reader * SLOTS + position.astype(jnp.int32))
        named = jnp.where(slot_row == position, targets_ref[r : r + 1, :].astype(F32), 0.0)
        named = jnp.where(slot_row == SLOTS, 1.0, named)
        cells = cells + lax.dot_general(
            hot.astype(BF16),
            named.astype(BF16),
            (((1,), (1,)), ((), ())),
            preferred_element_type=F32,
        )
    chunk = devices * SLOTS // 2
    pair = iota((chunk, rows), 0) * 2
    for half in range(2):
        chosen = (pair + half == slots[0]) | (pair + half == slots[1])
        sel_ref[:, half * rows : (half + 1) * rows] = jnp.where(chosen, 1.0, 0.0).astype(BF16)
    gamma = wall_ref[:, 384:512]
    gamma = jnp.where(left, gamma, pltpu.roll(gamma, 64, 1))
    for v in range(4):
        x = wall_ref[:, v * 128 : (v + 1) * 128]
        if v == 1:
            x = jnp.where(left, x, x * gamma)
        elif v == 2:
            x = x * gamma
        elif v == 3:
            x = jnp.where(left, x, x * gamma)
        turned = pltpu.roll(x, 64, 1)
        for odd in range(2):
            even_half = jnp.where(left, turned if odd else x, 0.0)
            odd_half = jnp.where(left, 0.0, x if odd else turned)
            for part, (e, o) in enumerate(zip(split3(even_half), split3(odd_half))):
                rhs_ref[0:rows, part * 128 : (part + 1) * 128] = e.astype(BF16)
                rhs_ref[rows : 2 * rows, part * 128 : (part + 1) * 128] = o.astype(BF16)
            got = jnp.dot(sel_ref[...], rhs_ref[...], preferred_element_type=F32)
            got = got[:, 0:128] + got[:, 128:256] + got[:, 256:384]
            got = got.reshape(devices, SLOTS // 2, 128)
            for q in range(SLOTS // 2):
                out_ref[:, q * 8 + 2 * v + odd, :] = got[:, q, :]
    for k in range(8):
        out_ref[:, 32 + k, :] = cells


def route_walls(devices, wall_blocks, readers_t, targets_t):
    rows = wall_blocks.shape[0]
    return pl.pallas_call(
        lambda *refs: route_kernel(devices, *refs),
        out_shape=jax.ShapeDtypeStruct((devices, 40, 128), F32),
        in_specs=[pl.BlockSpec(memory_space=pltpu.VMEM)] * 3,
        out_specs=pl.BlockSpec(memory_space=pltpu.VMEM),
        scratch_shapes=[
            pltpu.VMEM((devices * SLOTS // 2, 2 * rows), BF16),
            pltpu.VMEM((2 * rows, 384), BF16),
        ],
        compiler_params=pltpu.CompilerParams(vmem_limit_bytes=40 << 20),
        name="route_walls",
    )(wall_blocks, readers_t, targets_t)


def stack_rows(row8, rows):
    out = jnp.broadcast_to(rows[0], row8.shape)
    for n in range(1, len(rows)):
        out = jnp.where(row8 == n, rows[n], out)
    return out


def groups(high, middle, low, order):
    parts = {"h": high, "m": middle, "l": low}
    return [
        jnp.concatenate([parts[pair[0]], parts[pair[1]]], axis=0).astype(BF16) for pair in order
    ]


LEFT_ORDER = ("hh", "mh", "ml")
RIGHT_ORDER = ("hm", "hl", "mh")


def near_kernel(
    ext_ref, out_ref, feat_ref, turn_ref, side_ref, geo_ref, sd0, mid0, mix0, sd1, mid1, mix1
):
    left1 = iota((1, 128), 1) < 64
    left8 = iota((8, 128), 1) < 64
    left16 = iota((16, 128), 1) < 64
    row8 = iota((8, 128), 0)
    zero8 = jnp.zeros((8, 128), F32)
    zero16 = jnp.zeros((16, 128), BF16)
    own = jnp.where(left1, -1.0, 0.0)

    def prepare(a, p):
        row = lambda c: ext_ref[a, p, c : c + 1, :]
        x = row(0) - 0.5
        y = row(1) + own
        z = row(2) - 2.0
        u, v, w, mass = row(3), row(4), row(5), row(6) * (-32.0 * KERN_F)
        pres, visc, inv, h, heat = row(7), row(8), row(9), row(10), row(11)
        one = jnp.ones_like(x)
        head = [one, pres, u, one, pres, v]
        v0 = mass * stack_rows(row8, head + [w, z])
        place = jnp.where(row8 < 3, x, jnp.where(row8 < 6, y, z))
        v1 = mass * stack_rows(row8, head + [pres, w]) * place
        v2 = mass * jnp.where(row8 < 5, inv, visc)
        v2 = v2 * stack_rows(row8, [one, u, v, w, heat, one, u, v])
        v3 = jnp.where(row8 == 0, mass * visc * w, 0.0)
        fa = jnp.concatenate([v0, v1], axis=0)
        fb = jnp.concatenate([v2, v3], axis=0)
        turned = [pltpu.roll(t, 64, 1) for t in (v0, v1, v2, v3)]
        ta = jnp.concatenate(turned[:2], axis=0)
        tb = jnp.concatenate(turned[2:], axis=0)
        for variant in ((2,) if p == 0 else (1,) if p == 5 else (0, 1, 2)):
            if variant == 0:
                va, vb = fa, fb
            elif variant == 1:
                va, vb = jnp.where(left16, fa, ta), jnp.where(left16, fb, tb)
            else:
                va, vb = jnp.where(left16, ta, fa), jnp.where(left16, tb, fb)
            ha, la = split2(va)
            hb, lb = split2(vb)
            feat_ref[a, p, variant, 0:16, :] = ha
            feat_ref[a, p, variant, 16:32, :] = la
            feat_ref[a, p, variant, 32:48, :] = hb
            feat_ref[a, p, variant, 48:64, :] = lb
        norm = x * x + y * y + z * z
        tile = stack_rows(row8, [x, y, z, one, norm, h, one, jnp.zeros_like(x)])
        geo_ref[a, p] = stack_rows(row8, [x, y, z, norm, h, jnp.zeros_like(x)])
        half = jnp.concatenate(groups(*split3(tile), LEFT_ORDER) + [zero16], axis=0)
        turn_ref[a, p] = jnp.concatenate([half, half], axis=0).T

    def prepare_row(a, carry):
        for p in range(6):
            prepare(a, p)
        return carry

    lax.fori_loop(0, 18, prepare_row, 0)

    def sides(a, carry):
        for p in range(PAIRS):
            keep = iota((64, 128), 1) < 64
            side_ref[a, p] = jnp.where(
                keep,
                turn_ref[a, p, 64:128, :].astype(F32),
                turn_ref[a, p + 2, 0:64, :].astype(F32),
            ).astype(BF16)
        return carry

    lax.fori_loop(0, 18, sides, 0)

    row16 = iota((16, 128), 0)
    lane16 = iota((16, 128), 1)

    def scalars(s, wide, diagonal):
        s = jnp.maximum(s, 1e-20)
        w2 = wide * wide
        e = s + (0.25 * EPS_R) * w2
        w4 = w2 * w2
        den = w4 * w4 * e
        shell = jnp.maximum(wide - s * lax.rsqrt(s), 0.0)
        base = shell * shell * shell / den
        plain = base * e
        if diagonal is not None:
            plain = jnp.where(diagonal, 0.0, plain)
        return split2(plain), split2(base * s)

    y_shift = jnp.where(left1, -2.0, 2.0)
    geo_mask = jnp.where(row8 < 3, -2.0, 0.0)
    halves = lambda parts: (
        groups(*[jnp.where(left8, t, 0.0) for t in parts], RIGHT_ORDER)
        + [zero16]
        + groups(*[jnp.where(left8, 0.0, t) for t in parts], RIGHT_ORDER)
        + [zero16]
    )

    def distances(k, sd_ref):
        a = k // PAIRS
        p = k - a * PAIRS
        geo = lambda c: geo_ref[a + 1, p + 1, c : c + 1, :]
        x, y, norm, h = geo(0), geo(1), geo(3), geo(4)
        flat = geo_ref[a + 1, p + 1] * geo_mask
        wide_parts = split3(jnp.where(row8 == 5, 1.0, jnp.where(row8 == 6, h, 0.0)))
        wide_mid = jnp.concatenate(groups(*wide_parts, RIGHT_ORDER) + [zero16], axis=0)
        wide_mix = jnp.concatenate(halves(wide_parts), axis=0)
        for sx in (-1, 0, 1):
            r = a + 1 + sx
            at = (sx + 1) * 192
            n = norm - (2.0 * sx) * x + float(sx * sx) if sx else norm
            base = flat + jnp.where(row8 == 0, 2.0 * sx, jnp.where(row8 == 4, 1.0, 0.0))
            tile = jnp.where(row8 == 3, n, base)
            right = jnp.concatenate(groups(*split3(tile), RIGHT_ORDER) + [zero16], axis=0)
            sd_ref[at : at + 128, :] = jnp.dot(
                turn_ref[r, p + 1][:, 0:64],
                jnp.concatenate([right, wide_mid], axis=1),
                preferred_element_type=F32,
            )
            nm = n - 2.0 * y_shift * y + 4.0
            tile = jnp.where(row8 == 3, nm, base + jnp.where(row8 == 1, 2.0 * y_shift, 0.0))
            right = jnp.concatenate(halves(split3(tile)), axis=0)
            sd_ref[at + 128 : at + 192, :] = jnp.dot(
                side_ref[r, p],
                jnp.concatenate([right, wide_mix], axis=1),
                preferred_element_type=F32,
            )

    def weigh(sd_ref, mid_ref, mix_ref):
        for t in range(3):
            for c in range(12):
                at = t * 192 + c * 16
                diagonal = (row16 + c * 16 == lane16) if t == 1 and c < 8 else None
                (ah, al), (bh, bl) = scalars(
                    sd_ref[at : at + 16, 0:128], sd_ref[at : at + 16, 128:256], diagonal
                )
                if c < 8:
                    lo, step, ref = c * 16, 128, mid_ref
                else:
                    lo, step, ref = (c - 8) * 16, 64, mix_ref
                ref[t, 0, lo : lo + 16, :] = ah
                ref[t, 0, step + lo : step + lo + 16, :] = al
                ref[t, 1, lo : lo + 16, :] = bh
                ref[t, 1, step + lo : step + lo + 16, :] = bl

    def gather(k, mid_ref, mix_ref):
        a = k // PAIRS
        p = k - a * PAIRS
        sums = [zero8 for _ in range(4)]
        for sx in (-1, 0, 1):
            r = a + 1 + sx
            mid = feat_ref[r, p + 1, 0]
            fa = jnp.concatenate([mid[0:32], mid[0:32]], axis=1)
            fb = jnp.concatenate([mid[32:64], mid[32:64]], axis=1)
            ga = jnp.dot(fa, mid_ref[sx + 1, 0], preferred_element_type=F32)
            gb = jnp.dot(fb, mid_ref[sx + 1, 1], preferred_element_type=F32)
            side_l = feat_ref[r, p, 2]
            side_r = feat_ref[r, p + 2, 1]
            xa = jnp.dot(
                jnp.concatenate([side_l[0:32], side_r[0:32]], axis=0),
                mix_ref[sx + 1, 0],
                preferred_element_type=F32,
            )
            xb = jnp.dot(
                jnp.concatenate([side_l[32:64], side_r[32:64]], axis=0),
                mix_ref[sx + 1, 1],
                preferred_element_type=F32,
            )
            ga = ga[0:16] + ga[16:32]
            gb = gb[0:16] + gb[16:32]
            xa = jnp.where(left16, xa[0:16] + xa[16:32], xa[32:48] + xa[48:64])
            xb = jnp.where(left16, xb[0:16] + xb[16:32], xb[32:48] + xb[48:64])
            by_x = jnp.where(row8 < 3, float(sx), 0.0)
            by_y = jnp.where((row8 >= 3) & (row8 < 6), y_shift, 0.0)
            sums[0] = sums[0] + (ga[0:8] + xa[0:8])
            sums[1] = sums[1] + (ga[8:16] + xa[8:16] + by_y * xa[0:8])
            if sx:
                sums[1] = sums[1] + by_x * (ga[0:8] + xa[0:8])
            sums[2] = sums[2] + (gb[0:8] + xb[0:8])
            sums[3] = sums[3] + (gb[8:16] + xb[8:16])
        v0, v1, v2, v3 = sums
        geo = lambda c: geo_ref[a + 1, p + 1, c : c + 1, :]
        x, y, z = geo(0), geo(1), geo(2)
        row = lambda c: ext_ref[a + 1, p + 1, c : c + 1, :]
        u, v, w = row(3), row(4), row(5)
        sm, smp = v0[0:1], v0[1:2]
        gx = x * sm - v1[0:1]
        gy = y * sm - v1[3:4]
        gz = z * sm - v0[7:8]
        density = (
            u * gx
            - (x * v0[2:3] - v1[2:3])
            + v * gy
            - (y * v0[5:6] - v1[5:6])
            + w * gz
            - (z * v0[6:7] - v1[7:8])
        )
        pi, visc, inv = row(7), row(8), row(9)
        smi, smv = v2[0:1], v2[5:6]
        ax = visc * (u * smi - v2[1:2]) + inv * (u * smv - v2[6:7])
        ay = visc * (v * smi - v2[2:3]) + inv * (v * smv - v2[7:8])
        az = visc * (w * smi - v2[3:4]) + inv * (w * smv - v3[0:1])
        ax = ax - (pi * gx + (x * smp - v1[1:2]))
        ay = ay - (pi * gy + (y * smp - v1[4:5]))
        az = az - (pi * gz + (z * smp - v1[6:7]))
        heat = (2.0 * KAPPA) * inv * (row(11) * smi - v2[4:5])
        for n, line in enumerate((density, ax, ay, az, heat)):
            out_ref[a, p, n : n + 1, :] = line

    last = CA * PAIRS - 1
    slots = ((sd0, mid0, mix0), (sd1, mid1, mix1))
    for _, mid_ref, mix_ref in slots:
        mid_ref[...] = jnp.zeros(mid_ref.shape, BF16)
        mix_ref[...] = jnp.zeros(mix_ref.shape, BF16)
    distances(0, sd0)

    def step(m, carry):
        for odd in range(2):
            k = 2 * m + odd
            sd_ref, mid_ref, mix_ref = slots[odd]
            sd_next, mid_last, mix_last = slots[1 - odd]
            gather(jnp.clip(k - 1, 0, last), mid_last, mix_last)
            distances(jnp.minimum(k + 1, last), sd_next)
            weigh(sd_ref, mid_ref, mix_ref)
        return carry

    lax.fori_loop(0, CA * PAIRS // 2 + 1, step, 0)


def near_terms(ext):
    return pl.pallas_call(
        near_kernel,
        out_shape=jax.ShapeDtypeStruct((CA, PAIRS, 8, 128), F32),
        in_specs=[pl.BlockSpec(memory_space=pltpu.VMEM)],
        out_specs=pl.BlockSpec(memory_space=pltpu.VMEM),
        scratch_shapes=[
            pltpu.VMEM((18, 6, 3, 64, 128), BF16),
            pltpu.VMEM((18, 6, 128, 128), BF16),
            pltpu.VMEM((18, PAIRS, 64, 128), BF16),
            pltpu.VMEM((18, 6, 8, 128), F32),
        ]
        + [
            pltpu.VMEM((576, 256), F32),
            pltpu.VMEM((3, 2, 256, 128), BF16),
            pltpu.VMEM((3, 2, 128, 128), BF16),
        ]
        * 2,
        compiler_params=pltpu.CompilerParams(vmem_limit_bytes=48 << 20),
        name="near_terms",
    )(ext)


UNROLL = 16


def wall_kernel(cells_ref, recv_ref, rec_ref, near_ref, rates_ref, dens_ref, lhs_ref, acc_ref, list_ref):
    lane1 = iota((1, 128), 1)
    left1 = lane1 < 64
    row8 = iota((8, 128), 0)
    left8 = iota((8, 128), 1) < 64
    zero8 = jnp.zeros((8, 128), F32)
    zero16 = jnp.zeros((16, 128), BF16)

    def listing(src, m):
        for q in range(SLOTS // 2):
            list_ref[m + q] = src * (SLOTS // 2) + q
        return m + (cells_ref[src * 16 + SLOTS] + 1) // 2

    live = lax.fori_loop(0, recv_ref.shape[0], listing, 0)
    for q in range(UNROLL):
        list_ref[live + q] = 0

    def cell_features(k, carry):
        a = k // PAIRS
        p = k - a * PAIRS
        row = lambda c: rec_ref[a, p, c : c + 1, :]
        x = row(0) - 0.5
        y = row(1) - 0.5
        z = row(2) - 2.0
        h = row(10)
        s = 0.25 / (h * h)
        norm = x * x + y * y + z * z
        rows = s * stack_rows(
            row8, [-2.0 * x, -2.0 * y, -2.0 * z, jnp.ones_like(x), norm, jnp.zeros_like(x)]
        )
        half = jnp.concatenate(groups(*split3(rows), LEFT_ORDER) + [zero16], axis=0)
        both = jnp.concatenate([half, half], axis=0).T
        lhs_ref[2 * k] = both[:64]
        lhs_ref[2 * k + 1] = both[64:]
        acc_ref[2 * k] = zero8
        acc_ref[2 * k + 1] = zero8
        return carry

    lax.fori_loop(0, CA * PAIRS, cell_features, 0)

    center = jnp.where(row8 == 2, 2.0, jnp.where(row8 < 2, 0.5, 0.0))

    def block(k, carry):
        ids, tiles, squares = [], [], []
        for u in range(UNROLL):
            at = k * UNROLL + u
            pair = list_ref[at]
            src = pair // (SLOTS // 2)
            q = pair - src * (SLOTS // 2)
            ca = cells_ref[src * 16 + 2 * q]
            cb = cells_ref[src * 16 + 2 * q + 1]
            ids.append((ca, cb))
            tile = recv_ref[src, pl.ds(pl.multiple_of(q * 8, 8), 8), :]
            tiles.append(jnp.where(at < live, tile, 0.0))
            c = tile - center
            sq = c * c
            norm = sq[0:1] + sq[1:2] + sq[2:3]
            rows = jnp.where(
                row8 < 3, c, jnp.where(row8 == 3, norm, jnp.where(row8 == 4, 1.0, 0.0))
            )
            parts = split3(rows)
            lefts = groups(*[jnp.where(left8, t, 0.0) for t in parts], RIGHT_ORDER) + [zero16]
            rights = groups(*[jnp.where(left8, 0.0, t) for t in parts], RIGHT_ORDER) + [zero16]
            right = jnp.concatenate(lefts + rights, axis=0)
            lhs = jnp.concatenate([lhs_ref[ca][:, 0:64], lhs_ref[cb][:, 64:128]], axis=1)
            squares.append(jnp.dot(lhs, right, preferred_element_type=F32))
        weights = []
        for u in range(UNROLL):
            q2 = jnp.maximum(squares[u], 1e-20)
            t = q2 * lax.rsqrt(q2)
            shell = jnp.maximum(1.0 - t, 0.0)
            shell = shell * shell
            weights.append(jnp.concatenate(split2(shell * shell * (4.0 * t + 1.0)), axis=0))
        outs = []
        for u in range(UNROLL):
            tile = tiles[u]
            high = tile.astype(BF16).astype(F32)
            low = tile - high
            feats = jnp.concatenate(
                [
                    jnp.concatenate([jnp.where(left8, high, 0.0), jnp.where(left8, low, 0.0)], axis=0),
                    jnp.concatenate([jnp.where(left8, 0.0, high), jnp.where(left8, 0.0, low)], axis=0),
                ],
                axis=0,
            ).astype(BF16)
            outs.append(
                lax.dot_general(
                    feats, weights[u], (((1,), (1,)), ((), ())), preferred_element_type=F32
                )
            )
        for u in range(UNROLL):
            ca, cb = ids[u]
            got = outs[u]
            acc_ref[ca] = acc_ref[ca] + (got[0:8] + got[8:16])
            acc_ref[cb] = acc_ref[cb] + (got[16:24] + got[24:32])
        return carry

    lax.fori_loop(0, (live + UNROLL - 1) // UNROLL, block, 0)

    def finish(a, carry):
        for p in range(PAIRS):
            ta = acc_ref[a * CB + 2 * p]
            tb = acc_ref[a * CB + 2 * p + 1]
            total = jnp.where(left8, ta + pltpu.roll(ta, 64, 1), tb + pltpu.roll(tb, 64, 1))
            tile = rec_ref[a, p]
            near = near_ref[a, p]
            h, sound = tile[10:11], tile[12:13]
            scale = KERN_W / (h * h * h)
            push = WALL_PUSH * sound * sound * scale
            heat = WALL_HEAT * scale * (total[7:8] - tile[11:12] * total[6:7])
            r = [near[1 + n : 2 + n] + push * total[3 + n : 4 + n] for n in range(3)]
            r.append(near[4:5] + heat)
            t = [pltpu.roll(line, 64, 1) for line in r]
            for v in range(2):
                lo, hi = 2 * v, 2 * v + 1
                span = slice(v * 128, (v + 1) * 128)
                rates_ref[a, 2 * p : 2 * p + 1, span] = jnp.where(left1, r[lo], t[hi])
                rates_ref[a, 2 * p + 1 : 2 * p + 2, span] = jnp.where(left1, t[lo], r[hi])
            dens_ref[a, p : p + 1, :] = near[0:1]
        return carry

    lax.fori_loop(0, CA, finish, 0)


def wall_terms(cells, recv, records, near):
    return pl.pallas_call(
        wall_kernel,
        out_shape=(
            jax.ShapeDtypeStruct((CA, CB, 256), F32),
            jax.ShapeDtypeStruct((CA, PAIRS, 128), F32),
        ),
        in_specs=[pl.BlockSpec(memory_space=pltpu.SMEM)]
        + [pl.BlockSpec(memory_space=pltpu.VMEM)] * 3,
        out_specs=[pl.BlockSpec(memory_space=pltpu.VMEM)] * 2,
        scratch_shapes=[
            pltpu.VMEM((CA * CB, 64, 128), BF16),
            pltpu.VMEM((CA * CB, 8, 128), F32),
            pltpu.SMEM((recv.shape[0] * SLOTS // 2 + UNROLL + 8,), jnp.int32),
        ],
        compiler_params=pltpu.CompilerParams(vmem_limit_bytes=48 << 20),
        name="wall_terms",
    )(cells, recv, records, near)


def shift_from(array, axis, step):
    peers = lax.axis_size(axis)
    up = [(i, i + 1) for i in range(peers - 1)]
    pairs = up if step > 0 else [(j, i) for i, j in up]
    return lax.ppermute(array, axis, pairs)


def local(fluid_state, cell_counts, wall_blocks, readers, targets):
    devices = lax.axis_size("gx") * lax.axis_size("gy")
    records = pack_records(fluid_state, cell_counts.T)
    send = route_walls(devices, wall_blocks, readers.T, targets.T)
    before = shift_from(records[:, PAIRS - 1 :], "gy", 1)
    after = shift_from(records[:, :1], "gy", -1)
    wide = jnp.concatenate([before, records, after], axis=1)
    above = shift_from(wide[CA - 1 :], "gx", 1)
    below = shift_from(wide[:1], "gx", -1)
    ext = jnp.concatenate([above, wide, below], axis=0)
    recv = lax.all_to_all(send, ("gx", "gy"), split_axis=0, concat_axis=0, tiled=True)
    cells = recv[:, 32, :16].astype(jnp.int32).reshape(-1)
    near = near_terms(ext)
    rates, density = wall_terms(cells, recv, records, near)
    return (rates, density.reshape(CA, CB * 64))


def solution(mesh):
    placed = (
        P("gx", "gy", None),
        P("gx", "gy"),
        P(("gx", "gy"), None),
        P(("gx", "gy"), None),
        P(("gx", "gy"), None),
    )
    return jax.shard_map(
        local,
        mesh=mesh,
        in_specs=placed,
        out_specs=(P("gx", "gy", None), P("gx", "gy")),
        check_vma=False,
    )
```

```python
import math

import jax
import jax.numpy as jnp
from jax import lax
from jax.experimental import pallas as pl
from jax.experimental.pallas import tpu as pltpu
from jax.sharding import PartitionSpec as P

CA = 16
CB = 8
PAIRS = 4
SLOTS = 8
KERN_W = 21.0 / (16.0 * math.pi)
KERN_F = 105.0 / (16.0 * math.pi)
KAPPA = 0.02
WALL_PUSH = 0.03
WALL_HEAT = 0.02
EPS_R = 0.01
F32 = jnp.float32
BF16 = jnp.bfloat16


def iota(shape, axis):
    return lax.broadcasted_iota(jnp.int32, shape, axis)


def split2(value):
    high = value.astype(BF16)
    low = (value - high.astype(F32)).astype(BF16)
    return high, low


def split3(value):
    high = value.astype(BF16).astype(F32)
    rest = value - high
    middle = rest.astype(BF16).astype(F32)
    return high, middle, rest - middle


def pack_kernel(counts_ref, fluid_ref, out_ref):
    lane = iota((8, 128), 1)
    left = lane < 64
    slot = lane - jnp.where(left, 0, 64)

    def row(a, carry):
        comps = []
        for v in range(6):
            x = fluid_ref[a, :, v * 128 : (v + 1) * 128]
            turned = pltpu.roll(x, 64, 1)
            comps.append(jnp.where(left, x, pltpu.roll(turned, 7, 0)))
            comps.append(jnp.where(left, turned, pltpu.roll(x, 7, 0)))
        density, smooth, sound = comps[7], comps[8], comps[9]
        inverse = 1.0 / density
        d2 = density * density
        d4 = d2 * d2
        pressure = sound * sound / 7.0 * (d4 * d2 * density - 1.0)
        fields = comps[:6] + [
            comps[6],
            pressure * inverse * inverse,
            comps[10] * inverse,
            inverse,
            smooth,
            comps[11],
            sound,
        ]
        for p in range(PAIRS):
            count = jnp.where(left[:1], counts_ref[2 * p, a], counts_ref[2 * p + 1, a])
            for c, field in enumerate(fields):
                line = field[2 * p : 2 * p + 1]
                if c == 6:
                    line = jnp.where(slot[:1] < count, line, 0.0)
                out_ref[a, p, c : c + 1, :] = line
            out_ref[a, p, 13:16, :] = jnp.zeros((3, 128), F32)
        return carry

    lax.fori_loop(0, CA, row, 0)


def pack_records(fluid_state, counts_t):
    return pl.pallas_call(
        pack_kernel,
        out_shape=jax.ShapeDtypeStruct((CA, PAIRS, 16, 128), F32),
        in_specs=[
            pl.BlockSpec(memory_space=pltpu.SMEM),
            pl.BlockSpec(memory_space=pltpu.VMEM),
        ],
        out_specs=pl.BlockSpec(memory_space=pltpu.VMEM),
        name="pack_records",
    )(counts_t, fluid_state)


def route_kernel(devices, wall_ref, readers_ref, targets_ref, out_ref, sel_ref, rhs_ref):
    rows = wall_ref.shape[0]
    lane = iota((rows, 128), 1)
    left = lane < 64
    later = (iota((rows, rows), 0) < iota((rows, rows), 1)).astype(BF16)
    device = iota((devices, rows), 0)
    before = jnp.zeros((devices, 1), F32)
    slots = []
    cells = jnp.zeros((devices, 128), F32)
    slot_row = iota((128, rows), 0).astype(F32)
    for r in range(2):
        reader = readers_ref[r : r + 1, :]
        hot = (device == reader).astype(F32)
        earlier = jnp.dot(hot.astype(BF16), later, preferred_element_type=F32) + before
        position = jnp.sum(hot * earlier, axis=0, keepdims=True)
        before = before + jnp.sum(hot, axis=1, keepdims=True)
        slots.append(reader * SLOTS + position.astype(jnp.int32))
        named = jnp.where(slot_row == position, targets_ref[r : r + 1, :].astype(F32), 0.0)
        named = jnp.where(slot_row == SLOTS, 1.0, named)
        cells = cells + lax.dot_general(
            hot.astype(BF16),
            named.astype(BF16),
            (((1,), (1,)), ((), ())),
            preferred_element_type=F32,
        )
    chunk = devices * SLOTS // 2
    pair = iota((chunk, rows), 0) * 2
    for half in range(2):
        chosen = (pair + half == slots[0]) | (pair + half == slots[1])
        sel_ref[:, half * rows : (half + 1) * rows] = jnp.where(chosen, 1.0, 0.0).astype(BF16)
    gamma = wall_ref[:, 384:512]
    gamma = jnp.where(left, gamma, pltpu.roll(gamma, 64, 1))
    for v in range(4):
        x = wall_ref[:, v * 128 : (v + 1) * 128]
        if v == 1:
            x = jnp.where(left, x, x * gamma)
        elif v == 2:
            x = x * gamma
        elif v == 3:
            x = jnp.where(left, x, x * gamma)
        turned = pltpu.roll(x, 64, 1)
        for odd in range(2):
            even_half = jnp.where(left, turned if odd else x, 0.0)
            odd_half = jnp.where(left, 0.0, x if odd else turned)
            for part, (e, o) in enumerate(zip(split3(even_half), split3(odd_half))):
                rhs_ref[0:rows, part * 128 : (part + 1) * 128] = e.astype(BF16)
                rhs_ref[rows : 2 * rows, part * 128 : (part + 1) * 128] = o.astype(BF16)
            got = jnp.dot(sel_ref[...], rhs_ref[...], preferred_element_type=F32)
            got = got[:, 0:128] + got[:, 128:256] + got[:, 256:384]
            got = got.reshape(devices, SLOTS // 2, 128)
            for q in range(SLOTS // 2):
                out_ref[:, q * 8 + 2 * v + odd, :] = got[:, q, :]
    for k in range(8):
        out_ref[:, 32 + k, :] = cells


def route_walls(devices, wall_blocks, readers_t, targets_t):
    rows = wall_blocks.shape[0]
    return pl.pallas_call(
        lambda *refs: route_kernel(devices, *refs),
        out_shape=jax.ShapeDtypeStruct((devices, 40, 128), F32),
        in_specs=[pl.BlockSpec(memory_space=pltpu.VMEM)] * 3,
        out_specs=pl.BlockSpec(memory_space=pltpu.VMEM),
        scratch_shapes=[
            pltpu.VMEM((devices * SLOTS // 2, 2 * rows), BF16),
            pltpu.VMEM((2 * rows, 384), BF16),
        ],
        compiler_params=pltpu.CompilerParams(vmem_limit_bytes=40 << 20),
        name="route_walls",
    )(wall_blocks, readers_t, targets_t)


def stack_rows(row8, rows):
    out = jnp.broadcast_to(rows[0], row8.shape)
    for n in range(1, len(rows)):
        out = jnp.where(row8 == n, rows[n], out)
    return out


def groups(high, middle, low, order):
    parts = {"h": high, "m": middle, "l": low}
    return [
        jnp.concatenate([parts[pair[0]], parts[pair[1]]], axis=0).astype(BF16) for pair in order
    ]


LEFT_ORDER = ("hh", "mh", "ml")
RIGHT_ORDER = ("hm", "hl", "mh")


def near_compute(
    ext_ref, out_ref, feat_ref, turn_ref, side_ref, geo_ref, sd0, mid0, mix0, sd1, mid1, mix1
):
    left1 = iota((1, 128), 1) < 64
    left8 = iota((8, 128), 1) < 64
    left16 = iota((16, 128), 1) < 64
    row8 = iota((8, 128), 0)
    zero8 = jnp.zeros((8, 128), F32)
    zero16 = jnp.zeros((16, 128), BF16)
    own = jnp.where(left1, -1.0, 0.0)

    def prepare(a, p):
        row = lambda c: ext_ref[a, p, c : c + 1, :]
        x = row(0) - 0.5
        y = row(1) + own
        z = row(2) - 2.0
        u, v, w, mass = row(3), row(4), row(5), row(6) * (-32.0 * KERN_F)
        pres, visc, inv, h, heat = row(7), row(8), row(9), row(10), row(11)
        one = jnp.ones_like(x)
        head = [one, pres, u, one, pres, v]
        v0 = mass * stack_rows(row8, head + [w, z])
        place = jnp.where(row8 < 3, x, jnp.where(row8 < 6, y, z))
        v1 = mass * stack_rows(row8, head + [pres, w]) * place
        v2 = mass * jnp.where(row8 < 5, inv, visc)
        v2 = v2 * stack_rows(row8, [one, u, v, w, heat, one, u, v])
        v3 = jnp.where(row8 == 0, mass * visc * w, 0.0)
        fa = jnp.concatenate([v0, v1], axis=0)
        fb = jnp.concatenate([v2, v3], axis=0)
        turned = [pltpu.roll(t, 64, 1) for t in (v0, v1, v2, v3)]
        ta = jnp.concatenate(turned[:2], axis=0)
        tb = jnp.concatenate(turned[2:], axis=0)
        for variant in ((2,) if p == 0 else (1,) if p == 5 else (0, 1, 2)):
            if variant == 0:
                va, vb = fa, fb
            elif variant == 1:
                va, vb = jnp.where(left16, fa, ta), jnp.where(left16, fb, tb)
            else:
                va, vb = jnp.where(left16, ta, fa), jnp.where(left16, tb, fb)
            ha, la = split2(va)
            hb, lb = split2(vb)
            feat_ref[a, p, variant, 0:16, :] = ha
            feat_ref[a, p, variant, 16:32, :] = la
            feat_ref[a, p, variant, 32:48, :] = hb
            feat_ref[a, p, variant, 48:64, :] = lb
        norm = x * x + y * y + z * z
        tile = stack_rows(row8, [x, y, z, one, norm, h, one, jnp.zeros_like(x)])
        geo_ref[a, p] = stack_rows(row8, [x, y, z, norm, h, jnp.zeros_like(x)])
        half = jnp.concatenate(groups(*split3(tile), LEFT_ORDER) + [zero16], axis=0)
        turn_ref[a, p] = jnp.concatenate([half, half], axis=0).T

    def prepare_row(a, carry):
        for p in range(6):
            prepare(a, p)
        return carry

    lax.fori_loop(0, 18, prepare_row, 0)

    def sides(a, carry):
        for p in range(PAIRS):
            keep = iota((64, 128), 1) < 64
            side_ref[a, p] = jnp.where(
                keep,
                turn_ref[a, p, 64:128, :].astype(F32),
                turn_ref[a, p + 2, 0:64, :].astype(F32),
            ).astype(BF16)
        return carry

    lax.fori_loop(0, 18, sides, 0)

    row16 = iota((16, 128), 0)
    lane16 = iota((16, 128), 1)

    def scalars(s, wide, diagonal):
        s = jnp.maximum(s, 1e-20)
        w2 = wide * wide
        e = s + (0.25 * EPS_R) * w2
        w4 = w2 * w2
        den = w4 * w4 * e
        shell = jnp.maximum(wide - s * lax.rsqrt(s), 0.0)
        base = shell * shell * shell / den
        plain = base * e
        if diagonal is not None:
            plain = jnp.where(diagonal, 0.0, plain)
        return split2(plain), split2(base * s)

    y_shift = jnp.where(left1, -2.0, 2.0)
    geo_mask = jnp.where(row8 < 3, -2.0, 0.0)
    halves = lambda parts: (
        groups(*[jnp.where(left8, t, 0.0) for t in parts], RIGHT_ORDER)
        + [zero16]
        + groups(*[jnp.where(left8, 0.0, t) for t in parts], RIGHT_ORDER)
        + [zero16]
    )

    def distances(k, sd_ref):
        a = k // PAIRS
        p = k - a * PAIRS
        geo = lambda c: geo_ref[a + 1, p + 1, c : c + 1, :]
        x, y, norm, h = geo(0), geo(1), geo(3), geo(4)
        flat = geo_ref[a + 1, p + 1] * geo_mask
        wide_parts = split3(jnp.where(row8 == 5, 1.0, jnp.where(row8 == 6, h, 0.0)))
        wide_mid = jnp.concatenate(groups(*wide_parts, RIGHT_ORDER) + [zero16], axis=0)
        wide_mix = jnp.concatenate(halves(wide_parts), axis=0)
        for sx in (-1, 0, 1):
            r = a + 1 + sx
            at = (sx + 1) * 192
            n = norm - (2.0 * sx) * x + float(sx * sx) if sx else norm
            base = flat + jnp.where(row8 == 0, 2.0 * sx, jnp.where(row8 == 4, 1.0, 0.0))
            tile = jnp.where(row8 == 3, n, base)
            right = jnp.concatenate(groups(*split3(tile), RIGHT_ORDER) + [zero16], axis=0)
            sd_ref[at : at + 128, :] = jnp.dot(
                turn_ref[r, p + 1][:, 0:64],
                jnp.concatenate([right, wide_mid], axis=1),
                preferred_element_type=F32,
            )
            nm = n - 2.0 * y_shift * y + 4.0
            tile = jnp.where(row8 == 3, nm, base + jnp.where(row8 == 1, 2.0 * y_shift, 0.0))
            right = jnp.concatenate(halves(split3(tile)), axis=0)
            sd_ref[at + 128 : at + 192, :] = jnp.dot(
                side_ref[r, p],
                jnp.concatenate([right, wide_mix], axis=1),
                preferred_element_type=F32,
            )

    def weigh(sd_ref, mid_ref, mix_ref):
        for t in range(3):
            for c in range(12):
                at = t * 192 + c * 16
                diagonal = (row16 + c * 16 == lane16) if t == 1 and c < 8 else None
                (ah, al), (bh, bl) = scalars(
                    sd_ref[at : at + 16, 0:128], sd_ref[at : at + 16, 128:256], diagonal
                )
                if c < 8:
                    lo, step, ref = c * 16, 128, mid_ref
                else:
                    lo, step, ref = (c - 8) * 16, 64, mix_ref
                ref[t, 0, lo : lo + 16, :] = ah
                ref[t, 0, step + lo : step + lo + 16, :] = al
                ref[t, 1, lo : lo + 16, :] = bh
                ref[t, 1, step + lo : step + lo + 16, :] = bl

    def gather(k, mid_ref, mix_ref):
        a = k // PAIRS
        p = k - a * PAIRS
        sums = [zero8 for _ in range(4)]
        for sx in (-1, 0, 1):
            r = a + 1 + sx
            mid = feat_ref[r, p + 1, 0]
            fa = jnp.concatenate([mid[0:32], mid[0:32]], axis=1)
            fb = jnp.concatenate([mid[32:64], mid[32:64]], axis=1)
            ga = jnp.dot(fa, mid_ref[sx + 1, 0], preferred_element_type=F32)
            gb = jnp.dot(fb, mid_ref[sx + 1, 1], preferred_element_type=F32)
            side_l = feat_ref[r, p, 2]
            side_r = feat_ref[r, p + 2, 1]
            xa = jnp.dot(
                jnp.concatenate([side_l[0:32], side_r[0:32]], axis=0),
                mix_ref[sx + 1, 0],
                preferred_element_type=F32,
            )
            xb = jnp.dot(
                jnp.concatenate([side_l[32:64], side_r[32:64]], axis=0),
                mix_ref[sx + 1, 1],
                preferred_element_type=F32,
            )
            ga = ga[0:16] + ga[16:32]
            gb = gb[0:16] + gb[16:32]
            xa = jnp.where(left16, xa[0:16] + xa[16:32], xa[32:48] + xa[48:64])
            xb = jnp.where(left16, xb[0:16] + xb[16:32], xb[32:48] + xb[48:64])
            by_x = jnp.where(row8 < 3, float(sx), 0.0)
            by_y = jnp.where((row8 >= 3) & (row8 < 6), y_shift, 0.0)
            sums[0] = sums[0] + (ga[0:8] + xa[0:8])
            sums[1] = sums[1] + (ga[8:16] + xa[8:16] + by_y * xa[0:8])
            if sx:
                sums[1] = sums[1] + by_x * (ga[0:8] + xa[0:8])
            sums[2] = sums[2] + (gb[0:8] + xb[0:8])
            sums[3] = sums[3] + (gb[8:16] + xb[8:16])
        v0, v1, v2, v3 = sums
        geo = lambda c: geo_ref[a + 1, p + 1, c : c + 1, :]
        x, y, z = geo(0), geo(1), geo(2)
        row = lambda c: ext_ref[a + 1, p + 1, c : c + 1, :]
        u, v, w = row(3), row(4), row(5)
        sm, smp = v0[0:1], v0[1:2]
        gx = x * sm - v1[0:1]
        gy = y * sm - v1[3:4]
        gz = z * sm - v0[7:8]
        density = (
            u * gx
            - (x * v0[2:3] - v1[2:3])
            + v * gy
            - (y * v0[5:6] - v1[5:6])
            + w * gz
            - (z * v0[6:7] - v1[7:8])
        )
        pi, visc, inv = row(7), row(8), row(9)
        smi, smv = v2[0:1], v2[5:6]
        ax = visc * (u * smi - v2[1:2]) + inv * (u * smv - v2[6:7])
        ay = visc * (v * smi - v2[2:3]) + inv * (v * smv - v2[7:8])
        az = visc * (w * smi - v2[3:4]) + inv * (w * smv - v3[0:1])
        ax = ax - (pi * gx + (x * smp - v1[1:2]))
        ay = ay - (pi * gy + (y * smp - v1[4:5]))
        az = az - (pi * gz + (z * smp - v1[6:7]))
        heat = (2.0 * KAPPA) * inv * (row(11) * smi - v2[4:5])
        for n, line in enumerate((density, ax, ay, az, heat)):
            out_ref[a, p, n : n + 1, :] = line

    last = CA * PAIRS - 1
    slots = ((sd0, mid0, mix0), (sd1, mid1, mix1))
    for _, mid_ref, mix_ref in slots:
        mid_ref[...] = jnp.zeros(mid_ref.shape, BF16)
        mix_ref[...] = jnp.zeros(mix_ref.shape, BF16)
    distances(0, sd0)

    def step(m, carry):
        for odd in range(2):
            k = 2 * m + odd
            sd_ref, mid_ref, mix_ref = slots[odd]
            sd_next, mid_last, mix_last = slots[1 - odd]
            gather(jnp.clip(k - 1, 0, last), mid_last, mix_last)
            distances(jnp.minimum(k + 1, last), sd_next)
            weigh(sd_ref, mid_ref, mix_ref)
        return carry

    lax.fori_loop(0, CA * PAIRS // 2 + 1, step, 0)


def exchange_kernel(devices, rec_ref, send_ref, out_ref, recv_ref, ext_ref, *rest):
    scratch, sems = rest[:-5], rest[-5:]
    wall_send, wall_recv, own_sem, halo_send, halo_recv = sems
    gx, gy = lax.axis_index("gx"), lax.axis_index("gy")
    nx, ny = lax.axis_size("gx"), lax.axis_size("gy")
    me = gx * ny + gy
    barrier = pltpu.get_barrier_semaphore()

    def greet(d, carry):
        other = lax.rem(me + d, devices)
        pl.semaphore_signal(
            barrier,
            inc=1,
            device_id=(other // ny, lax.rem(other, ny)),
            device_id_type=pl.DeviceIdType.MESH,
        )
        return carry

    lax.fori_loop(1, devices, greet, 0)

    own_copy = pltpu.make_async_copy(send_ref.at[me], recv_ref.at[me], own_sem)
    own_copy.start()

    def keep(a, carry):
        for p in range(PAIRS):
            ext_ref[a + 1, p + 1] = rec_ref[a, p]
        return carry

    lax.fori_loop(0, CA, keep, 0)
    blank = jnp.zeros((16, 128), F32)

    @pl.when(gx == 0)
    def _():
        for p in range(6):
            ext_ref[0, p] = blank

    @pl.when(gx == nx - 1)
    def _():
        for p in range(6):
            ext_ref[CA + 1, p] = blank

    @pl.when(gy == 0)
    def _():
        for a in range(CA + 2):
            ext_ref[a, 0] = blank

    @pl.when(gy == ny - 1)
    def _():
        for a in range(CA + 2):
            ext_ref[a, PAIRS + 1] = blank

    pl.semaphore_wait(barrier, devices - 1)

    rows = {-1: (0, CA + 1), 1: (CA - 1, 0)}
    cols = {-1: (0, PAIRS + 1), 1: (PAIRS - 1, 0)}
    halos = []
    for n, (dx, dy) in enumerate(
        [(0, 1), (0, -1), (1, 0), (-1, 0), (1, 1), (1, -1), (-1, 1), (-1, -1)]
    ):
        src_a, dst_a = rows[dx] if dx else (pl.ds(0, CA), pl.ds(1, CA))
        src_p, dst_p = cols[dy] if dy else (pl.ds(0, PAIRS), pl.ds(1, PAIRS))
        to_x, to_y = gx + dx, gy + dy
        sends = (to_x >= 0) & (to_x < nx) & (to_y >= 0) & (to_y < ny)
        from_x, from_y = gx - dx, gy - dy
        receives = (from_x >= 0) & (from_x < nx) & (from_y >= 0) & (from_y < ny)
        copy = pltpu.make_async_remote_copy(
            src_ref=rec_ref.at[src_a, src_p],
            dst_ref=ext_ref.at[dst_a, dst_p],
            send_sem=halo_send.at[n],
            recv_sem=halo_recv.at[n],
            device_id=(jnp.clip(to_x, 0, nx - 1), jnp.clip(to_y, 0, ny - 1)),
            device_id_type=pl.DeviceIdType.MESH,
        )
        halos.append((sends, receives, copy))
        pl.when(sends)(copy.start)

    def post(d, carry):
        other = lax.rem(me + d, devices)
        pltpu.make_async_remote_copy(
            src_ref=send_ref.at[other],
            dst_ref=recv_ref.at[me],
            send_sem=wall_send,
            recv_sem=wall_recv,
            device_id=(other // ny, lax.rem(other, ny)),
            device_id_type=pl.DeviceIdType.MESH,
        ).start()
        return carry

    lax.fori_loop(1, devices, post, 0)
    for sends, receives, copy in halos:
        pl.when(receives)(copy.wait_recv)
    near_compute(ext_ref, out_ref, *scratch)
    for sends, receives, copy in halos:
        pl.when(sends)(copy.wait_send)
    own_copy.wait()
    everyone = recv_ref.at[pl.ds(0, devices - 1)]
    pltpu.make_async_copy(everyone, everyone, wall_send).wait()
    pltpu.make_async_copy(everyone, everyone, wall_recv).wait()


def near_and_exchange(devices, records, send):
    return pl.pallas_call(
        lambda *refs: exchange_kernel(devices, *refs),
        out_shape=(
            jax.ShapeDtypeStruct((CA, PAIRS, 8, 128), F32),
            jax.ShapeDtypeStruct(send.shape, F32),
        ),
        in_specs=[pl.BlockSpec(memory_space=pltpu.VMEM), pl.BlockSpec(memory_space=pl.ANY)],
        out_specs=[pl.BlockSpec(memory_space=pltpu.VMEM), pl.BlockSpec(memory_space=pl.ANY)],
        scratch_shapes=[
            pltpu.VMEM((18, 6, 16, 128), F32),
            pltpu.VMEM((18, 6, 3, 64, 128), BF16),
            pltpu.VMEM((18, 6, 128, 128), BF16),
            pltpu.VMEM((18, PAIRS, 64, 128), BF16),
            pltpu.VMEM((18, 6, 8, 128), F32),
        ]
        + [
            pltpu.VMEM((576, 256), F32),
            pltpu.VMEM((3, 2, 256, 128), BF16),
            pltpu.VMEM((3, 2, 128, 128), BF16),
        ]
        * 2
        + [
            pltpu.SemaphoreType.DMA,
            pltpu.SemaphoreType.DMA,
            pltpu.SemaphoreType.DMA,
            pltpu.SemaphoreType.DMA((8,)),
            pltpu.SemaphoreType.DMA((8,)),
        ],
        compiler_params=pltpu.CompilerParams(
            vmem_limit_bytes=40 << 20, collective_id=0, has_side_effects=True
        ),
        name="near_and_exchange",
    )(records, send)


UNROLL = 16


def wall_kernel(cells_ref, recv_ref, rec_ref, near_ref, rates_ref, dens_ref, lhs_ref, acc_ref, list_ref):
    lane1 = iota((1, 128), 1)
    left1 = lane1 < 64
    row8 = iota((8, 128), 0)
    left8 = iota((8, 128), 1) < 64
    zero8 = jnp.zeros((8, 128), F32)
    zero16 = jnp.zeros((16, 128), BF16)

    def listing(src, m):
        for q in range(SLOTS // 2):
            list_ref[m + q] = src * (SLOTS // 2) + q
        return m + (cells_ref[src * 16 + SLOTS] + 1) // 2

    live = lax.fori_loop(0, recv_ref.shape[0], listing, 0)
    for q in range(UNROLL):
        list_ref[live + q] = 0

    def cell_features(k, carry):
        a = k // PAIRS
        p = k - a * PAIRS
        row = lambda c: rec_ref[a, p, c : c + 1, :]
        x = row(0) - 0.5
        y = row(1) - 0.5
        z = row(2) - 2.0
        h = row(10)
        s = 0.25 / (h * h)
        norm = x * x + y * y + z * z
        rows = s * stack_rows(
            row8, [-2.0 * x, -2.0 * y, -2.0 * z, jnp.ones_like(x), norm, jnp.zeros_like(x)]
        )
        half = jnp.concatenate(groups(*split3(rows), LEFT_ORDER) + [zero16], axis=0)
        both = jnp.concatenate([half, half], axis=0).T
        lhs_ref[2 * k] = both[:64]
        lhs_ref[2 * k + 1] = both[64:]
        acc_ref[2 * k] = zero8
        acc_ref[2 * k + 1] = zero8
        return carry

    lax.fori_loop(0, CA * PAIRS, cell_features, 0)

    center = jnp.where(row8 == 2, 2.0, jnp.where(row8 < 2, 0.5, 0.0))

    def block(k, carry):
        ids, tiles, squares = [], [], []
        for u in range(UNROLL):
            at = k * UNROLL + u
            pair = list_ref[at]
            src = pair // (SLOTS // 2)
            q = pair - src * (SLOTS // 2)
            ca = cells_ref[src * 16 + 2 * q]
            cb = cells_ref[src * 16 + 2 * q + 1]
            ids.append((ca, cb))
            tile = recv_ref[src, pl.ds(pl.multiple_of(q * 8, 8), 8), :]
            tiles.append(jnp.where(at < live, tile, 0.0))
            c = tile - center
            sq = c * c
            norm = sq[0:1] + sq[1:2] + sq[2:3]
            rows = jnp.where(
                row8 < 3, c, jnp.where(row8 == 3, norm, jnp.where(row8 == 4, 1.0, 0.0))
            )
            parts = split3(rows)
            lefts = groups(*[jnp.where(left8, t, 0.0) for t in parts], RIGHT_ORDER) + [zero16]
            rights = groups(*[jnp.where(left8, 0.0, t) for t in parts], RIGHT_ORDER) + [zero16]
            right = jnp.concatenate(lefts + rights, axis=0)
            lhs = jnp.concatenate([lhs_ref[ca][:, 0:64], lhs_ref[cb][:, 64:128]], axis=1)
            squares.append(jnp.dot(lhs, right, preferred_element_type=F32))
        weights = []
        for u in range(UNROLL):
            q2 = jnp.maximum(squares[u], 1e-20)
            t = q2 * lax.rsqrt(q2)
            shell = jnp.maximum(1.0 - t, 0.0)
            shell = shell * shell
            weights.append(jnp.concatenate(split2(shell * shell * (4.0 * t + 1.0)), axis=0))
        outs = []
        for u in range(UNROLL):
            tile = tiles[u]
            high = tile.astype(BF16).astype(F32)
            low = tile - high
            feats = jnp.concatenate(
                [
                    jnp.concatenate([jnp.where(left8, high, 0.0), jnp.where(left8, low, 0.0)], axis=0),
                    jnp.concatenate([jnp.where(left8, 0.0, high), jnp.where(left8, 0.0, low)], axis=0),
                ],
                axis=0,
            ).astype(BF16)
            outs.append(
                lax.dot_general(
                    feats, weights[u], (((1,), (1,)), ((), ())), preferred_element_type=F32
                )
            )
        for u in range(UNROLL):
            ca, cb = ids[u]
            got = outs[u]
            acc_ref[ca] = acc_ref[ca] + (got[0:8] + got[8:16])
            acc_ref[cb] = acc_ref[cb] + (got[16:24] + got[24:32])
        return carry

    lax.fori_loop(0, (live + UNROLL - 1) // UNROLL, block, 0)

    def finish(a, carry):
        for p in range(PAIRS):
            ta = acc_ref[a * CB + 2 * p]
            tb = acc_ref[a * CB + 2 * p + 1]
            total = jnp.where(left8, ta + pltpu.roll(ta, 64, 1), tb + pltpu.roll(tb, 64, 1))
            tile = rec_ref[a, p]
            near = near_ref[a, p]
            h, sound = tile[10:11], tile[12:13]
            scale = KERN_W / (h * h * h)
            push = WALL_PUSH * sound * sound * scale
            heat = WALL_HEAT * scale * (total[7:8] - tile[11:12] * total[6:7])
            r = [near[1 + n : 2 + n] + push * total[3 + n : 4 + n] for n in range(3)]
            r.append(near[4:5] + heat)
            t = [pltpu.roll(line, 64, 1) for line in r]
            for v in range(2):
                lo, hi = 2 * v, 2 * v + 1
                span = slice(v * 128, (v + 1) * 128)
                rates_ref[a, 2 * p : 2 * p + 1, span] = jnp.where(left1, r[lo], t[hi])
                rates_ref[a, 2 * p + 1 : 2 * p + 2, span] = jnp.where(left1, t[lo], r[hi])
            dens_ref[a, p : p + 1, :] = near[0:1]
        return carry

    lax.fori_loop(0, CA, finish, 0)


def wall_terms(cells, recv, records, near):
    return pl.pallas_call(
        wall_kernel,
        out_shape=(
            jax.ShapeDtypeStruct((CA, CB, 256), F32),
            jax.ShapeDtypeStruct((CA, PAIRS, 128), F32),
        ),
        in_specs=[pl.BlockSpec(memory_space=pltpu.SMEM)]
        + [pl.BlockSpec(memory_space=pltpu.VMEM)] * 3,
        out_specs=[pl.BlockSpec(memory_space=pltpu.VMEM)] * 2,
        scratch_shapes=[
            pltpu.VMEM((CA * CB, 64, 128), BF16),
            pltpu.VMEM((CA * CB, 8, 128), F32),
            pltpu.SMEM((recv.shape[0] * SLOTS // 2 + UNROLL + 8,), jnp.int32),
        ],
        compiler_params=pltpu.CompilerParams(vmem_limit_bytes=48 << 20),
        name="wall_terms",
    )(cells, recv, records, near)


def local(fluid_state, cell_counts, wall_blocks, readers, targets):
    devices = lax.axis_size("gx") * lax.axis_size("gy")
    records = pack_records(fluid_state, cell_counts.T)
    send = route_walls(devices, wall_blocks, readers.T, targets.T)
    near, recv = near_and_exchange(devices, records, send)
    cells = recv[:, 32, :16].astype(jnp.int32).reshape(-1)
    rates, density = wall_terms(cells, recv, records, near)
    return (rates, density.reshape(CA, CB * 64))


def solution(mesh):
    placed = (
        P("gx", "gy", None),
        P("gx", "gy"),
        P(("gx", "gy"), None),
        P(("gx", "gy"), None),
        P(("gx", "gy"), None),
    )
    return jax.shard_map(
        local,
        mesh=mesh,
        in_specs=placed,
        out_specs=(P("gx", "gy", None), P("gx", "gy")),
        check_vma=False,
    )
```

```python
import math

import jax
import jax.numpy as jnp
from jax import lax
from jax.experimental import pallas as pl
from jax.experimental.pallas import tpu as pltpu
from jax.sharding import PartitionSpec as P

CA = 16
CB = 8
PAIRS = 4
SLOTS = 8
SENDS = 8
KERN_W = 21.0 / (16.0 * math.pi)
KERN_F = 105.0 / (16.0 * math.pi)
KAPPA = 0.02
WALL_PUSH = 0.03
WALL_HEAT = 0.02
EPS_R = 0.01
F32 = jnp.float32
BF16 = jnp.bfloat16


def iota(shape, axis):
    return lax.broadcasted_iota(jnp.int32, shape, axis)


def split2(value):
    high = value.astype(BF16)
    low = (value - high.astype(F32)).astype(BF16)
    return high, low


def split3(value):
    high = value.astype(BF16).astype(F32)
    rest = value - high
    middle = rest.astype(BF16).astype(F32)
    return high, middle, rest - middle


def pack_records(counts_ref, fluid_ref, out_ref):
    lane = iota((8, 128), 1)
    left = lane < 64
    slot = lane - jnp.where(left, 0, 64)

    def row(a, carry):
        comps = []
        for v in range(6):
            x = fluid_ref[a, :, v * 128 : (v + 1) * 128]
            turned = pltpu.roll(x, 64, 1)
            comps.append(jnp.where(left, x, pltpu.roll(turned, 7, 0)))
            comps.append(jnp.where(left, turned, pltpu.roll(x, 7, 0)))
        density, smooth, sound = comps[7], comps[8], comps[9]
        inverse = 1.0 / density
        d2 = density * density
        d4 = d2 * d2
        pressure = sound * sound / 7.0 * (d4 * d2 * density - 1.0)
        fields = comps[:6] + [
            comps[6],
            pressure * inverse * inverse,
            comps[10] * inverse,
            inverse,
            smooth,
            comps[11],
            sound,
        ]
        for p in range(PAIRS):
            count = jnp.where(left[:1], counts_ref[2 * p, a], counts_ref[2 * p + 1, a])
            for c, field in enumerate(fields):
                line = field[2 * p : 2 * p + 1]
                if c == 6:
                    line = jnp.where(slot[:1] < count, line, 0.0)
                out_ref[a, p, c : c + 1, :] = line
            out_ref[a, p, 13:16, :] = jnp.zeros((3, 128), F32)
        return carry

    lax.fori_loop(0, CA, row, 0)


def route_walls(devices, wall_ref, readers_ref, targets_ref, out_ref, sel_ref, rhs_ref):
    rows = wall_ref.shape[0]
    lane = iota((rows, 128), 1)
    left = lane < 64
    later = (iota((rows, rows), 0) < iota((rows, rows), 1)).astype(BF16)
    device = iota((devices, rows), 0)
    before = jnp.zeros((devices, 1), F32)
    slots = []
    cells = jnp.zeros((devices, 128), F32)
    slot_row = iota((128, rows), 0).astype(F32)
    for r in range(2):
        reader = readers_ref[r : r + 1, :]
        hot = (device == reader).astype(F32)
        earlier = jnp.dot(hot.astype(BF16), later, preferred_element_type=F32) + before
        position = jnp.sum(hot * earlier, axis=0, keepdims=True)
        before = before + jnp.sum(hot, axis=1, keepdims=True)
        slots.append(reader * SLOTS + position.astype(jnp.int32))
        named = jnp.where(slot_row == position, targets_ref[r : r + 1, :].astype(F32), 0.0)
        named = jnp.where(slot_row == SLOTS, 1.0, named)
        cells = cells + lax.dot_general(
            hot.astype(BF16),
            named.astype(BF16),
            (((1,), (1,)), ((), ())),
            preferred_element_type=F32,
        )
    chunk = devices * SLOTS // 2
    pair = iota((chunk, rows), 0) * 2
    for half in range(2):
        chosen = (pair + half == slots[0]) | (pair + half == slots[1])
        sel_ref[:, half * rows : (half + 1) * rows] = jnp.where(chosen, 1.0, 0.0).astype(BF16)
    gamma = wall_ref[:, 384:512]
    gamma = jnp.where(left, gamma, pltpu.roll(gamma, 64, 1))
    for v in range(4):
        x = wall_ref[:, v * 128 : (v + 1) * 128]
        if v == 1:
            x = jnp.where(left, x, x * gamma)
        elif v == 2:
            x = x * gamma
        elif v == 3:
            x = jnp.where(left, x, x * gamma)
        turned = pltpu.roll(x, 64, 1)
        for odd in range(2):
            even_half = jnp.where(left, turned if odd else x, 0.0)
            odd_half = jnp.where(left, 0.0, x if odd else turned)
            for part, (e, o) in enumerate(zip(split3(even_half), split3(odd_half))):
                rhs_ref[0:rows, part * 128 : (part + 1) * 128] = e.astype(BF16)
                rhs_ref[rows : 2 * rows, part * 128 : (part + 1) * 128] = o.astype(BF16)
            got = jnp.dot(sel_ref[...], rhs_ref[...], preferred_element_type=F32)
            got = got[:, 0:128] + got[:, 128:256] + got[:, 256:384]
            got = got.reshape(devices, SLOTS // 2, 128)
            for q in range(SLOTS // 2):
                out_ref[:, q * 8 + 2 * v + odd, :] = got[:, q, :]
    out_ref[:, 32, :] = cells


def stack_rows(row8, rows):
    out = jnp.broadcast_to(rows[0], row8.shape)
    for n in range(1, len(rows)):
        out = jnp.where(row8 == n, rows[n], out)
    return out


def groups(high, middle, low, order):
    parts = {"h": high, "m": middle, "l": low}
    return [
        jnp.concatenate([parts[pair[0]], parts[pair[1]]], axis=0).astype(BF16) for pair in order
    ]


LEFT_ORDER = ("hh", "mh", "ml")
RIGHT_ORDER = ("hm", "hl", "mh")


def near_compute(
    post, settle, ext_ref, out_ref, feat_ref, turn_ref, side_ref, geo_ref, sd0, mid0, mix0, sd1, mid1, mix1
):
    left1 = iota((1, 128), 1) < 64
    left8 = iota((8, 128), 1) < 64
    left16 = iota((16, 128), 1) < 64
    row8 = iota((8, 128), 0)
    zero8 = jnp.zeros((8, 128), F32)
    zero16 = jnp.zeros((16, 128), BF16)
    own = jnp.where(left1, -1.0, 0.0)

    def prepare(a, p):
        row = lambda c: ext_ref[a, p, c : c + 1, :]
        x = row(0) - 0.5
        y = row(1) + own
        z = row(2) - 2.0
        u, v, w, mass = row(3), row(4), row(5), row(6) * (-32.0 * KERN_F)
        pres, visc, inv, h, heat = row(7), row(8), row(9), row(10), row(11)
        one = jnp.ones_like(x)
        head = [one, pres, u, one, pres, v]
        v0 = mass * stack_rows(row8, head + [w, z])
        place = jnp.where(row8 < 3, x, jnp.where(row8 < 6, y, z))
        v1 = mass * stack_rows(row8, head + [pres, w]) * place
        v2 = mass * jnp.where(row8 < 5, inv, visc)
        v2 = v2 * stack_rows(row8, [one, u, v, w, heat, one, u, v])
        v3 = jnp.where(row8 == 0, mass * visc * w, 0.0)
        fa = jnp.concatenate([v0, v1], axis=0)
        fb = jnp.concatenate([v2, v3], axis=0)
        turned = [pltpu.roll(t, 64, 1) for t in (v0, v1, v2, v3)]
        ta = jnp.concatenate(turned[:2], axis=0)
        tb = jnp.concatenate(turned[2:], axis=0)
        for variant in ((2,) if p == 0 else (1,) if p == 5 else (0, 1, 2)):
            if variant == 0:
                va, vb = fa, fb
            elif variant == 1:
                va, vb = jnp.where(left16, fa, ta), jnp.where(left16, fb, tb)
            else:
                va, vb = jnp.where(left16, ta, fa), jnp.where(left16, tb, fb)
            ha, la = split2(va)
            hb, lb = split2(vb)
            feat_ref[a, p, variant, 0:16, :] = ha
            feat_ref[a, p, variant, 16:32, :] = la
            feat_ref[a, p, variant, 32:48, :] = hb
            feat_ref[a, p, variant, 48:64, :] = lb
        norm = x * x + y * y + z * z
        tile = stack_rows(row8, [x, y, z, one, norm, h, one, jnp.zeros_like(x)])
        geo_ref[a, p] = stack_rows(row8, [x, y, z, norm, h, jnp.zeros_like(x)])
        half = jnp.concatenate(groups(*split3(tile), LEFT_ORDER) + [zero16], axis=0)
        turn_ref[a, p] = jnp.concatenate([half, half], axis=0).T

    def prepare_row(a, carry):
        for p in range(PAIRS):
            prepare(a + 1, p + 1)
        for n in range(SENDS):
            post(a * SENDS + n + 1)
        return carry

    lax.fori_loop(0, CA, prepare_row, 0)
    settle()

    def prepare_columns(a, carry):
        for p in (0, PAIRS + 1):
            prepare(a + 1, p)
        return carry

    lax.fori_loop(0, CA, prepare_columns, 0)
    for p in range(PAIRS + 2):
        prepare(0, p)
        prepare(CA + 1, p)

    def sides(a, carry):
        for p in range(PAIRS):
            keep = iota((64, 128), 1) < 64
            side_ref[a, p] = jnp.where(
                keep,
                turn_ref[a, p, 64:128, :].astype(F32),
                turn_ref[a, p + 2, 0:64, :].astype(F32),
            ).astype(BF16)
        return carry

    lax.fori_loop(0, 18, sides, 0)

    row16 = iota((16, 128), 0)
    lane16 = iota((16, 128), 1)

    def scalars(s, wide, diagonal):
        s = jnp.maximum(s, 1e-20)
        w2 = wide * wide
        e = s + (0.25 * EPS_R) * w2
        w4 = w2 * w2
        den = w4 * w4 * e
        shell = jnp.maximum(wide - s * lax.rsqrt(s), 0.0)
        base = shell * shell * shell / den
        plain = base * e
        if diagonal is not None:
            plain = jnp.where(diagonal, 0.0, plain)
        return split2(plain), split2(base * s)

    y_shift = jnp.where(left1, -2.0, 2.0)
    geo_mask = jnp.where(row8 < 3, -2.0, 0.0)
    halves = lambda parts: (
        groups(*[jnp.where(left8, t, 0.0) for t in parts], RIGHT_ORDER)
        + [zero16]
        + groups(*[jnp.where(left8, 0.0, t) for t in parts], RIGHT_ORDER)
        + [zero16]
    )

    def distances(k, sd_ref):
        a = k // PAIRS
        p = k - a * PAIRS
        geo = lambda c: geo_ref[a + 1, p + 1, c : c + 1, :]
        x, y, norm, h = geo(0), geo(1), geo(3), geo(4)
        flat = geo_ref[a + 1, p + 1] * geo_mask
        wide_parts = split3(jnp.where(row8 == 5, 1.0, jnp.where(row8 == 6, h, 0.0)))
        wide_mid = jnp.concatenate(groups(*wide_parts, RIGHT_ORDER) + [zero16], axis=0)
        wide_mix = jnp.concatenate(halves(wide_parts), axis=0)
        for sx in (-1, 0, 1):
            r = a + 1 + sx
            at = (sx + 1) * 192
            n = norm - (2.0 * sx) * x + float(sx * sx) if sx else norm
            base = flat + jnp.where(row8 == 0, 2.0 * sx, jnp.where(row8 == 4, 1.0, 0.0))
            tile = jnp.where(row8 == 3, n, base)
            right = jnp.concatenate(groups(*split3(tile), RIGHT_ORDER) + [zero16], axis=0)
            sd_ref[at : at + 128, :] = jnp.dot(
                turn_ref[r, p + 1][:, 0:64],
                jnp.concatenate([right, wide_mid], axis=1),
                preferred_element_type=F32,
            )
            nm = n - 2.0 * y_shift * y + 4.0
            tile = jnp.where(row8 == 3, nm, base + jnp.where(row8 == 1, 2.0 * y_shift, 0.0))
            right = jnp.concatenate(halves(split3(tile)), axis=0)
            sd_ref[at + 128 : at + 192, :] = jnp.dot(
                side_ref[r, p],
                jnp.concatenate([right, wide_mix], axis=1),
                preferred_element_type=F32,
            )

    def weigh(sd_ref, mid_ref, mix_ref):
        for t in range(3):
            for c in range(12):
                at = t * 192 + c * 16
                diagonal = (row16 + c * 16 == lane16) if t == 1 and c < 8 else None
                (ah, al), (bh, bl) = scalars(
                    sd_ref[at : at + 16, 0:128], sd_ref[at : at + 16, 128:256], diagonal
                )
                if c < 8:
                    lo, step, ref = c * 16, 128, mid_ref
                else:
                    lo, step, ref = (c - 8) * 16, 64, mix_ref
                ref[t, 0, lo : lo + 16, :] = ah
                ref[t, 0, step + lo : step + lo + 16, :] = al
                ref[t, 1, lo : lo + 16, :] = bh
                ref[t, 1, step + lo : step + lo + 16, :] = bl

    def gather(k, mid_ref, mix_ref):
        a = k // PAIRS
        p = k - a * PAIRS
        sums = [zero8 for _ in range(4)]
        for sx in (-1, 0, 1):
            r = a + 1 + sx
            mid = feat_ref[r, p + 1, 0]
            fa = jnp.concatenate([mid[0:32], mid[0:32]], axis=1)
            fb = jnp.concatenate([mid[32:64], mid[32:64]], axis=1)
            ga = jnp.dot(fa, mid_ref[sx + 1, 0], preferred_element_type=F32)
            gb = jnp.dot(fb, mid_ref[sx + 1, 1], preferred_element_type=F32)
            side_l = feat_ref[r, p, 2]
            side_r = feat_ref[r, p + 2, 1]
            xa = jnp.dot(
                jnp.concatenate([side_l[0:32], side_r[0:32]], axis=0),
                mix_ref[sx + 1, 0],
                preferred_element_type=F32,
            )
            xb = jnp.dot(
                jnp.concatenate([side_l[32:64], side_r[32:64]], axis=0),
                mix_ref[sx + 1, 1],
                preferred_element_type=F32,
            )
            ga = ga[0:16] + ga[16:32]
            gb = gb[0:16] + gb[16:32]
            xa = jnp.where(left16, xa[0:16] + xa[16:32], xa[32:48] + xa[48:64])
            xb = jnp.where(left16, xb[0:16] + xb[16:32], xb[32:48] + xb[48:64])
            by_x = jnp.where(row8 < 3, float(sx), 0.0)
            by_y = jnp.where((row8 >= 3) & (row8 < 6), y_shift, 0.0)
            sums[0] = sums[0] + (ga[0:8] + xa[0:8])
            sums[1] = sums[1] + (ga[8:16] + xa[8:16] + by_y * xa[0:8])
            if sx:
                sums[1] = sums[1] + by_x * (ga[0:8] + xa[0:8])
            sums[2] = sums[2] + (gb[0:8] + xb[0:8])
            sums[3] = sums[3] + (gb[8:16] + xb[8:16])
        v0, v1, v2, v3 = sums
        geo = lambda c: geo_ref[a + 1, p + 1, c : c + 1, :]
        x, y, z = geo(0), geo(1), geo(2)
        row = lambda c: ext_ref[a + 1, p + 1, c : c + 1, :]
        u, v, w = row(3), row(4), row(5)
        sm, smp = v0[0:1], v0[1:2]
        gx = x * sm - v1[0:1]
        gy = y * sm - v1[3:4]
        gz = z * sm - v0[7:8]
        density = (
            u * gx
            - (x * v0[2:3] - v1[2:3])
            + v * gy
            - (y * v0[5:6] - v1[5:6])
            + w * gz
            - (z * v0[6:7] - v1[7:8])
        )
        pi, visc, inv = row(7), row(8), row(9)
        smi, smv = v2[0:1], v2[5:6]
        ax = visc * (u * smi - v2[1:2]) + inv * (u * smv - v2[6:7])
        ay = visc * (v * smi - v2[2:3]) + inv * (v * smv - v2[7:8])
        az = visc * (w * smi - v2[3:4]) + inv * (w * smv - v3[0:1])
        ax = ax - (pi * gx + (x * smp - v1[1:2]))
        ay = ay - (pi * gy + (y * smp - v1[4:5]))
        az = az - (pi * gz + (z * smp - v1[6:7]))
        heat = (2.0 * KAPPA) * inv * (row(11) * smi - v2[4:5])
        for n, line in enumerate((density, ax, ay, az, heat)):
            out_ref[a, p, n : n + 1, :] = line

    last = CA * PAIRS - 1
    slots = ((sd0, mid0, mix0), (sd1, mid1, mix1))
    for _, mid_ref, mix_ref in slots:
        mid_ref[...] = jnp.zeros(mid_ref.shape, BF16)
        mix_ref[...] = jnp.zeros(mix_ref.shape, BF16)
    distances(0, sd0)

    def step(m, carry):
        for odd in range(2):
            k = 2 * m + odd
            sd_ref, mid_ref, mix_ref = slots[odd]
            sd_next, mid_last, mix_last = slots[1 - odd]
            gather(jnp.clip(k - 1, 0, last), mid_last, mix_last)
            distances(jnp.minimum(k + 1, last), sd_next)
            weigh(sd_ref, mid_ref, mix_ref)
        return carry

    lax.fori_loop(0, CA * PAIRS // 2 + 1, step, 0)


def exchange_kernel(
    devices,
    counts_ref,
    fluid_hbm,
    wall_hbm,
    readers_hbm,
    targets_hbm,
    out_ref,
    rec_ref,
    recv_ref,
    fluid_ref,
    wall_ref,
    readers_ref,
    targets_ref,
    send_ref,
    sel_ref,
    rhs_ref,
    ext_ref,
    *rest,
):
    scratch, (load_sem, wall_send, wall_recv, own_sem, halo_send, halo_recv) = rest[:-6], rest[-6:]
    gx, gy = lax.axis_index("gx"), lax.axis_index("gy")
    nx, ny = lax.axis_size("gx"), lax.axis_size("gy")
    me = gx * ny + gy
    loads = [
        pltpu.make_async_copy(src, dst, load_sem.at[n])
        for n, (src, dst) in enumerate(
            [
                (readers_hbm, readers_ref),
                (targets_hbm, targets_ref),
                (wall_hbm, wall_ref),
                (fluid_hbm, fluid_ref),
            ]
        )
    ]
    for load in loads:
        load.start()
    barrier = pltpu.get_barrier_semaphore()

    def greet(d, carry):
        other = lax.rem(me + d, devices)
        pl.semaphore_signal(
            barrier,
            inc=1,
            device_id=(other // ny, lax.rem(other, ny)),
            device_id_type=pl.DeviceIdType.MESH,
        )
        return carry

    lax.fori_loop(1, devices, greet, 0)
    blank = jnp.zeros((16, 128), F32)

    @pl.when(gx == 0)
    def _():
        for p in range(6):
            ext_ref[0, p] = blank

    @pl.when(gx == nx - 1)
    def _():
        for p in range(6):
            ext_ref[CA + 1, p] = blank

    @pl.when(gy == 0)
    def _():
        for a in range(CA + 2):
            ext_ref[a, 0] = blank

    @pl.when(gy == ny - 1)
    def _():
        for a in range(CA + 2):
            ext_ref[a, PAIRS + 1] = blank

    for load in loads[:3]:
        load.wait()
    route_walls(devices, wall_ref, readers_ref, targets_ref, send_ref, sel_ref, rhs_ref)
    loads[3].wait()
    pack_records(counts_ref, fluid_ref, rec_ref)

    def keep(a, carry):
        for p in range(PAIRS):
            ext_ref[a + 1, p + 1] = rec_ref[a, p]
        return carry

    lax.fori_loop(0, CA, keep, 0)
    pl.semaphore_wait(barrier, devices - 1)

    rows = {-1: (0, CA + 1), 1: (CA - 1, 0)}
    cols = {-1: (0, PAIRS + 1), 1: (PAIRS - 1, 0)}
    halos = []
    for n, (dx, dy) in enumerate(
        [(0, 1), (0, -1), (1, 0), (-1, 0), (1, 1), (1, -1), (-1, 1), (-1, -1)]
    ):
        src_a, dst_a = rows[dx] if dx else (pl.ds(0, CA), pl.ds(1, CA))
        src_p, dst_p = cols[dy] if dy else (pl.ds(0, PAIRS), pl.ds(1, PAIRS))
        to_x, to_y = gx + dx, gy + dy
        sends = (to_x >= 0) & (to_x < nx) & (to_y >= 0) & (to_y < ny)
        from_x, from_y = gx - dx, gy - dy
        receives = (from_x >= 0) & (from_x < nx) & (from_y >= 0) & (from_y < ny)
        copy = pltpu.make_async_remote_copy(
            src_ref=rec_ref.at[src_a, src_p],
            dst_ref=ext_ref.at[dst_a, dst_p],
            send_sem=halo_send.at[n],
            recv_sem=halo_recv.at[n],
            device_id=(jnp.clip(to_x, 0, nx - 1), jnp.clip(to_y, 0, ny - 1)),
            device_id_type=pl.DeviceIdType.MESH,
        )
        halos.append((sends, receives, copy))
        pl.when(sends)(copy.start)

    used = pl.ds(0, 33)
    own_copy = pltpu.make_async_copy(send_ref.at[me, used], recv_ref.at[me, used], own_sem)
    own_copy.start()

    def post(d):
        other = lax.rem(me + d * 37, devices)

        @pl.when(d < devices)
        def _():
            pltpu.make_async_remote_copy(
                src_ref=send_ref.at[other, used],
                dst_ref=recv_ref.at[me, used],
                send_sem=wall_send,
                recv_sem=wall_recv,
                device_id=(other // ny, lax.rem(other, ny)),
                device_id_type=pl.DeviceIdType.MESH,
            ).start()

    def settle():
        for sends, receives, copy in halos:
            pl.when(receives)(copy.wait_recv)

    near_compute(post, settle, ext_ref, out_ref, *scratch)
    for sends, receives, copy in halos:
        pl.when(sends)(copy.wait_send)
    own_copy.wait()
    everyone = recv_ref.at[pl.ds(0, devices - 1), used]
    pltpu.make_async_copy(everyone, everyone, wall_send).wait()
    pltpu.make_async_copy(everyone, everyone, wall_recv).wait()


def near_and_exchange(devices, counts_t, fluid_state, wall_blocks, readers_t, targets_t):
    walls = wall_blocks.shape[0]
    vmem = pl.BlockSpec(memory_space=pltpu.VMEM)
    anywhere = pl.BlockSpec(memory_space=pl.ANY)
    return pl.pallas_call(
        lambda *refs: exchange_kernel(devices, *refs),
        out_shape=(
            jax.ShapeDtypeStruct((CA, PAIRS, 8, 128), F32),
            jax.ShapeDtypeStruct((CA, PAIRS, 16, 128), F32),
            jax.ShapeDtypeStruct((devices, 40, 128), F32),
        ),
        in_specs=[pl.BlockSpec(memory_space=pltpu.SMEM)] + [anywhere] * 4,
        out_specs=[vmem, vmem, anywhere],
        scratch_shapes=[
            pltpu.VMEM(fluid_state.shape, F32),
            pltpu.VMEM(wall_blocks.shape, F32),
            pltpu.VMEM(readers_t.shape, jnp.int32),
            pltpu.VMEM(targets_t.shape, jnp.int32),
            pltpu.VMEM((devices, 40, 128), F32),
            pltpu.VMEM((devices * SLOTS // 2, 2 * walls), BF16),
            pltpu.VMEM((2 * walls, 384), BF16),
            pltpu.VMEM((18, 6, 16, 128), F32),
            pltpu.VMEM((18, 6, 3, 64, 128), BF16),
            pltpu.VMEM((18, 6, 128, 128), BF16),
            pltpu.VMEM((18, PAIRS, 64, 128), BF16),
            pltpu.VMEM((18, 6, 8, 128), F32),
        ]
        + [
            pltpu.VMEM((576, 256), F32),
            pltpu.VMEM((3, 2, 256, 128), BF16),
            pltpu.VMEM((3, 2, 128, 128), BF16),
        ]
        * 2
        + [
            pltpu.SemaphoreType.DMA((4,)),
            pltpu.SemaphoreType.DMA,
            pltpu.SemaphoreType.DMA,
            pltpu.SemaphoreType.DMA,
            pltpu.SemaphoreType.DMA((8,)),
            pltpu.SemaphoreType.DMA((8,)),
        ],
        compiler_params=pltpu.CompilerParams(
            vmem_limit_bytes=40 << 20, collective_id=0, has_side_effects=True
        ),
        name="near_and_exchange",
    )(counts_t, fluid_state, wall_blocks, readers_t, targets_t)


UNROLL = 16


def wall_kernel(cells_ref, recv_ref, rec_ref, near_ref, rates_ref, dens_ref, lhs_ref, acc_ref, list_ref):
    lane1 = iota((1, 128), 1)
    left1 = lane1 < 64
    row8 = iota((8, 128), 0)
    left8 = iota((8, 128), 1) < 64
    zero8 = jnp.zeros((8, 128), F32)
    zero16 = jnp.zeros((16, 128), BF16)

    def listing(src, m):
        for q in range(SLOTS // 2):
            list_ref[m + q] = src * (SLOTS // 2) + q
        return m + (cells_ref[src * 16 + SLOTS] + 1) // 2

    live = lax.fori_loop(0, recv_ref.shape[0], listing, 0)
    for q in range(UNROLL):
        list_ref[live + q] = 0

    def cell_features(k, carry):
        a = k // PAIRS
        p = k - a * PAIRS
        row = lambda c: rec_ref[a, p, c : c + 1, :]
        x = row(0) - 0.5
        y = row(1) - 0.5
        z = row(2) - 2.0
        h = row(10)
        s = 0.25 / (h * h)
        norm = x * x + y * y + z * z
        rows = s * stack_rows(
            row8, [-2.0 * x, -2.0 * y, -2.0 * z, jnp.ones_like(x), norm, jnp.zeros_like(x)]
        )
        half = jnp.concatenate(groups(*split3(rows), LEFT_ORDER) + [zero16], axis=0)
        both = jnp.concatenate([half, half], axis=0).T
        lhs_ref[2 * k] = both[:64]
        lhs_ref[2 * k + 1] = both[64:]
        acc_ref[2 * k] = zero8
        acc_ref[2 * k + 1] = zero8
        return carry

    lax.fori_loop(0, CA * PAIRS, cell_features, 0)

    center = jnp.where(row8 == 2, 2.0, jnp.where(row8 < 2, 0.5, 0.0))

    def block(k, carry):
        ids, tiles, squares = [], [], []
        for u in range(UNROLL):
            at = k * UNROLL + u
            pair = list_ref[at]
            src = pair // (SLOTS // 2)
            q = pair - src * (SLOTS // 2)
            ca = cells_ref[src * 16 + 2 * q]
            cb = cells_ref[src * 16 + 2 * q + 1]
            ids.append((ca, cb))
            tile = recv_ref[src, pl.ds(pl.multiple_of(q * 8, 8), 8), :]
            tiles.append(jnp.where(at < live, tile, 0.0))
            c = tile - center
            sq = c * c
            norm = sq[0:1] + sq[1:2] + sq[2:3]
            rows = jnp.where(
                row8 < 3, c, jnp.where(row8 == 3, norm, jnp.where(row8 == 4, 1.0, 0.0))
            )
            parts = split3(rows)
            lefts = groups(*[jnp.where(left8, t, 0.0) for t in parts], RIGHT_ORDER) + [zero16]
            rights = groups(*[jnp.where(left8, 0.0, t) for t in parts], RIGHT_ORDER) + [zero16]
            right = jnp.concatenate(lefts + rights, axis=0)
            lhs = jnp.concatenate([lhs_ref[ca][:, 0:64], lhs_ref[cb][:, 64:128]], axis=1)
            squares.append(jnp.dot(lhs, right, preferred_element_type=F32))
        weights = []
        for u in range(UNROLL):
            q2 = jnp.maximum(squares[u], 1e-20)
            t = q2 * lax.rsqrt(q2)
            shell = jnp.maximum(1.0 - t, 0.0)
            shell = shell * shell
            weights.append(jnp.concatenate(split2(shell * shell * (4.0 * t + 1.0)), axis=0))
        outs = []
        for u in range(UNROLL):
            tile = tiles[u]
            high = tile.astype(BF16).astype(F32)
            low = tile - high
            feats = jnp.concatenate(
                [
                    jnp.concatenate([jnp.where(left8, high, 0.0), jnp.where(left8, low, 0.0)], axis=0),
                    jnp.concatenate([jnp.where(left8, 0.0, high), jnp.where(left8, 0.0, low)], axis=0),
                ],
                axis=0,
            ).astype(BF16)
            outs.append(
                lax.dot_general(
                    feats, weights[u], (((1,), (1,)), ((), ())), preferred_element_type=F32
                )
            )
        for u in range(UNROLL):
            ca, cb = ids[u]
            got = outs[u]
            acc_ref[ca] = acc_ref[ca] + (got[0:8] + got[8:16])
            acc_ref[cb] = acc_ref[cb] + (got[16:24] + got[24:32])
        return carry

    lax.fori_loop(0, (live + UNROLL - 1) // UNROLL, block, 0)

    def finish(a, carry):
        for p in range(PAIRS):
            ta = acc_ref[a * CB + 2 * p]
            tb = acc_ref[a * CB + 2 * p + 1]
            total = jnp.where(left8, ta + pltpu.roll(ta, 64, 1), tb + pltpu.roll(tb, 64, 1))
            tile = rec_ref[a, p]
            near = near_ref[a, p]
            h, sound = tile[10:11], tile[12:13]
            scale = KERN_W / (h * h * h)
            push = WALL_PUSH * sound * sound * scale
            heat = WALL_HEAT * scale * (total[7:8] - tile[11:12] * total[6:7])
            r = [near[1 + n : 2 + n] + push * total[3 + n : 4 + n] for n in range(3)]
            r.append(near[4:5] + heat)
            t = [pltpu.roll(line, 64, 1) for line in r]
            for v in range(2):
                lo, hi = 2 * v, 2 * v + 1
                span = slice(v * 128, (v + 1) * 128)
                rates_ref[a, 2 * p : 2 * p + 1, span] = jnp.where(left1, r[lo], t[hi])
                rates_ref[a, 2 * p + 1 : 2 * p + 2, span] = jnp.where(left1, t[lo], r[hi])
            dens_ref[a, p : p + 1, :] = near[0:1]
        return carry

    lax.fori_loop(0, CA, finish, 0)


def wall_terms(cells, recv, records, near):
    return pl.pallas_call(
        wall_kernel,
        out_shape=(
            jax.ShapeDtypeStruct((CA, CB, 256), F32),
            jax.ShapeDtypeStruct((CA, PAIRS, 128), F32),
        ),
        in_specs=[pl.BlockSpec(memory_space=pltpu.SMEM)]
        + [pl.BlockSpec(memory_space=pltpu.VMEM)] * 3,
        out_specs=[pl.BlockSpec(memory_space=pltpu.VMEM)] * 2,
        scratch_shapes=[
            pltpu.VMEM((CA * CB, 64, 128), BF16),
            pltpu.VMEM((CA * CB, 8, 128), F32),
            pltpu.SMEM((recv.shape[0] * SLOTS // 2 + UNROLL + 8,), jnp.int32),
        ],
        compiler_params=pltpu.CompilerParams(vmem_limit_bytes=48 << 20),
        name="wall_terms",
    )(cells, recv, records, near)


def local(fluid_state, cell_counts, wall_blocks, readers, targets):
    devices = lax.axis_size("gx") * lax.axis_size("gy")
    near, records, recv = near_and_exchange(
        devices, cell_counts.T, fluid_state, wall_blocks, readers.T, targets.T
    )
    cells = recv[:, 32, :16].astype(jnp.int32).reshape(-1)
    rates, density = wall_terms(cells, recv, records, near)
    return (rates, density.reshape(CA, CB * 64))


def solution(mesh):
    placed = (
        P("gx", "gy", None),
        P("gx", "gy"),
        P(("gx", "gy"), None),
        P(("gx", "gy"), None),
        P(("gx", "gy"), None),
    )
    return jax.shard_map(
        local,
        mesh=mesh,
        in_specs=placed,
        out_specs=(P("gx", "gy", None), P("gx", "gy")),
        check_vma=False,
    )
```

```python
import math

import jax
import jax.numpy as jnp
from jax import lax
from jax.experimental import pallas as pl
from jax.experimental.pallas import tpu as pltpu
from jax.sharding import PartitionSpec as P

CA = 16
CB = 8
PAIRS = 4
SLOTS = 8
SENDS = 1
STEP_SENDS = 2
KERN_W = 21.0 / (16.0 * math.pi)
KERN_F = 105.0 / (16.0 * math.pi)
KAPPA = 0.02
WALL_PUSH = 0.03
WALL_HEAT = 0.02
EPS_R = 0.01
F32 = jnp.float32
BF16 = jnp.bfloat16


def iota(shape, axis):
    return lax.broadcasted_iota(jnp.int32, shape, axis)


def split2(value):
    high = value.astype(BF16)
    low = (value - high.astype(F32)).astype(BF16)
    return high, low


def split3(value):
    high = value.astype(BF16).astype(F32)
    rest = value - high
    middle = rest.astype(BF16).astype(F32)
    return high, middle, rest - middle


def pack_records(counts_ref, fluid_ref, out_ref, greet):
    lane = iota((8, 128), 1)
    left = lane < 64
    slot = lane - jnp.where(left, 0, 64)

    def row(a, carry):
        comps = []
        for v in range(6):
            x = fluid_ref[a, :, v * 128 : (v + 1) * 128]
            turned = pltpu.roll(x, 64, 1)
            comps.append(jnp.where(left, x, pltpu.roll(turned, 7, 0)))
            comps.append(jnp.where(left, turned, pltpu.roll(x, 7, 0)))
        density, smooth, sound = comps[7], comps[8], comps[9]
        inverse = 1.0 / density
        d2 = density * density
        d4 = d2 * d2
        pressure = sound * sound / 7.0 * (d4 * d2 * density - 1.0)
        fields = comps[:6] + [
            comps[6],
            pressure * inverse * inverse,
            comps[10] * inverse,
            inverse,
            smooth,
            comps[11],
            sound,
        ]
        for p in range(PAIRS):
            count = jnp.where(left[:1], counts_ref[2 * p, a], counts_ref[2 * p + 1, a])
            for c, field in enumerate(fields):
                line = field[2 * p : 2 * p + 1]
                if c == 6:
                    line = jnp.where(slot[:1] < count, line, 0.0)
                out_ref[a, p, c : c + 1, :] = line
            out_ref[a, p, 13:16, :] = jnp.zeros((3, 128), F32)
        for n in range(SLOTS):
            greet(a * SLOTS + n + 1)
        return carry

    lax.fori_loop(0, CA, row, 0)


def route_walls(devices, wall_ref, readers_ref, targets_ref, out_ref, sel_ref, rhs_ref):
    rows = wall_ref.shape[0]
    lane = iota((rows, 128), 1)
    left = lane < 64
    later = (iota((rows, rows), 0) < iota((rows, rows), 1)).astype(BF16)
    device = iota((devices, rows), 0)
    before = jnp.zeros((devices, 1), F32)
    slots = []
    cells = jnp.zeros((devices, 128), F32)
    slot_row = iota((128, rows), 0).astype(F32)
    for r in range(2):
        reader = readers_ref[r : r + 1, :]
        hot = (device == reader).astype(F32)
        earlier = jnp.dot(hot.astype(BF16), later, preferred_element_type=F32) + before
        position = jnp.sum(hot * earlier, axis=0, keepdims=True)
        before = before + jnp.sum(hot, axis=1, keepdims=True)
        slots.append(reader * SLOTS + position.astype(jnp.int32))
        named = jnp.where(slot_row == position, targets_ref[r : r + 1, :].astype(F32), 0.0)
        named = jnp.where(slot_row == SLOTS, 1.0, named)
        cells = cells + lax.dot_general(
            hot.astype(BF16),
            named.astype(BF16),
            (((1,), (1,)), ((), ())),
            preferred_element_type=F32,
        )
    chunk = devices * SLOTS // 2
    pair = iota((chunk, rows), 0) * 2
    for half in range(2):
        chosen = (pair + half == slots[0]) | (pair + half == slots[1])
        sel_ref[:, half * rows : (half + 1) * rows] = jnp.where(chosen, 1.0, 0.0).astype(BF16)
    gamma = wall_ref[:, 384:512]
    gamma = jnp.where(left, gamma, pltpu.roll(gamma, 64, 1))
    for v in range(4):
        x = wall_ref[:, v * 128 : (v + 1) * 128]
        if v == 1:
            x = jnp.where(left, x, x * gamma)
        elif v == 2:
            x = x * gamma
        elif v == 3:
            x = jnp.where(left, x, x * gamma)
        turned = pltpu.roll(x, 64, 1)
        for odd in range(2):
            even_half = jnp.where(left, turned if odd else x, 0.0)
            odd_half = jnp.where(left, 0.0, x if odd else turned)
            for part, (e, o) in enumerate(zip(split3(even_half), split3(odd_half))):
                rhs_ref[0:rows, part * 128 : (part + 1) * 128] = e.astype(BF16)
                rhs_ref[rows : 2 * rows, part * 128 : (part + 1) * 128] = o.astype(BF16)
            got = jnp.dot(sel_ref[...], rhs_ref[...], preferred_element_type=F32)
            got = got[:, 0:128] + got[:, 128:256] + got[:, 256:384]
            got = got.reshape(devices, SLOTS // 2, 128)
            for q in range(SLOTS // 2):
                out_ref[:, q * 8 + 2 * v + odd, :] = got[:, q, :]
    out_ref[:, 32, :] = cells


def stack_rows(row8, rows):
    out = jnp.broadcast_to(rows[0], row8.shape)
    for n in range(1, len(rows)):
        out = jnp.where(row8 == n, rows[n], out)
    return out


def groups(high, middle, low, order):
    parts = {"h": high, "m": middle, "l": low}
    return [
        jnp.concatenate([parts[pair[0]], parts[pair[1]]], axis=0).astype(BF16) for pair in order
    ]


LEFT_ORDER = ("hh", "mh", "ml")
RIGHT_ORDER = ("hm", "hl", "mh")


def near_compute(
    post, settle, ext_ref, out_ref, lhs_ref, feat_ref, turn_ref, side_ref, geo_ref, sd0, mid0, mix0, sd1, mid1, mix1
):
    left1 = iota((1, 128), 1) < 64
    left8 = iota((8, 128), 1) < 64
    left16 = iota((16, 128), 1) < 64
    row8 = iota((8, 128), 0)
    zero8 = jnp.zeros((8, 128), F32)
    zero16 = jnp.zeros((16, 128), BF16)
    own = jnp.where(left1, -1.0, 0.0)

    def prepare(a, p):
        row = lambda c: ext_ref[a, p, c : c + 1, :]
        x = row(0) - 0.5
        y = row(1) + own
        z = row(2) - 2.0
        u, v, w, mass = row(3), row(4), row(5), row(6) * (-32.0 * KERN_F)
        pres, visc, inv, h, heat = row(7), row(8), row(9), row(10), row(11)
        one = jnp.ones_like(x)
        head = [one, pres, u, one, pres, v]
        v0 = mass * stack_rows(row8, head + [w, z])
        place = jnp.where(row8 < 3, x, jnp.where(row8 < 6, y, z))
        v1 = mass * stack_rows(row8, head + [pres, w]) * place
        v2 = mass * jnp.where(row8 < 5, inv, visc)
        v2 = v2 * stack_rows(row8, [one, u, v, w, heat, one, u, v])
        v3 = jnp.where(row8 == 0, mass * visc * w, 0.0)
        fa = jnp.concatenate([v0, v1], axis=0)
        fb = jnp.concatenate([v2, v3], axis=0)
        turned = [pltpu.roll(t, 64, 1) for t in (v0, v1, v2, v3)]
        ta = jnp.concatenate(turned[:2], axis=0)
        tb = jnp.concatenate(turned[2:], axis=0)
        for variant in ((2,) if p == 0 else (1,) if p == 5 else (0, 1, 2)):
            if variant == 0:
                va, vb = fa, fb
            elif variant == 1:
                va, vb = jnp.where(left16, fa, ta), jnp.where(left16, fb, tb)
            else:
                va, vb = jnp.where(left16, ta, fa), jnp.where(left16, tb, fb)
            ha, la = split2(va)
            hb, lb = split2(vb)
            feat_ref[a, p, variant, 0:16, :] = ha
            feat_ref[a, p, variant, 16:32, :] = la
            feat_ref[a, p, variant, 32:48, :] = hb
            feat_ref[a, p, variant, 48:64, :] = lb
        norm = x * x + y * y + z * z
        tile = stack_rows(row8, [x, y, z, one, norm, h, one, jnp.zeros_like(x)])
        geo_ref[a, p] = stack_rows(row8, [x, y, z, norm, h, jnp.zeros_like(x)])
        half = jnp.concatenate(groups(*split3(tile), LEFT_ORDER) + [zero16], axis=0)
        turn_ref[a, p] = jnp.concatenate([half, half], axis=0).T

    def prepare_row(a, carry):
        for p in range(PAIRS):
            prepare(a + 1, p + 1)
        for n in range(SENDS):
            post(a * SENDS + n + 1)
        return carry

    lax.fori_loop(0, CA, prepare_row, 0)
    settle()

    def prepare_columns(a, carry):
        for p in (0, PAIRS + 1):
            prepare(a + 1, p)
        return carry

    lax.fori_loop(0, CA, prepare_columns, 0)
    for p in range(PAIRS + 2):
        prepare(0, p)
        prepare(CA + 1, p)

    def sides(a, carry):
        for p in range(PAIRS):
            keep = iota((64, 128), 1) < 64
            side_ref[a, p] = jnp.where(
                keep,
                turn_ref[a, p, 64:128, :].astype(F32),
                turn_ref[a, p + 2, 0:64, :].astype(F32),
            ).astype(BF16)
        return carry

    lax.fori_loop(0, 18, sides, 0)

    row16 = iota((16, 128), 0)
    lane16 = iota((16, 128), 1)

    def scalars(s, wide, diagonal):
        s = jnp.maximum(s, 1e-20)
        w2 = wide * wide
        e = s + (0.25 * EPS_R) * w2
        w4 = w2 * w2
        den = w4 * w4 * e
        shell = jnp.maximum(wide - s * lax.rsqrt(s), 0.0)
        base = shell * shell * shell / den
        plain = base * e
        if diagonal is not None:
            plain = jnp.where(diagonal, 0.0, plain)
        return split2(plain), split2(base * s)

    y_shift = jnp.where(left1, -2.0, 2.0)
    geo_mask = jnp.where(row8 < 3, -2.0, 0.0)
    halves = lambda parts: (
        groups(*[jnp.where(left8, t, 0.0) for t in parts], RIGHT_ORDER)
        + [zero16]
        + groups(*[jnp.where(left8, 0.0, t) for t in parts], RIGHT_ORDER)
        + [zero16]
    )

    def distances(k, sd_ref):
        a = k // PAIRS
        p = k - a * PAIRS
        geo = lambda c: geo_ref[a + 1, p + 1, c : c + 1, :]
        x, y, norm, h = geo(0), geo(1), geo(3), geo(4)
        flat = geo_ref[a + 1, p + 1] * geo_mask
        wide_parts = split3(jnp.where(row8 == 5, 1.0, jnp.where(row8 == 6, h, 0.0)))
        wide_mid = jnp.concatenate(groups(*wide_parts, RIGHT_ORDER) + [zero16], axis=0)
        wide_mix = jnp.concatenate(halves(wide_parts), axis=0)
        for sx in (-1, 0, 1):
            r = a + 1 + sx
            at = (sx + 1) * 192
            n = norm - (2.0 * sx) * x + float(sx * sx) if sx else norm
            base = flat + jnp.where(row8 == 0, 2.0 * sx, jnp.where(row8 == 4, 1.0, 0.0))
            tile = jnp.where(row8 == 3, n, base)
            right = jnp.concatenate(groups(*split3(tile), RIGHT_ORDER) + [zero16], axis=0)
            sd_ref[at : at + 128, :] = jnp.dot(
                turn_ref[r, p + 1][:, 0:64],
                jnp.concatenate([right, wide_mid], axis=1),
                preferred_element_type=F32,
            )
            nm = n - 2.0 * y_shift * y + 4.0
            tile = jnp.where(row8 == 3, nm, base + jnp.where(row8 == 1, 2.0 * y_shift, 0.0))
            right = jnp.concatenate(halves(split3(tile)), axis=0)
            sd_ref[at + 128 : at + 192, :] = jnp.dot(
                side_ref[r, p],
                jnp.concatenate([right, wide_mix], axis=1),
                preferred_element_type=F32,
            )

    def weigh(sd_ref, mid_ref, mix_ref):
        for t in range(3):
            for c in range(12):
                at = t * 192 + c * 16
                diagonal = (row16 + c * 16 == lane16) if t == 1 and c < 8 else None
                (ah, al), (bh, bl) = scalars(
                    sd_ref[at : at + 16, 0:128], sd_ref[at : at + 16, 128:256], diagonal
                )
                if c < 8:
                    lo, step, ref = c * 16, 128, mid_ref
                else:
                    lo, step, ref = (c - 8) * 16, 64, mix_ref
                ref[t, 0, lo : lo + 16, :] = ah
                ref[t, 0, step + lo : step + lo + 16, :] = al
                ref[t, 1, lo : lo + 16, :] = bh
                ref[t, 1, step + lo : step + lo + 16, :] = bl

    def gather(k, mid_ref, mix_ref):
        a = k // PAIRS
        p = k - a * PAIRS
        sums = [zero8 for _ in range(4)]
        for sx in (-1, 0, 1):
            r = a + 1 + sx
            mid = feat_ref[r, p + 1, 0]
            fa = jnp.concatenate([mid[0:32], mid[0:32]], axis=1)
            fb = jnp.concatenate([mid[32:64], mid[32:64]], axis=1)
            ga = jnp.dot(fa, mid_ref[sx + 1, 0], preferred_element_type=F32)
            gb = jnp.dot(fb, mid_ref[sx + 1, 1], preferred_element_type=F32)
            side_l = feat_ref[r, p, 2]
            side_r = feat_ref[r, p + 2, 1]
            xa = jnp.dot(
                jnp.concatenate([side_l[0:32], side_r[0:32]], axis=0),
                mix_ref[sx + 1, 0],
                preferred_element_type=F32,
            )
            xb = jnp.dot(
                jnp.concatenate([side_l[32:64], side_r[32:64]], axis=0),
                mix_ref[sx + 1, 1],
                preferred_element_type=F32,
            )
            ga = ga[0:16] + ga[16:32]
            gb = gb[0:16] + gb[16:32]
            xa = jnp.where(left16, xa[0:16] + xa[16:32], xa[32:48] + xa[48:64])
            xb = jnp.where(left16, xb[0:16] + xb[16:32], xb[32:48] + xb[48:64])
            by_x = jnp.where(row8 < 3, float(sx), 0.0)
            by_y = jnp.where((row8 >= 3) & (row8 < 6), y_shift, 0.0)
            sums[0] = sums[0] + (ga[0:8] + xa[0:8])
            sums[1] = sums[1] + (ga[8:16] + xa[8:16] + by_y * xa[0:8])
            if sx:
                sums[1] = sums[1] + by_x * (ga[0:8] + xa[0:8])
            sums[2] = sums[2] + (gb[0:8] + xb[0:8])
            sums[3] = sums[3] + (gb[8:16] + xb[8:16])
        v0, v1, v2, v3 = sums
        geo = lambda c: geo_ref[a + 1, p + 1, c : c + 1, :]
        x, y, z = geo(0), geo(1), geo(2)
        row = lambda c: ext_ref[a + 1, p + 1, c : c + 1, :]
        u, v, w = row(3), row(4), row(5)
        sm, smp = v0[0:1], v0[1:2]
        gx = x * sm - v1[0:1]
        gy = y * sm - v1[3:4]
        gz = z * sm - v0[7:8]
        density = (
            u * gx
            - (x * v0[2:3] - v1[2:3])
            + v * gy
            - (y * v0[5:6] - v1[5:6])
            + w * gz
            - (z * v0[6:7] - v1[7:8])
        )
        pi, visc, inv = row(7), row(8), row(9)
        smi, smv = v2[0:1], v2[5:6]
        ax = visc * (u * smi - v2[1:2]) + inv * (u * smv - v2[6:7])
        ay = visc * (v * smi - v2[2:3]) + inv * (v * smv - v2[7:8])
        az = visc * (w * smi - v2[3:4]) + inv * (w * smv - v3[0:1])
        ax = ax - (pi * gx + (x * smp - v1[1:2]))
        ay = ay - (pi * gy + (y * smp - v1[4:5]))
        az = az - (pi * gz + (z * smp - v1[6:7]))
        heat = (2.0 * KAPPA) * inv * (row(11) * smi - v2[4:5])
        for n, line in enumerate((density, ax, ay, az, heat)):
            out_ref[a, p, n : n + 1, :] = line

    def wall_side(k):
        a = k // PAIRS
        p = k - a * PAIRS
        row = lambda c: ext_ref[a + 1, p + 1, c : c + 1, :]
        x = row(0) - 0.5
        y = row(1) - 0.5
        z = row(2) - 2.0
        h = row(10)
        s = 0.25 / (h * h)
        norm = x * x + y * y + z * z
        rows = s * stack_rows(
            row8, [-2.0 * x, -2.0 * y, -2.0 * z, jnp.ones_like(x), norm, jnp.zeros_like(x)]
        )
        half = jnp.concatenate(groups(*split3(rows), LEFT_ORDER) + [zero16], axis=0)
        both = jnp.concatenate([half, half], axis=0).T
        lhs_ref[2 * k] = both[:64]
        lhs_ref[2 * k + 1] = both[64:]

    last = CA * PAIRS - 1
    slots = ((sd0, mid0, mix0), (sd1, mid1, mix1))
    for _, mid_ref, mix_ref in slots:
        mid_ref[...] = jnp.zeros(mid_ref.shape, BF16)
        mix_ref[...] = jnp.zeros(mix_ref.shape, BF16)
    distances(0, sd0)

    def step(m, carry):
        for odd in range(2):
            k = 2 * m + odd
            sd_ref, mid_ref, mix_ref = slots[odd]
            sd_next, mid_last, mix_last = slots[1 - odd]
            gather(jnp.clip(k - 1, 0, last), mid_last, mix_last)
            distances(jnp.minimum(k + 1, last), sd_next)
            weigh(sd_ref, mid_ref, mix_ref)
            wall_side(jnp.minimum(k, last))
            for n in range(STEP_SENDS):
                post(CA * SENDS + k * STEP_SENDS + n + 1)
        return carry

    lax.fori_loop(0, CA * PAIRS // 2 + 1, step, 0)


def exchange_kernel(
    devices,
    counts_ref,
    fluid_hbm,
    wall_hbm,
    readers_hbm,
    targets_hbm,
    out_ref,
    rec_ref,
    lhs_hbm,
    recv_ref,
    lhs_ref,
    fluid_ref,
    wall_ref,
    readers_ref,
    targets_ref,
    send_ref,
    sel_ref,
    rhs_ref,
    ext_ref,
    *rest,
):
    scratch, (load_sem, wall_send, wall_recv, own_sem, halo_send, halo_recv) = rest[:-6], rest[-6:]
    gx, gy = lax.axis_index("gx"), lax.axis_index("gy")
    nx, ny = lax.axis_size("gx"), lax.axis_size("gy")
    me = gx * ny + gy
    loads = [
        pltpu.make_async_copy(src, dst, load_sem.at[n])
        for n, (src, dst) in enumerate(
            [
                (readers_hbm, readers_ref),
                (targets_hbm, targets_ref),
                (wall_hbm, wall_ref),
                (fluid_hbm, fluid_ref),
            ]
        )
    ]
    for load in loads[::-1]:
        load.start()
    barrier = pltpu.get_barrier_semaphore()

    def greet(d):
        other = lax.rem(me + d, devices)

        @pl.when(d < devices)
        def _():
            pl.semaphore_signal(
                barrier,
                inc=1,
                device_id=(other // ny, lax.rem(other, ny)),
                device_id_type=pl.DeviceIdType.MESH,
            )

    blank = jnp.zeros((16, 128), F32)

    @pl.when(gx == 0)
    def _():
        for p in range(6):
            ext_ref[0, p] = blank

    @pl.when(gx == nx - 1)
    def _():
        for p in range(6):
            ext_ref[CA + 1, p] = blank

    @pl.when(gy == 0)
    def _():
        for a in range(CA + 2):
            ext_ref[a, 0] = blank

    @pl.when(gy == ny - 1)
    def _():
        for a in range(CA + 2):
            ext_ref[a, PAIRS + 1] = blank

    loads[3].wait()
    pack_records(counts_ref, fluid_ref, rec_ref, greet)
    for load in loads[:3]:
        load.wait()
    route_walls(devices, wall_ref, readers_ref, targets_ref, send_ref, sel_ref, rhs_ref)

    def keep(a, carry):
        for p in range(PAIRS):
            ext_ref[a + 1, p + 1] = rec_ref[a, p]
        return carry

    lax.fori_loop(0, CA, keep, 0)
    pl.semaphore_wait(barrier, devices - 1)

    rows = {-1: (0, CA + 1), 1: (CA - 1, 0)}
    cols = {-1: (0, PAIRS + 1), 1: (PAIRS - 1, 0)}
    halos = []
    for n, (dx, dy) in enumerate(
        [(0, 1), (0, -1), (1, 0), (-1, 0), (1, 1), (1, -1), (-1, 1), (-1, -1)]
    ):
        src_a, dst_a = rows[dx] if dx else (pl.ds(0, CA), pl.ds(1, CA))
        src_p, dst_p = cols[dy] if dy else (pl.ds(0, PAIRS), pl.ds(1, PAIRS))
        to_x, to_y = gx + dx, gy + dy
        sends = (to_x >= 0) & (to_x < nx) & (to_y >= 0) & (to_y < ny)
        from_x, from_y = gx - dx, gy - dy
        receives = (from_x >= 0) & (from_x < nx) & (from_y >= 0) & (from_y < ny)
        copy = pltpu.make_async_remote_copy(
            src_ref=rec_ref.at[src_a, src_p],
            dst_ref=ext_ref.at[dst_a, dst_p],
            send_sem=halo_send.at[n],
            recv_sem=halo_recv.at[n],
            device_id=(jnp.clip(to_x, 0, nx - 1), jnp.clip(to_y, 0, ny - 1)),
            device_id_type=pl.DeviceIdType.MESH,
        )
        halos.append((sends, receives, copy))
        pl.when(sends)(copy.start)

    used = pl.ds(0, 33)
    own_copy = pltpu.make_async_copy(send_ref.at[me, used], recv_ref.at[me, used], own_sem)
    own_copy.start()

    def post(d):
        other = lax.rem(me + d * 37, devices)

        @pl.when(d < devices)
        def _():
            pltpu.make_async_remote_copy(
                src_ref=send_ref.at[other, used],
                dst_ref=recv_ref.at[me, used],
                send_sem=wall_send,
                recv_sem=wall_recv,
                device_id=(other // ny, lax.rem(other, ny)),
                device_id_type=pl.DeviceIdType.MESH,
            ).start()

    def settle():
        for sends, receives, copy in halos:
            pl.when(receives)(copy.wait_recv)

    near_compute(post, settle, ext_ref, out_ref, lhs_ref, *scratch)
    leave = pltpu.make_async_copy(lhs_ref, lhs_hbm, load_sem.at[0])
    leave.start()
    for sends, receives, copy in halos:
        pl.when(sends)(copy.wait_send)
    own_copy.wait()
    everyone = recv_ref.at[pl.ds(0, devices - 1), used]
    pltpu.make_async_copy(everyone, everyone, wall_send).wait()
    pltpu.make_async_copy(everyone, everyone, wall_recv).wait()
    leave.wait()


def near_and_exchange(devices, counts_t, fluid_state, wall_blocks, readers_t, targets_t):
    walls = wall_blocks.shape[0]
    vmem = pl.BlockSpec(memory_space=pltpu.VMEM)
    anywhere = pl.BlockSpec(memory_space=pl.ANY)
    hbm = pl.BlockSpec(memory_space=pltpu.HBM)
    return pl.pallas_call(
        lambda *refs: exchange_kernel(devices, *refs),
        out_shape=(
            jax.ShapeDtypeStruct((CA, PAIRS, 8, 128), F32),
            jax.ShapeDtypeStruct((CA, PAIRS, 16, 128), F32),
            jax.ShapeDtypeStruct((CA * CB, 64, 128), BF16),
            jax.ShapeDtypeStruct((devices, 40, 128), F32),
        ),
        in_specs=[pl.BlockSpec(memory_space=pltpu.SMEM)] + [hbm] * 4,
        out_specs=[vmem, vmem, anywhere, anywhere],
        scratch_shapes=[
            pltpu.VMEM((CA * CB, 64, 128), BF16),
            pltpu.VMEM(fluid_state.shape, F32),
            pltpu.VMEM(wall_blocks.shape, F32),
            pltpu.VMEM(readers_t.shape, jnp.int32),
            pltpu.VMEM(targets_t.shape, jnp.int32),
            pltpu.VMEM((devices, 40, 128), F32),
            pltpu.VMEM((devices * SLOTS // 2, 2 * walls), BF16),
            pltpu.VMEM((2 * walls, 384), BF16),
            pltpu.VMEM((18, 6, 16, 128), F32),
            pltpu.VMEM((18, 6, 3, 64, 128), BF16),
            pltpu.VMEM((18, 6, 128, 128), BF16),
            pltpu.VMEM((18, PAIRS, 64, 128), BF16),
            pltpu.VMEM((18, 6, 8, 128), F32),
        ]
        + [
            pltpu.VMEM((576, 256), F32),
            pltpu.VMEM((3, 2, 256, 128), BF16),
            pltpu.VMEM((3, 2, 128, 128), BF16),
        ]
        * 2
        + [
            pltpu.SemaphoreType.DMA((4,)),
            pltpu.SemaphoreType.DMA,
            pltpu.SemaphoreType.DMA,
            pltpu.SemaphoreType.DMA,
            pltpu.SemaphoreType.DMA((8,)),
            pltpu.SemaphoreType.DMA((8,)),
        ],
        compiler_params=pltpu.CompilerParams(
            vmem_limit_bytes=26 << 20, collective_id=0, has_side_effects=True
        ),
        name="near_and_exchange",
    )(
        counts_t,
        *[
            pltpu.with_memory_space_constraint(array, pltpu.HBM)
            for array in (fluid_state, wall_blocks, readers_t, targets_t)
        ],
    )


UNROLL = 16


def wall_kernel(
    recv_ref,
    rec_ref,
    near_ref,
    lhs_hbm,
    rates_ref,
    dens_ref,
    lhs_ref,
    acc_ref,
    turn_ref,
    cells_ref,
    list_ref,
    sems,
):
    enter = pltpu.make_async_copy(lhs_hbm, lhs_ref, sems.at[0])
    enter.start()
    turn_ref[...] = recv_ref[:, 32, :].astype(jnp.int32)
    spread = pltpu.make_async_copy(turn_ref, cells_ref, sems.at[1])
    spread.start()
    spread.wait()
    lane1 = iota((1, 128), 1)
    left1 = lane1 < 64
    row8 = iota((8, 128), 0)
    left8 = iota((8, 128), 1) < 64
    zero8 = jnp.zeros((8, 128), F32)
    zero16 = jnp.zeros((16, 128), BF16)

    def listing(src, m):
        for q in range(SLOTS // 2):
            list_ref[m + q] = src * (SLOTS // 2) + q
        return m + (cells_ref[src, SLOTS] + 1) // 2

    def clear(a, m):
        for n in range(CB):
            acc_ref[a * CB + n] = zero8
        for n in range(recv_ref.shape[0] // CA):
            m = listing(a * (recv_ref.shape[0] // CA) + n, m)
        return m

    live = lax.fori_loop(0, CA, clear, 0)
    for q in range(UNROLL):
        list_ref[live + q] = 0

    enter.wait()
    center = jnp.where(row8 == 2, 2.0, jnp.where(row8 < 2, 0.5, 0.0))

    def block(k, carry):
        ids, tiles, squares = [], [], []
        for u in range(UNROLL):
            at = k * UNROLL + u
            pair = list_ref[at]
            src = pair // (SLOTS // 2)
            q = pair - src * (SLOTS // 2)
            ca = cells_ref[src, 2 * q]
            cb = cells_ref[src, 2 * q + 1]
            ids.append((ca, cb))
            tile = recv_ref[src, pl.ds(pl.multiple_of(q * 8, 8), 8), :]
            tiles.append(jnp.where(at < live, tile, 0.0))
            c = tile - center
            sq = c * c
            norm = sq[0:1] + sq[1:2] + sq[2:3]
            rows = jnp.where(
                row8 < 3, c, jnp.where(row8 == 3, norm, jnp.where(row8 == 4, 1.0, 0.0))
            )
            parts = split3(rows)
            lefts = groups(*[jnp.where(left8, t, 0.0) for t in parts], RIGHT_ORDER) + [zero16]
            rights = groups(*[jnp.where(left8, 0.0, t) for t in parts], RIGHT_ORDER) + [zero16]
            right = jnp.concatenate(lefts + rights, axis=0)
            lhs = jnp.concatenate([lhs_ref[ca][:, 0:64], lhs_ref[cb][:, 64:128]], axis=1)
            squares.append(jnp.dot(lhs, right, preferred_element_type=F32))
        weights = []
        for u in range(UNROLL):
            q2 = jnp.maximum(squares[u], 1e-20)
            t = q2 * lax.rsqrt(q2)
            shell = jnp.maximum(1.0 - t, 0.0)
            shell = shell * shell
            weights.append(jnp.concatenate(split2(shell * shell * (4.0 * t + 1.0)), axis=0))
        outs, lines = [], []
        for u in range(UNROLL):
            tile = tiles[u]
            high = tile.astype(BF16).astype(F32)
            low = tile - high
            feats = jnp.concatenate(
                [
                    jnp.concatenate([jnp.where(left8, high, 0.0), jnp.where(left8, low, 0.0)], axis=0),
                    jnp.concatenate([jnp.where(left8, 0.0, high), jnp.where(left8, 0.0, low)], axis=0),
                ],
                axis=0,
            ).astype(BF16)
            blank = jnp.zeros((32, 128), BF16)
            lines.append(
                jnp.concatenate([blank, feats] if u % 2 else [feats, blank], axis=1)
            )
            if u % 2:
                got = lax.dot_general(
                    jnp.concatenate(lines, axis=0),
                    jnp.concatenate([weights[u - 1], weights[u]], axis=1),
                    (((1,), (1,)), ((), ())),
                    preferred_element_type=F32,
                )
                outs += [got[0:32], got[32:64]]
                lines = []
        for u in range(UNROLL):
            ca, cb = ids[u]
            got = outs[u]
            acc_ref[ca] = acc_ref[ca] + (got[0:8] + got[8:16])
            acc_ref[cb] = acc_ref[cb] + (got[16:24] + got[24:32])
        return carry

    lax.fori_loop(0, (live + UNROLL - 1) // UNROLL, block, 0)

    def finish(a, carry):
        for p in range(PAIRS):
            ta = acc_ref[a * CB + 2 * p]
            tb = acc_ref[a * CB + 2 * p + 1]
            total = jnp.where(left8, ta + pltpu.roll(ta, 64, 1), tb + pltpu.roll(tb, 64, 1))
            tile = rec_ref[a, p]
            near = near_ref[a, p]
            h, sound = tile[10:11], tile[12:13]
            scale = KERN_W / (h * h * h)
            push = WALL_PUSH * sound * sound * scale
            heat = WALL_HEAT * scale * (total[7:8] - tile[11:12] * total[6:7])
            r = [near[1 + n : 2 + n] + push * total[3 + n : 4 + n] for n in range(3)]
            r.append(near[4:5] + heat)
            t = [pltpu.roll(line, 64, 1) for line in r]
            for v in range(2):
                lo, hi = 2 * v, 2 * v + 1
                span = slice(v * 128, (v + 1) * 128)
                rates_ref[a, 2 * p : 2 * p + 1, span] = jnp.where(left1, r[lo], t[hi])
                rates_ref[a, 2 * p + 1 : 2 * p + 2, span] = jnp.where(left1, t[lo], r[hi])
            dens_ref[a, p : p + 1, :] = near[0:1]
        return carry

    lax.fori_loop(0, CA, finish, 0)


def wall_terms(recv, records, near, sides):
    return pl.pallas_call(
        wall_kernel,
        out_shape=(
            jax.ShapeDtypeStruct((CA, CB, 256), F32),
            jax.ShapeDtypeStruct((CA, PAIRS, 128), F32),
        ),
        in_specs=[pl.BlockSpec(memory_space=pltpu.VMEM)] * 3
        + [pl.BlockSpec(memory_space=pl.ANY)],
        out_specs=[pl.BlockSpec(memory_space=pltpu.VMEM)] * 2,
        scratch_shapes=[
            pltpu.VMEM((CA * CB, 64, 128), BF16),
            pltpu.VMEM((CA * CB, 8, 128), F32),
            pltpu.VMEM((recv.shape[0], 128), jnp.int32),
            pltpu.SMEM((recv.shape[0], 128), jnp.int32),
            pltpu.SMEM((recv.shape[0] * SLOTS // 2 + UNROLL + 8,), jnp.int32),
            pltpu.SemaphoreType.DMA((2,)),
        ],
        compiler_params=pltpu.CompilerParams(vmem_limit_bytes=10 << 20),
        name="wall_terms",
    )(recv, records, near, sides)


def local(fluid_state, cell_counts, wall_blocks, readers, targets):
    devices = lax.axis_size("gx") * lax.axis_size("gy")
    near, records, sides, recv = near_and_exchange(
        devices, cell_counts.T, fluid_state, wall_blocks, readers.T, targets.T
    )
    rates, density = wall_terms(recv, records, near, sides)
    return (rates, density.reshape(CA, CB * 64))


def solution(mesh):
    placed = (
        P("gx", "gy", None),
        P("gx", "gy"),
        P(("gx", "gy"), None),
        P(("gx", "gy"), None),
        P(("gx", "gy"), None),
    )
    return jax.shard_map(
        local,
        mesh=mesh,
        in_specs=placed,
        out_specs=(P("gx", "gy", None), P("gx", "gy")),
        check_vma=False,
    )
```

```python
import math

import jax
import jax.numpy as jnp
from jax import lax
from jax.experimental import pallas as pl
from jax.experimental.pallas import tpu as pltpu
from jax.sharding import PartitionSpec as P

CA = 16
CB = 8
PAIRS = 4
SLOTS = 8
SENDS = 1
STEP_SENDS = 2
KERN_W = 21.0 / (16.0 * math.pi)
KERN_F = 105.0 / (16.0 * math.pi)
KAPPA = 0.02
WALL_PUSH = 0.03
WALL_HEAT = 0.02
EPS_R = 0.01
F32 = jnp.float32
BF16 = jnp.bfloat16


def iota(shape, axis):
    return lax.broadcasted_iota(jnp.int32, shape, axis)


def split2(value):
    high = value.astype(BF16)
    low = (value - high.astype(F32)).astype(BF16)
    return high, low


def split3(value):
    high = value.astype(BF16).astype(F32)
    rest = value - high
    middle = rest.astype(BF16).astype(F32)
    return high, middle, rest - middle


def pack_records(counts_ref, fluid_ref, out_ref, greet):
    lane = iota((8, 128), 1)
    left = lane < 64
    slot = lane - jnp.where(left, 0, 64)

    def row(a, carry):
        comps = []
        for v in range(6):
            x = fluid_ref[a, :, v * 128 : (v + 1) * 128]
            turned = pltpu.roll(x, 64, 1)
            comps.append(jnp.where(left, x, pltpu.roll(turned, 7, 0)))
            comps.append(jnp.where(left, turned, pltpu.roll(x, 7, 0)))
        density, smooth, sound = comps[7], comps[8], comps[9]
        inverse = 1.0 / density
        d2 = density * density
        d4 = d2 * d2
        pressure = sound * sound / 7.0 * (d4 * d2 * density - 1.0)
        fields = comps[:6] + [
            comps[6],
            pressure * inverse * inverse,
            comps[10] * inverse,
            inverse,
            smooth,
            comps[11],
            sound,
        ]
        for p in range(PAIRS):
            count = jnp.where(left[:1], counts_ref[2 * p, a], counts_ref[2 * p + 1, a])
            for c, field in enumerate(fields):
                line = field[2 * p : 2 * p + 1]
                if c == 6:
                    line = jnp.where(slot[:1] < count, line, 0.0)
                out_ref[a, p, c : c + 1, :] = line
            out_ref[a, p, 13:16, :] = jnp.zeros((3, 128), F32)
        for n in range(SLOTS):
            greet(a * SLOTS + n + 1)
        return carry

    lax.fori_loop(0, CA, row, 0)


def route_walls(devices, wall_ref, readers_ref, targets_ref, out_ref, sel_ref, rhs_ref):
    rows = wall_ref.shape[0]
    lane = iota((rows, 128), 1)
    left = lane < 64
    later = (iota((rows, rows), 0) < iota((rows, rows), 1)).astype(BF16)
    device = iota((devices, rows), 0)
    before = jnp.zeros((devices, 1), F32)
    slots = []
    cells = jnp.zeros((devices, 128), F32)
    slot_row = iota((128, rows), 0).astype(F32)
    for r in range(2):
        reader = readers_ref[r : r + 1, :]
        hot = (device == reader).astype(F32)
        earlier = jnp.dot(hot.astype(BF16), later, preferred_element_type=F32) + before
        position = jnp.sum(hot * earlier, axis=0, keepdims=True)
        before = before + jnp.sum(hot, axis=1, keepdims=True)
        slots.append(reader * SLOTS + position.astype(jnp.int32))
        named = jnp.where(slot_row == position, targets_ref[r : r + 1, :].astype(F32), 0.0)
        named = jnp.where(slot_row == SLOTS, 1.0, named)
        cells = cells + lax.dot_general(
            hot.astype(BF16),
            named.astype(BF16),
            (((1,), (1,)), ((), ())),
            preferred_element_type=F32,
        )
    chunk = devices * SLOTS // 2
    pair = iota((chunk, rows), 0) * 2
    for half in range(2):
        chosen = (pair + half == slots[0]) | (pair + half == slots[1])
        sel_ref[:, half * rows : (half + 1) * rows] = jnp.where(chosen, 1.0, 0.0).astype(BF16)
    gamma = wall_ref[:, 384:512]
    gamma = jnp.where(left, gamma, pltpu.roll(gamma, 64, 1))
    for v in range(4):
        x = wall_ref[:, v * 128 : (v + 1) * 128]
        if v == 1:
            x = jnp.where(left, x, x * gamma)
        elif v == 2:
            x = x * gamma
        elif v == 3:
            x = jnp.where(left, x, x * gamma)
        turned = pltpu.roll(x, 64, 1)
        for odd in range(2):
            even_half = jnp.where(left, turned if odd else x, 0.0)
            odd_half = jnp.where(left, 0.0, x if odd else turned)
            for part, (e, o) in enumerate(zip(split3(even_half), split3(odd_half))):
                rhs_ref[0:rows, part * 128 : (part + 1) * 128] = e.astype(BF16)
                rhs_ref[rows : 2 * rows, part * 128 : (part + 1) * 128] = o.astype(BF16)
            got = jnp.dot(sel_ref[...], rhs_ref[...], preferred_element_type=F32)
            got = got[:, 0:128] + got[:, 128:256] + got[:, 256:384]
            got = got.reshape(devices, SLOTS // 2, 128)
            for q in range(SLOTS // 2):
                out_ref[:, q * 8 + 2 * v + odd, :] = got[:, q, :]
    out_ref[:, 32, :] = cells


def stack_rows(row8, rows):
    out = jnp.broadcast_to(rows[0], row8.shape)
    for n in range(1, len(rows)):
        out = jnp.where(row8 == n, rows[n], out)
    return out


def groups(high, middle, low, order):
    parts = {"h": high, "m": middle, "l": low}
    return [
        jnp.concatenate([parts[pair[0]], parts[pair[1]]], axis=0).astype(BF16) for pair in order
    ]


LEFT_ORDER = ("hh", "mh", "ml")
RIGHT_ORDER = ("hm", "hl", "mh")


def near_compute(
    post, settle, ext_ref, out_ref, side_out, feat_ref, turn_ref, side_ref, geo_ref, sd0, mid0, mix0, sd1, mid1, mix1
):
    left1 = iota((1, 128), 1) < 64
    left8 = iota((8, 128), 1) < 64
    left16 = iota((16, 128), 1) < 64
    row8 = iota((8, 128), 0)
    zero8 = jnp.zeros((8, 128), F32)
    zero16 = jnp.zeros((16, 128), BF16)
    own = jnp.where(left1, -1.0, 0.0)

    def prepare(a, p):
        row = lambda c: ext_ref[a, p, c : c + 1, :]
        x = row(0) - 0.5
        y = row(1) + own
        z = row(2) - 2.0
        u, v, w, mass = row(3), row(4), row(5), row(6) * (-32.0 * KERN_F)
        pres, visc, inv, h, heat = row(7), row(8), row(9), row(10), row(11)
        one = jnp.ones_like(x)
        head = [one, pres, u, one, pres, v]
        v0 = mass * stack_rows(row8, head + [w, z])
        place = jnp.where(row8 < 3, x, jnp.where(row8 < 6, y, z))
        v1 = mass * stack_rows(row8, head + [pres, w]) * place
        v2 = mass * jnp.where(row8 < 5, inv, visc)
        v2 = v2 * stack_rows(row8, [one, u, v, w, heat, one, u, v])
        v3 = jnp.where(row8 == 0, mass * visc * w, 0.0)
        fa = jnp.concatenate([v0, v1], axis=0)
        fb = jnp.concatenate([v2, v3], axis=0)
        turned = [pltpu.roll(t, 64, 1) for t in (v0, v1, v2, v3)]
        ta = jnp.concatenate(turned[:2], axis=0)
        tb = jnp.concatenate(turned[2:], axis=0)
        for variant in ((2,) if p == 0 else (1,) if p == 5 else (0, 1, 2)):
            if variant == 0:
                va, vb = fa, fb
            elif variant == 1:
                va, vb = jnp.where(left16, fa, ta), jnp.where(left16, fb, tb)
            else:
                va, vb = jnp.where(left16, ta, fa), jnp.where(left16, tb, fb)
            ha, la = split2(va)
            hb, lb = split2(vb)
            feat_ref[a, p, variant, 0:16, :] = ha
            feat_ref[a, p, variant, 16:32, :] = la
            feat_ref[a, p, variant, 32:48, :] = hb
            feat_ref[a, p, variant, 48:64, :] = lb
        norm = x * x + y * y + z * z
        tile = stack_rows(row8, [x, y, z, one, norm, h, one, jnp.zeros_like(x)])
        geo_ref[a, p] = stack_rows(row8, [x, y, z, norm, h, jnp.zeros_like(x)])
        half = jnp.concatenate(groups(*split3(tile), LEFT_ORDER) + [zero16], axis=0)
        turn_ref[a, p] = jnp.concatenate([half, half], axis=0).T

    def prepare_row(a, carry):
        for p in range(PAIRS):
            prepare(a + 1, p + 1)
        for n in range(SENDS):
            post(a * SENDS + n + 1)
        return carry

    lax.fori_loop(0, CA, prepare_row, 0)
    settle()

    def prepare_columns(a, carry):
        for p in (0, PAIRS + 1):
            prepare(a + 1, p)
        return carry

    lax.fori_loop(0, CA, prepare_columns, 0)
    for p in range(PAIRS + 2):
        prepare(0, p)
        prepare(CA + 1, p)

    def sides(a, carry):
        for p in range(PAIRS):
            keep = iota((64, 128), 1) < 64
            side_ref[a, p] = jnp.where(
                keep,
                turn_ref[a, p, 64:128, :].astype(F32),
                turn_ref[a, p + 2, 0:64, :].astype(F32),
            ).astype(BF16)
        return carry

    lax.fori_loop(0, 18, sides, 0)

    row16 = iota((16, 128), 0)
    lane16 = iota((16, 128), 1)

    def scalars(s, wide, diagonal):
        s = jnp.maximum(s, 1e-20)
        w2 = wide * wide
        e = s + (0.25 * EPS_R) * w2
        w4 = w2 * w2
        den = w4 * w4 * e
        shell = jnp.maximum(wide - s * lax.rsqrt(s), 0.0)
        base = shell * shell * shell / den
        plain = base * e
        if diagonal is not None:
            plain = jnp.where(diagonal, 0.0, plain)
        return split2(plain), split2(base * s)

    y_shift = jnp.where(left1, -2.0, 2.0)
    geo_mask = jnp.where(row8 < 3, -2.0, 0.0)
    halves = lambda parts: (
        groups(*[jnp.where(left8, t, 0.0) for t in parts], RIGHT_ORDER)
        + [zero16]
        + groups(*[jnp.where(left8, 0.0, t) for t in parts], RIGHT_ORDER)
        + [zero16]
    )

    def distances(k, sd_ref):
        a = k // PAIRS
        p = k - a * PAIRS
        geo = lambda c: geo_ref[a + 1, p + 1, c : c + 1, :]
        x, y, norm, h = geo(0), geo(1), geo(3), geo(4)
        flat = geo_ref[a + 1, p + 1] * geo_mask
        wide_parts = split3(jnp.where(row8 == 5, 1.0, jnp.where(row8 == 6, h, 0.0)))
        wide_mid = jnp.concatenate(groups(*wide_parts, RIGHT_ORDER) + [zero16], axis=0)
        wide_mix = jnp.concatenate(halves(wide_parts), axis=0)
        for sx in (-1, 0, 1):
            r = a + 1 + sx
            at = (sx + 1) * 192
            n = norm - (2.0 * sx) * x + float(sx * sx) if sx else norm
            base = flat + jnp.where(row8 == 0, 2.0 * sx, jnp.where(row8 == 4, 1.0, 0.0))
            tile = jnp.where(row8 == 3, n, base)
            right = jnp.concatenate(groups(*split3(tile), RIGHT_ORDER) + [zero16], axis=0)
            sd_ref[at : at + 128, :] = jnp.dot(
                turn_ref[r, p + 1][:, 0:64],
                jnp.concatenate([right, wide_mid], axis=1),
                preferred_element_type=F32,
            )
            nm = n - 2.0 * y_shift * y + 4.0
            tile = jnp.where(row8 == 3, nm, base + jnp.where(row8 == 1, 2.0 * y_shift, 0.0))
            right = jnp.concatenate(halves(split3(tile)), axis=0)
            sd_ref[at + 128 : at + 192, :] = jnp.dot(
                side_ref[r, p],
                jnp.concatenate([right, wide_mix], axis=1),
                preferred_element_type=F32,
            )

    def weigh(sd_ref, mid_ref, mix_ref):
        for t in range(3):
            for c in range(12):
                at = t * 192 + c * 16
                diagonal = (row16 + c * 16 == lane16) if t == 1 and c < 8 else None
                (ah, al), (bh, bl) = scalars(
                    sd_ref[at : at + 16, 0:128], sd_ref[at : at + 16, 128:256], diagonal
                )
                if c < 8:
                    lo, step, ref = c * 16, 128, mid_ref
                else:
                    lo, step, ref = (c - 8) * 16, 64, mix_ref
                ref[t, 0, lo : lo + 16, :] = ah
                ref[t, 0, step + lo : step + lo + 16, :] = al
                ref[t, 1, lo : lo + 16, :] = bh
                ref[t, 1, step + lo : step + lo + 16, :] = bl

    def gather(k, mid_ref, mix_ref):
        a = k // PAIRS
        p = k - a * PAIRS
        sums = [zero8 for _ in range(4)]
        for sx in (-1, 0, 1):
            r = a + 1 + sx
            mid = feat_ref[r, p + 1, 0]
            fa = jnp.concatenate([mid[0:32], mid[0:32]], axis=1)
            fb = jnp.concatenate([mid[32:64], mid[32:64]], axis=1)
            ga = jnp.dot(fa, mid_ref[sx + 1, 0], preferred_element_type=F32)
            gb = jnp.dot(fb, mid_ref[sx + 1, 1], preferred_element_type=F32)
            side_l = feat_ref[r, p, 2]
            side_r = feat_ref[r, p + 2, 1]
            xa = jnp.dot(
                jnp.concatenate([side_l[0:32], side_r[0:32]], axis=0),
                mix_ref[sx + 1, 0],
                preferred_element_type=F32,
            )
            xb = jnp.dot(
                jnp.concatenate([side_l[32:64], side_r[32:64]], axis=0),
                mix_ref[sx + 1, 1],
                preferred_element_type=F32,
            )
            ga = ga[0:16] + ga[16:32]
            gb = gb[0:16] + gb[16:32]
            xa = jnp.where(left16, xa[0:16] + xa[16:32], xa[32:48] + xa[48:64])
            xb = jnp.where(left16, xb[0:16] + xb[16:32], xb[32:48] + xb[48:64])
            by_x = jnp.where(row8 < 3, float(sx), 0.0)
            by_y = jnp.where((row8 >= 3) & (row8 < 6), y_shift, 0.0)
            sums[0] = sums[0] + (ga[0:8] + xa[0:8])
            sums[1] = sums[1] + (ga[8:16] + xa[8:16] + by_y * xa[0:8])
            if sx:
                sums[1] = sums[1] + by_x * (ga[0:8] + xa[0:8])
            sums[2] = sums[2] + (gb[0:8] + xb[0:8])
            sums[3] = sums[3] + (gb[8:16] + xb[8:16])
        v0, v1, v2, v3 = sums
        geo = lambda c: geo_ref[a + 1, p + 1, c : c + 1, :]
        x, y, z = geo(0), geo(1), geo(2)
        row = lambda c: ext_ref[a + 1, p + 1, c : c + 1, :]
        u, v, w = row(3), row(4), row(5)
        sm, smp = v0[0:1], v0[1:2]
        gx = x * sm - v1[0:1]
        gy = y * sm - v1[3:4]
        gz = z * sm - v0[7:8]
        density = (
            u * gx
            - (x * v0[2:3] - v1[2:3])
            + v * gy
            - (y * v0[5:6] - v1[5:6])
            + w * gz
            - (z * v0[6:7] - v1[7:8])
        )
        pi, visc, inv = row(7), row(8), row(9)
        smi, smv = v2[0:1], v2[5:6]
        ax = visc * (u * smi - v2[1:2]) + inv * (u * smv - v2[6:7])
        ay = visc * (v * smi - v2[2:3]) + inv * (v * smv - v2[7:8])
        az = visc * (w * smi - v2[3:4]) + inv * (w * smv - v3[0:1])
        ax = ax - (pi * gx + (x * smp - v1[1:2]))
        ay = ay - (pi * gy + (y * smp - v1[4:5]))
        az = az - (pi * gz + (z * smp - v1[6:7]))
        heat = (2.0 * KAPPA) * inv * (row(11) * smi - v2[4:5])
        for n, line in enumerate((density, ax, ay, az, heat)):
            out_ref[a, p, n : n + 1, :] = line

    def wall_side(k):
        a = k // PAIRS
        p = k - a * PAIRS
        row = lambda c: ext_ref[a + 1, p + 1, c : c + 1, :]
        x = row(0) - 0.5
        y = row(1) - 0.5
        z = row(2) - 2.0
        h = row(10)
        s = 0.25 / (h * h)
        norm = x * x + y * y + z * z
        rows = s * stack_rows(
            row8, [-2.0 * x, -2.0 * y, -2.0 * z, jnp.ones_like(x), norm, jnp.zeros_like(x)]
        )
        here, there = split3(rows), split3(pltpu.roll(rows, 64, 1))
        for n, side, parts in ((0, 0, here), (0, 1, there), (1, 0, there), (1, 1, here)):
            kept = [jnp.where(left8, 0.0, t) if side else jnp.where(left8, t, 0.0) for t in parts]
            side_out[2 * k + n, side] = jnp.concatenate(
                groups(*kept, RIGHT_ORDER) + [zero16], axis=0
            )

    last = CA * PAIRS - 1
    slots = ((sd0, mid0, mix0), (sd1, mid1, mix1))
    for _, mid_ref, mix_ref in slots:
        mid_ref[...] = jnp.zeros(mid_ref.shape, BF16)
        mix_ref[...] = jnp.zeros(mix_ref.shape, BF16)
    distances(0, sd0)

    def step(m, carry):
        for odd in range(2):
            k = 2 * m + odd
            sd_ref, mid_ref, mix_ref = slots[odd]
            sd_next, mid_last, mix_last = slots[1 - odd]
            gather(jnp.clip(k - 1, 0, last), mid_last, mix_last)
            distances(jnp.minimum(k + 1, last), sd_next)
            weigh(sd_ref, mid_ref, mix_ref)
            wall_side(jnp.minimum(k, last))
            for n in range(STEP_SENDS):
                post(CA * SENDS + k * STEP_SENDS + n + 1)
        return carry

    lax.fori_loop(0, CA * PAIRS // 2, step, 0)
    gather(last, mid1, mix1)


def exchange_kernel(
    devices,
    counts_ref,
    fluid_hbm,
    wall_hbm,
    readers_hbm,
    targets_hbm,
    out_ref,
    rec_ref,
    side_out,
    recv_ref,
    fluid_ref,
    wall_ref,
    readers_ref,
    targets_ref,
    send_ref,
    sel_ref,
    rhs_ref,
    ext_ref,
    *rest,
):
    scratch, (load_sem, wall_send, wall_recv, own_sem, halo_send, halo_recv) = rest[:-6], rest[-6:]
    gx, gy = lax.axis_index("gx"), lax.axis_index("gy")
    nx, ny = lax.axis_size("gx"), lax.axis_size("gy")
    me = gx * ny + gy
    loads = [
        pltpu.make_async_copy(src, dst, load_sem.at[n])
        for n, (src, dst) in enumerate(
            [
                (readers_hbm, readers_ref),
                (targets_hbm, targets_ref),
                (wall_hbm, wall_ref),
                (fluid_hbm, fluid_ref),
            ]
        )
    ]
    for load in loads[::-1]:
        load.start()
    barrier = pltpu.get_barrier_semaphore()

    def greet(d):
        other = lax.rem(me + d, devices)

        @pl.when(d < devices)
        def _():
            pl.semaphore_signal(
                barrier,
                inc=1,
                device_id=(other // ny, lax.rem(other, ny)),
                device_id_type=pl.DeviceIdType.MESH,
            )

    blank = jnp.zeros((16, 128), F32)

    @pl.when(gx == 0)
    def _():
        for p in range(6):
            ext_ref[0, p] = blank

    @pl.when(gx == nx - 1)
    def _():
        for p in range(6):
            ext_ref[CA + 1, p] = blank

    @pl.when(gy == 0)
    def _():
        for a in range(CA + 2):
            ext_ref[a, 0] = blank

    @pl.when(gy == ny - 1)
    def _():
        for a in range(CA + 2):
            ext_ref[a, PAIRS + 1] = blank

    loads[3].wait()
    pack_records(counts_ref, fluid_ref, rec_ref, greet)
    for load in loads[:3]:
        load.wait()
    route_walls(devices, wall_ref, readers_ref, targets_ref, send_ref, sel_ref, rhs_ref)

    def keep(a, carry):
        for p in range(PAIRS):
            ext_ref[a + 1, p + 1] = rec_ref[a, p]
        return carry

    lax.fori_loop(0, CA, keep, 0)
    pl.semaphore_wait(barrier, devices - 1)

    rows = {-1: (0, CA + 1), 1: (CA - 1, 0)}
    cols = {-1: (0, PAIRS + 1), 1: (PAIRS - 1, 0)}
    halos = []
    for n, (dx, dy) in enumerate(
        [(0, 1), (0, -1), (1, 0), (-1, 0), (1, 1), (1, -1), (-1, 1), (-1, -1)]
    ):
        src_a, dst_a = rows[dx] if dx else (pl.ds(0, CA), pl.ds(1, CA))
        src_p, dst_p = cols[dy] if dy else (pl.ds(0, PAIRS), pl.ds(1, PAIRS))
        to_x, to_y = gx + dx, gy + dy
        sends = (to_x >= 0) & (to_x < nx) & (to_y >= 0) & (to_y < ny)
        from_x, from_y = gx - dx, gy - dy
        receives = (from_x >= 0) & (from_x < nx) & (from_y >= 0) & (from_y < ny)
        copy = pltpu.make_async_remote_copy(
            src_ref=rec_ref.at[src_a, src_p],
            dst_ref=ext_ref.at[dst_a, dst_p],
            send_sem=halo_send.at[n],
            recv_sem=halo_recv.at[n],
            device_id=(jnp.clip(to_x, 0, nx - 1), jnp.clip(to_y, 0, ny - 1)),
            device_id_type=pl.DeviceIdType.MESH,
        )
        halos.append((sends, receives, copy))
        pl.when(sends)(copy.start)

    used = pl.ds(0, 33)
    own_copy = pltpu.make_async_copy(send_ref.at[me, used], recv_ref.at[me, used], own_sem)
    own_copy.start()

    def post(d):
        other = lax.rem(me + d * 37, devices)

        @pl.when(d < devices)
        def _():
            pltpu.make_async_remote_copy(
                src_ref=send_ref.at[other, used],
                dst_ref=recv_ref.at[me, used],
                send_sem=wall_send,
                recv_sem=wall_recv,
                device_id=(other // ny, lax.rem(other, ny)),
                device_id_type=pl.DeviceIdType.MESH,
            ).start()

    def settle():
        for sends, receives, copy in halos:
            pl.when(receives)(copy.wait_recv)

    near_compute(post, settle, ext_ref, out_ref, side_out, *scratch)
    for sends, receives, copy in halos:
        pl.when(sends)(copy.wait_send)
    own_copy.wait()
    everyone = recv_ref.at[pl.ds(0, devices - 1), used]
    pltpu.make_async_copy(everyone, everyone, wall_send).wait()
    pltpu.make_async_copy(everyone, everyone, wall_recv).wait()


def near_and_exchange(devices, counts_t, fluid_state, wall_blocks, readers_t, targets_t):
    walls = wall_blocks.shape[0]
    vmem = pl.BlockSpec(memory_space=pltpu.VMEM)
    anywhere = pl.BlockSpec(memory_space=pl.ANY)
    hbm = pl.BlockSpec(memory_space=pltpu.HBM)
    return pl.pallas_call(
        lambda *refs: exchange_kernel(devices, *refs),
        out_shape=(
            jax.ShapeDtypeStruct((CA, PAIRS, 8, 128), F32),
            jax.ShapeDtypeStruct((CA, PAIRS, 16, 128), F32),
            jax.ShapeDtypeStruct((CA * CB, 2, 64, 128), BF16),
            jax.ShapeDtypeStruct((devices, 40, 128), F32),
        ),
        in_specs=[pl.BlockSpec(memory_space=pltpu.SMEM)] + [hbm] * 4,
        out_specs=[vmem, vmem, vmem, anywhere],
        scratch_shapes=[
            pltpu.VMEM(fluid_state.shape, F32),
            pltpu.VMEM(wall_blocks.shape, F32),
            pltpu.VMEM(readers_t.shape, jnp.int32),
            pltpu.VMEM(targets_t.shape, jnp.int32),
            pltpu.VMEM((devices, 40, 128), F32),
            pltpu.VMEM((devices * SLOTS // 2, 2 * walls), BF16),
            pltpu.VMEM((2 * walls, 384), BF16),
            pltpu.VMEM((18, 6, 16, 128), F32),
            pltpu.VMEM((18, 6, 3, 64, 128), BF16),
            pltpu.VMEM((18, 6, 128, 128), BF16),
            pltpu.VMEM((18, PAIRS, 64, 128), BF16),
            pltpu.VMEM((18, 6, 8, 128), F32),
        ]
        + [
            pltpu.VMEM((576, 256), F32),
            pltpu.VMEM((3, 2, 256, 128), BF16),
            pltpu.VMEM((3, 2, 128, 128), BF16),
        ]
        * 2
        + [
            pltpu.SemaphoreType.DMA((4,)),
            pltpu.SemaphoreType.DMA,
            pltpu.SemaphoreType.DMA,
            pltpu.SemaphoreType.DMA,
            pltpu.SemaphoreType.DMA((8,)),
            pltpu.SemaphoreType.DMA((8,)),
        ],
        compiler_params=pltpu.CompilerParams(
            vmem_limit_bytes=26 << 20, collective_id=0, has_side_effects=True
        ),
        name="near_and_exchange",
    )(
        counts_t,
        *[
            pltpu.with_memory_space_constraint(array, pltpu.HBM)
            for array in (fluid_state, wall_blocks, readers_t, targets_t)
        ],
    )


UNROLL = 32


def wall_kernel(
    recv_ref,
    rec_ref,
    near_ref,
    side_ref,
    rates_ref,
    dens_ref,
    acc_ref,
    turn_ref,
    cells_ref,
    list_ref,
    sems,
):
    turn_ref[...] = recv_ref[:, 32, :].T[0:16].astype(jnp.int32)
    spread = pltpu.make_async_copy(turn_ref, cells_ref, sems.at[0])
    spread.start()
    spread.wait()
    lane1 = iota((1, 128), 1)
    left1 = lane1 < 64
    row8 = iota((8, 128), 0)
    left8 = iota((8, 128), 1) < 64
    zero8 = jnp.zeros((8, 128), F32)
    zero16 = jnp.zeros((16, 128), BF16)

    def listing(src, m):
        for q in range(SLOTS // 2):
            list_ref[m + q] = src * (SLOTS // 2) + q
        return m + (cells_ref[SLOTS, src] + 1) // 2

    def clear(a, m):
        for n in range(CB):
            acc_ref[0, a * CB + n] = zero8
            acc_ref[1, a * CB + n] = zero8
        for n in range(recv_ref.shape[0] // CA):
            m = listing(a * (recv_ref.shape[0] // CA) + n, m)
        return m

    live = lax.fori_loop(0, CA, clear, 0)
    for q in range(UNROLL):
        list_ref[live + q] = 0

    center = jnp.where(row8 == 2, 2.0, jnp.where(row8 < 2, 0.5, 0.0))

    def block(k, carry):
        ids, tiles, squares = [], [], []
        for u in range(UNROLL):
            at = k * UNROLL + u
            pair = list_ref[at]
            src = pair // (SLOTS // 2)
            q = pair - src * (SLOTS // 2)
            ids.append((cells_ref[2 * q, src], cells_ref[2 * q + 1, src]))
            tile = recv_ref[src, pl.ds(pl.multiple_of(q * 8, 8), 8), :]
            tiles.append(jnp.where(at < live, tile, 0.0))
        for u in range(0, UNROLL, 2):
            stacks = []
            for tile in tiles[u : u + 2]:
                c = tile - center
                sq = c * c
                norm = sq[0:1] + sq[1:2] + sq[2:3]
                rows = jnp.where(
                    row8 < 3, c, jnp.where(row8 == 3, norm, jnp.where(row8 == 4, 1.0, 0.0))
                )
                stacks += groups(*split3(rows), LEFT_ORDER) + [zero16]
            turned = jnp.concatenate(stacks, axis=0).T
            for side in range(2):
                right = jnp.concatenate(
                    [side_ref[ids[u][side], 0], side_ref[ids[u + 1][side], 1]], axis=0
                )
                squares.append(
                    jnp.dot(
                        turned[64 * side : 64 * side + 64], right, preferred_element_type=F32
                    )
                )
        weights = []
        for q2 in squares:
            q2 = jnp.maximum(q2, 1e-20)
            t = q2 * lax.rsqrt(q2)
            shell = jnp.maximum(1.0 - t, 0.0)
            shell = shell * shell
            weights.append(jnp.concatenate(split2(shell * shell * (4.0 * t + 1.0)), axis=0))
        outs = []
        for u in range(0, UNROLL, 2):
            rolled = [pltpu.roll(tile, 64, 1) for tile in tiles[u : u + 2]]
            for side in range(2):
                lines = []
                for tile, turn in zip(tiles[u : u + 2], rolled):
                    twice = jnp.where(left8, turn, tile) if side else jnp.where(left8, tile, turn)
                    high = twice.astype(BF16).astype(F32)
                    lines.append(jnp.concatenate([high, twice - high], axis=0).astype(BF16))
                outs.append(
                    jnp.dot(
                        jnp.concatenate(lines, axis=0),
                        weights[u + side],
                        preferred_element_type=F32,
                    )
                )
        for u in range(0, UNROLL, 2):
            for side in range(2):
                got = outs[u + side]
                for n in range(2):
                    cell = ids[u + n][side]
                    acc_ref[n, cell] = acc_ref[n, cell] + (
                        got[16 * n : 16 * n + 8] + got[16 * n + 8 : 16 * n + 16]
                    )
        return carry

    lax.fori_loop(0, (live + UNROLL - 1) // UNROLL, block, 0)

    def finish(a, carry):
        for p in range(PAIRS):
            one, two = a * CB + 2 * p, a * CB + 2 * p + 1
            total = jnp.where(
                left8,
                acc_ref[0, one] + pltpu.roll(acc_ref[1, one], 64, 1),
                pltpu.roll(acc_ref[0, two], 64, 1) + acc_ref[1, two],
            )
            tile = rec_ref[a, p]
            near = near_ref[a, p]
            h, sound = tile[10:11], tile[12:13]
            scale = KERN_W / (h * h * h)
            push = WALL_PUSH * sound * sound * scale
            heat = WALL_HEAT * scale * (total[7:8] - tile[11:12] * total[6:7])
            r = [near[1 + n : 2 + n] + push * total[3 + n : 4 + n] for n in range(3)]
            r.append(near[4:5] + heat)
            t = [pltpu.roll(line, 64, 1) for line in r]
            for v in range(2):
                lo, hi = 2 * v, 2 * v + 1
                span = slice(v * 128, (v + 1) * 128)
                rates_ref[a, 2 * p : 2 * p + 1, span] = jnp.where(left1, r[lo], t[hi])
                rates_ref[a, 2 * p + 1 : 2 * p + 2, span] = jnp.where(left1, t[lo], r[hi])
            dens_ref[a, p : p + 1, :] = near[0:1]
        return carry

    lax.fori_loop(0, CA, finish, 0)


def wall_terms(recv, records, near, sides):
    return pl.pallas_call(
        wall_kernel,
        out_shape=(
            jax.ShapeDtypeStruct((CA, CB, 256), F32),
            jax.ShapeDtypeStruct((CA, PAIRS, 128), F32),
        ),
        in_specs=[pl.BlockSpec(memory_space=pltpu.VMEM)] * 4,
        out_specs=[pl.BlockSpec(memory_space=pltpu.VMEM)] * 2,
        scratch_shapes=[
            pltpu.VMEM((2, CA * CB, 8, 128), F32),
            pltpu.VMEM((16, recv.shape[0]), jnp.int32),
            pltpu.SMEM((16, recv.shape[0]), jnp.int32),
            pltpu.SMEM((recv.shape[0] * SLOTS // 2 + UNROLL + 8,), jnp.int32),
            pltpu.SemaphoreType.DMA((1,)),
        ],
        compiler_params=pltpu.CompilerParams(vmem_limit_bytes=10 << 20),
        name="wall_terms",
    )(recv, records, near, sides)


def local(fluid_state, cell_counts, wall_blocks, readers, targets):
    devices = lax.axis_size("gx") * lax.axis_size("gy")
    near, records, sides, recv = near_and_exchange(
        devices, cell_counts.T, fluid_state, wall_blocks, readers.T, targets.T
    )
    rates, density = wall_terms(recv, records, near, sides)
    return (rates, density.reshape(CA, CB * 64))


def solution(mesh):
    placed = (
        P("gx", "gy", None),
        P("gx", "gy"),
        P(("gx", "gy"), None),
        P(("gx", "gy"), None),
        P(("gx", "gy"), None),
    )
    return jax.shard_map(
        local,
        mesh=mesh,
        in_specs=placed,
        out_specs=(P("gx", "gy", None), P("gx", "gy")),
        check_vma=False,
    )
```

```python
import math

import jax
import jax.numpy as jnp
from jax import lax
from jax.experimental import pallas as pl
from jax.experimental.pallas import tpu as pltpu
from jax.sharding import PartitionSpec as P

CA = 16
CB = 8
PAIRS = 4
SLOTS = 8
SENDS = 1
STEP_SENDS = 2
KERN_W = 21.0 / (16.0 * math.pi)
KERN_F = 105.0 / (16.0 * math.pi)
KAPPA = 0.02
WALL_PUSH = 0.03
WALL_HEAT = 0.02
EPS_R = 0.01
F32 = jnp.float32
BF16 = jnp.bfloat16


def iota(shape, axis):
    return lax.broadcasted_iota(jnp.int32, shape, axis)


def split2(value):
    high = value.astype(BF16)
    low = (value - high.astype(F32)).astype(BF16)
    return high, low


def split3(value):
    high = value.astype(BF16).astype(F32)
    rest = value - high
    middle = rest.astype(BF16).astype(F32)
    return high, middle, rest - middle


def pack_records(counts_ref, fluid_ref, out_ref, greet):
    lane = iota((8, 128), 1)
    left = lane < 64
    slot = lane - jnp.where(left, 0, 64)

    def row(a, carry):
        comps = []
        for v in range(6):
            x = fluid_ref[a, :, v * 128 : (v + 1) * 128]
            turned = pltpu.roll(x, 64, 1)
            comps.append(jnp.where(left, x, pltpu.roll(turned, 7, 0)))
            comps.append(jnp.where(left, turned, pltpu.roll(x, 7, 0)))
        density, smooth, sound = comps[7], comps[8], comps[9]
        inverse = 1.0 / density
        d2 = density * density
        d4 = d2 * d2
        pressure = sound * sound / 7.0 * (d4 * d2 * density - 1.0)
        fields = comps[:6] + [
            comps[6],
            pressure * inverse * inverse,
            comps[10] * inverse,
            inverse,
            smooth,
            comps[11],
            sound,
        ]
        for p in range(PAIRS):
            count = jnp.where(left[:1], counts_ref[2 * p, a], counts_ref[2 * p + 1, a])
            for c, field in enumerate(fields):
                line = field[2 * p : 2 * p + 1]
                if c == 6:
                    line = jnp.where(slot[:1] < count, line, 0.0)
                out_ref[a, p, c : c + 1, :] = line
            out_ref[a, p, 13:16, :] = jnp.zeros((3, 128), F32)
        for n in range(SLOTS):
            greet(a * SLOTS + n + 1)
        return carry

    lax.fori_loop(0, CA, row, 0)


def route_walls(devices, wall_ref, readers_ref, targets_ref, out_ref, sel_ref, rhs_ref):
    rows = wall_ref.shape[0]
    lane = iota((rows, 128), 1)
    left = lane < 64
    later = (iota((rows, rows), 0) < iota((rows, rows), 1)).astype(BF16)
    device = iota((devices, rows), 0)
    before = jnp.zeros((devices, 1), F32)
    slots = []
    cells = jnp.zeros((devices, 128), F32)
    slot_row = iota((128, rows), 0).astype(F32)
    for r in range(2):
        reader = readers_ref[r : r + 1, :]
        hot = (device == reader).astype(F32)
        earlier = jnp.dot(hot.astype(BF16), later, preferred_element_type=F32) + before
        position = jnp.sum(hot * earlier, axis=0, keepdims=True)
        before = before + jnp.sum(hot, axis=1, keepdims=True)
        slots.append(reader * SLOTS + position.astype(jnp.int32))
        named = jnp.where(slot_row == position, targets_ref[r : r + 1, :].astype(F32), 0.0)
        named = jnp.where(slot_row == SLOTS, 1.0, named)
        cells = cells + lax.dot_general(
            hot.astype(BF16),
            named.astype(BF16),
            (((1,), (1,)), ((), ())),
            preferred_element_type=F32,
        )
    chunk = devices * SLOTS // 2
    pair = iota((chunk, rows), 0) * 2
    for half in range(2):
        chosen = (pair + half == slots[0]) | (pair + half == slots[1])
        sel_ref[:, half * rows : (half + 1) * rows] = jnp.where(chosen, 1.0, 0.0).astype(BF16)
    gamma = wall_ref[:, 384:512]
    gamma = jnp.where(left, gamma, pltpu.roll(gamma, 64, 1))
    for v in range(4):
        x = wall_ref[:, v * 128 : (v + 1) * 128]
        if v == 1:
            x = jnp.where(left, x, x * gamma)
        elif v == 2:
            x = x * gamma
        elif v == 3:
            x = jnp.where(left, x, x * gamma)
        turned = pltpu.roll(x, 64, 1)
        for odd in range(2):
            even_half = jnp.where(left, turned if odd else x, 0.0)
            odd_half = jnp.where(left, 0.0, x if odd else turned)
            for part, (e, o) in enumerate(zip(split3(even_half), split3(odd_half))):
                rhs_ref[0:rows, part * 128 : (part + 1) * 128] = e.astype(BF16)
                rhs_ref[rows : 2 * rows, part * 128 : (part + 1) * 128] = o.astype(BF16)
            got = jnp.dot(sel_ref[...], rhs_ref[...], preferred_element_type=F32)
            got = got[:, 0:128] + got[:, 128:256] + got[:, 256:384]
            got = got.reshape(devices, SLOTS // 2, 128)
            for q in range(SLOTS // 2):
                out_ref[:, q * 8 + 2 * v + odd, :] = got[:, q, :]
    out_ref[:, 32, :] = cells


def stack_rows(row8, rows):
    out = jnp.broadcast_to(rows[0], row8.shape)
    for n in range(1, len(rows)):
        out = jnp.where(row8 == n, rows[n], out)
    return out


def groups(high, middle, low, order):
    parts = {"h": high, "m": middle, "l": low}
    return [
        jnp.concatenate([parts[pair[0]], parts[pair[1]]], axis=0).astype(BF16) for pair in order
    ]


LEFT_ORDER = ("hh", "mh", "ml")
RIGHT_ORDER = ("hm", "hl", "mh")


def near_compute(
    post, settle, ext_ref, out_ref, side_out, mean_ref, feat_ref, turn_ref, side_ref, geo_ref, sd0, mid0, mix0, sd1, mid1, mix1
):
    left1 = iota((1, 128), 1) < 64
    left8 = iota((8, 128), 1) < 64
    left16 = iota((16, 128), 1) < 64
    row8 = iota((8, 128), 0)
    zero8 = jnp.zeros((8, 128), F32)
    zero16 = jnp.zeros((16, 128), BF16)
    own = jnp.where(left1, -1.0, 0.0)
    for n, c in enumerate((3, 4, 5, 11)):
        mean_ref[n : n + 1, :] = jnp.broadcast_to(
            jnp.mean(ext_ref[CA // 2, 2, c : c + 1, :], axis=1, keepdims=True), (1, 128)
        )
    mean = {c: mean_ref.at[n : n + 1, :] for n, c in enumerate((3, 4, 5, 11))}

    def prepare(a, p):
        row = lambda c: ext_ref[a, p, c : c + 1, :]
        level = lambda c: row(c) - mean[c][...]
        x = row(0) - 0.5
        y = row(1) + own
        z = row(2) - 2.0
        u, v, w, mass = level(3), level(4), level(5), row(6) * (-32.0 * KERN_F)
        pres, visc, inv, h, heat = row(7), row(8), row(9), row(10), level(11)
        one = jnp.ones_like(x)
        head = [one, pres, u, one, pres, v]
        v0 = mass * stack_rows(row8, head + [w, z])
        place = jnp.where(row8 < 3, x, jnp.where(row8 < 6, y, z))
        v1 = mass * stack_rows(row8, head + [pres, w]) * place
        v2 = mass * jnp.where(row8 < 5, inv, visc)
        v2 = v2 * stack_rows(row8, [one, u, v, w, heat, one, u, v])
        v3 = jnp.where(row8 == 0, mass * visc * w, 0.0)
        fa = jnp.concatenate([v0, v1], axis=0)
        fb = jnp.concatenate([v2, v3], axis=0)
        turned = [pltpu.roll(t, 64, 1) for t in (v0, v1, v2, v3)]
        ta = jnp.concatenate(turned[:2], axis=0)
        tb = jnp.concatenate(turned[2:], axis=0)
        for variant in ((2,) if p == 0 else (1,) if p == 5 else (0, 1, 2)):
            if variant == 0:
                va, vb = fa, fb
            elif variant == 1:
                va, vb = jnp.where(left16, fa, ta), jnp.where(left16, fb, tb)
            else:
                va, vb = jnp.where(left16, ta, fa), jnp.where(left16, tb, fb)
            ha, la = split2(va)
            hb, lb = split2(vb)
            feat_ref[a, p, variant, 0:16, :] = ha
            feat_ref[a, p, variant, 16:32, :] = la
            feat_ref[a, p, variant, 32:48, :] = hb
            feat_ref[a, p, variant, 48:64, :] = lb
        norm = x * x + y * y + z * z
        tile = stack_rows(row8, [x, y, z, one, norm, h, one, jnp.zeros_like(x)])
        geo_ref[a, p] = stack_rows(row8, [x, y, z, norm, h, jnp.zeros_like(x)])
        half = jnp.concatenate(groups(*split3(tile), LEFT_ORDER) + [zero16], axis=0)
        turn_ref[a, p] = jnp.concatenate([half, half], axis=0).T

    def prepare_row(a, carry):
        for p in range(PAIRS):
            prepare(a + 1, p + 1)
        for n in range(SENDS):
            post(a * SENDS + n + 1)
        return carry

    lax.fori_loop(0, CA, prepare_row, 0)
    settle()

    def prepare_columns(a, carry):
        for p in (0, PAIRS + 1):
            prepare(a + 1, p)
        return carry

    lax.fori_loop(0, CA, prepare_columns, 0)
    for p in range(PAIRS + 2):
        prepare(0, p)
        prepare(CA + 1, p)

    def sides(a, carry):
        for p in range(PAIRS):
            keep = iota((64, 128), 1) < 64
            side_ref[a, p] = jnp.where(
                keep,
                turn_ref[a, p, 64:128, :].astype(F32),
                turn_ref[a, p + 2, 0:64, :].astype(F32),
            ).astype(BF16)
        return carry

    lax.fori_loop(0, 18, sides, 0)

    row16 = iota((16, 128), 0)
    lane16 = iota((16, 128), 1)

    def scalars(s, wide, diagonal):
        s = jnp.maximum(s, 1e-20)
        w2 = wide * wide
        e = s + (0.25 * EPS_R) * w2
        w4 = w2 * w2
        den = w4 * w4 * e
        shell = jnp.maximum(wide - s * lax.rsqrt(s), 0.0)
        base = shell * shell * shell / den
        plain = base * e
        if diagonal is not None:
            plain = jnp.where(diagonal, 0.0, plain)
        return split2(plain), split2(base * s)

    y_shift = jnp.where(left1, -2.0, 2.0)
    geo_mask = jnp.where(row8 < 3, -2.0, 0.0)
    halves = lambda parts: (
        groups(*[jnp.where(left8, t, 0.0) for t in parts], RIGHT_ORDER)
        + [zero16]
        + groups(*[jnp.where(left8, 0.0, t) for t in parts], RIGHT_ORDER)
        + [zero16]
    )

    def distances(k, sd_ref):
        a = k // PAIRS
        p = k - a * PAIRS
        geo = lambda c: geo_ref[a + 1, p + 1, c : c + 1, :]
        x, y, norm, h = geo(0), geo(1), geo(3), geo(4)
        flat = geo_ref[a + 1, p + 1] * geo_mask
        wide_parts = split3(jnp.where(row8 == 5, 1.0, jnp.where(row8 == 6, h, 0.0)))
        wide_mid = jnp.concatenate(groups(*wide_parts, RIGHT_ORDER) + [zero16], axis=0)
        wide_mix = jnp.concatenate(halves(wide_parts), axis=0)
        for sx in (-1, 0, 1):
            r = a + 1 + sx
            at = (sx + 1) * 192
            n = norm - (2.0 * sx) * x + float(sx * sx) if sx else norm
            base = flat + jnp.where(row8 == 0, 2.0 * sx, jnp.where(row8 == 4, 1.0, 0.0))
            tile = jnp.where(row8 == 3, n, base)
            right = jnp.concatenate(groups(*split3(tile), RIGHT_ORDER) + [zero16], axis=0)
            sd_ref[at : at + 128, :] = jnp.dot(
                turn_ref[r, p + 1][:, 0:64],
                jnp.concatenate([right, wide_mid], axis=1),
                preferred_element_type=F32,
            )
            nm = n - 2.0 * y_shift * y + 4.0
            tile = jnp.where(row8 == 3, nm, base + jnp.where(row8 == 1, 2.0 * y_shift, 0.0))
            right = jnp.concatenate(halves(split3(tile)), axis=0)
            sd_ref[at + 128 : at + 192, :] = jnp.dot(
                side_ref[r, p],
                jnp.concatenate([right, wide_mix], axis=1),
                preferred_element_type=F32,
            )

    def weigh(sd_ref, mid_ref, mix_ref):
        for t in range(3):
            for c in range(12):
                at = t * 192 + c * 16
                diagonal = (row16 + c * 16 == lane16) if t == 1 and c < 8 else None
                (ah, al), (bh, bl) = scalars(
                    sd_ref[at : at + 16, 0:128], sd_ref[at : at + 16, 128:256], diagonal
                )
                if c < 8:
                    lo, step, ref = c * 16, 128, mid_ref
                else:
                    lo, step, ref = (c - 8) * 16, 64, mix_ref
                ref[t, 0, lo : lo + 16, :] = ah
                ref[t, 0, step + lo : step + lo + 16, :] = al
                ref[t, 1, lo : lo + 16, :] = bh
                ref[t, 1, step + lo : step + lo + 16, :] = bl

    def gather(k, mid_ref, mix_ref):
        a = k // PAIRS
        p = k - a * PAIRS
        sums = [zero8 for _ in range(4)]
        for sx in (-1, 0, 1):
            r = a + 1 + sx
            mid = feat_ref[r, p + 1, 0]
            fa = jnp.concatenate([mid[0:32], mid[0:32]], axis=1)
            fb = jnp.concatenate([mid[32:64], mid[32:64]], axis=1)
            ga = jnp.dot(fa, mid_ref[sx + 1, 0], preferred_element_type=F32)
            gb = jnp.dot(fb, mid_ref[sx + 1, 1], preferred_element_type=F32)
            side_l = feat_ref[r, p, 2]
            side_r = feat_ref[r, p + 2, 1]
            xa = jnp.dot(
                jnp.concatenate([side_l[0:32], side_r[0:32]], axis=0),
                mix_ref[sx + 1, 0],
                preferred_element_type=F32,
            )
            xb = jnp.dot(
                jnp.concatenate([side_l[32:64], side_r[32:64]], axis=0),
                mix_ref[sx + 1, 1],
                preferred_element_type=F32,
            )
            ga = ga[0:16] + ga[16:32]
            gb = gb[0:16] + gb[16:32]
            xa = jnp.where(left16, xa[0:16] + xa[16:32], xa[32:48] + xa[48:64])
            xb = jnp.where(left16, xb[0:16] + xb[16:32], xb[32:48] + xb[48:64])
            by_x = jnp.where(row8 < 3, float(sx), 0.0)
            by_y = jnp.where((row8 >= 3) & (row8 < 6), y_shift, 0.0)
            sums[0] = sums[0] + (ga[0:8] + xa[0:8])
            sums[1] = sums[1] + (ga[8:16] + xa[8:16] + by_y * xa[0:8])
            if sx:
                sums[1] = sums[1] + by_x * (ga[0:8] + xa[0:8])
            sums[2] = sums[2] + (gb[0:8] + xb[0:8])
            sums[3] = sums[3] + (gb[8:16] + xb[8:16])
        v0, v1, v2, v3 = sums
        geo = lambda c: geo_ref[a + 1, p + 1, c : c + 1, :]
        x, y, z = geo(0), geo(1), geo(2)
        row = lambda c: ext_ref[a + 1, p + 1, c : c + 1, :]
        u, v, w = [row(c) - mean[c][...] for c in (3, 4, 5)]
        sm, smp = v0[0:1], v0[1:2]
        gx = x * sm - v1[0:1]
        gy = y * sm - v1[3:4]
        gz = z * sm - v0[7:8]
        density = (
            u * gx
            - (x * v0[2:3] - v1[2:3])
            + v * gy
            - (y * v0[5:6] - v1[5:6])
            + w * gz
            - (z * v0[6:7] - v1[7:8])
        )
        pi, visc, inv = row(7), row(8), row(9)
        smi, smv = v2[0:1], v2[5:6]
        ax = visc * (u * smi - v2[1:2]) + inv * (u * smv - v2[6:7])
        ay = visc * (v * smi - v2[2:3]) + inv * (v * smv - v2[7:8])
        az = visc * (w * smi - v2[3:4]) + inv * (w * smv - v3[0:1])
        ax = ax - (pi * gx + (x * smp - v1[1:2]))
        ay = ay - (pi * gy + (y * smp - v1[4:5]))
        az = az - (pi * gz + (z * smp - v1[6:7]))
        heat = (2.0 * KAPPA) * inv * ((row(11) - mean[11][...]) * smi - v2[4:5])
        for n, line in enumerate((density, ax, ay, az, heat)):
            out_ref[a, p, n : n + 1, :] = line

    def wall_side(k):
        a = k // PAIRS
        p = k - a * PAIRS
        row = lambda c: ext_ref[a + 1, p + 1, c : c + 1, :]
        x = row(0) - 0.5
        y = row(1) - 0.5
        z = row(2) - 2.0
        h = row(10)
        s = 0.25 / (h * h)
        norm = x * x + y * y + z * z
        rows = s * stack_rows(
            row8, [-2.0 * x, -2.0 * y, -2.0 * z, jnp.ones_like(x), norm, jnp.zeros_like(x)]
        )
        here, there = split3(rows), split3(pltpu.roll(rows, 64, 1))
        for n, side, parts in ((0, 0, here), (0, 1, there), (1, 0, there), (1, 1, here)):
            kept = [jnp.where(left8, 0.0, t) if side else jnp.where(left8, t, 0.0) for t in parts]
            side_out[2 * k + n, side] = jnp.concatenate(
                groups(*kept, RIGHT_ORDER) + [zero16], axis=0
            )

    last = CA * PAIRS - 1
    slots = ((sd0, mid0, mix0), (sd1, mid1, mix1))
    for _, mid_ref, mix_ref in slots:
        mid_ref[...] = jnp.zeros(mid_ref.shape, BF16)
        mix_ref[...] = jnp.zeros(mix_ref.shape, BF16)
    distances(0, sd0)

    def step(m, carry):
        for odd in range(2):
            k = 2 * m + odd
            sd_ref, mid_ref, mix_ref = slots[odd]
            sd_next, mid_last, mix_last = slots[1 - odd]
            post(CA * SENDS + k * STEP_SENDS + 1)
            gather(jnp.clip(k - 1, 0, last), mid_last, mix_last)
            distances(jnp.minimum(k + 1, last), sd_next)
            weigh(sd_ref, mid_ref, mix_ref)
            wall_side(jnp.minimum(k, last))
            post(CA * SENDS + k * STEP_SENDS + 2)
        return carry

    lax.fori_loop(0, CA * PAIRS // 2, step, 0)
    gather(last, mid1, mix1)


def exchange_kernel(
    devices,
    counts_hbm,
    fluid_hbm,
    wall_hbm,
    readers_hbm,
    targets_hbm,
    out_ref,
    rec_ref,
    side_out,
    recv_ref,
    counts_ref,
    fluid_ref,
    wall_ref,
    readers_ref,
    targets_ref,
    send_ref,
    sel_ref,
    rhs_ref,
    ext_ref,
    *rest,
):
    scratch, (load_sem, wall_send, wall_recv, own_sem, halo_send, halo_recv) = rest[:-6], rest[-6:]
    gx, gy = lax.axis_index("gx"), lax.axis_index("gy")
    nx, ny = lax.axis_size("gx"), lax.axis_size("gy")
    me = gx * ny + gy
    loads = [
        pltpu.make_async_copy(src, dst, load_sem.at[n])
        for n, (src, dst) in enumerate(
            [
                (readers_hbm, readers_ref),
                (targets_hbm, targets_ref),
                (wall_hbm, wall_ref),
                (fluid_hbm, fluid_ref),
                (counts_hbm, counts_ref),
            ]
        )
    ]
    for load in loads[::-1]:
        load.start()
    barrier = pltpu.get_barrier_semaphore()

    def greet(d):
        other = lax.rem(me + d, devices)

        @pl.when(d < devices)
        def _():
            pl.semaphore_signal(
                barrier,
                inc=1,
                device_id=(other // ny, lax.rem(other, ny)),
                device_id_type=pl.DeviceIdType.MESH,
            )

    blank = jnp.zeros((16, 128), F32)

    @pl.when(gx == 0)
    def _():
        for p in range(6):
            ext_ref[0, p] = blank

    @pl.when(gx == nx - 1)
    def _():
        for p in range(6):
            ext_ref[CA + 1, p] = blank

    @pl.when(gy == 0)
    def _():
        for a in range(CA + 2):
            ext_ref[a, 0] = blank

    @pl.when(gy == ny - 1)
    def _():
        for a in range(CA + 2):
            ext_ref[a, PAIRS + 1] = blank

    loads[3].wait()
    loads[4].wait()
    pack_records(counts_ref, fluid_ref, rec_ref, greet)
    for load in loads[:3]:
        load.wait()
    route_walls(devices, wall_ref, readers_ref, targets_ref, send_ref, sel_ref, rhs_ref)

    def keep(a, carry):
        for p in range(PAIRS):
            ext_ref[a + 1, p + 1] = rec_ref[a, p]
        return carry

    lax.fori_loop(0, CA, keep, 0)
    pl.semaphore_wait(barrier, devices - 1)

    rows = {-1: (0, CA + 1), 1: (CA - 1, 0)}
    cols = {-1: (0, PAIRS + 1), 1: (PAIRS - 1, 0)}
    halos = []
    for n, (dx, dy) in enumerate(
        [(0, 1), (0, -1), (1, 0), (-1, 0), (1, 1), (1, -1), (-1, 1), (-1, -1)]
    ):
        src_a, dst_a = rows[dx] if dx else (pl.ds(0, CA), pl.ds(1, CA))
        src_p, dst_p = cols[dy] if dy else (pl.ds(0, PAIRS), pl.ds(1, PAIRS))
        to_x, to_y = gx + dx, gy + dy
        sends = (to_x >= 0) & (to_x < nx) & (to_y >= 0) & (to_y < ny)
        from_x, from_y = gx - dx, gy - dy
        receives = (from_x >= 0) & (from_x < nx) & (from_y >= 0) & (from_y < ny)
        copy = pltpu.make_async_remote_copy(
            src_ref=rec_ref.at[src_a, src_p],
            dst_ref=ext_ref.at[dst_a, dst_p],
            send_sem=halo_send.at[n],
            recv_sem=halo_recv.at[n],
            device_id=(jnp.clip(to_x, 0, nx - 1), jnp.clip(to_y, 0, ny - 1)),
            device_id_type=pl.DeviceIdType.MESH,
        )
        halos.append((sends, receives, copy))
        pl.when(sends)(copy.start)

    used = pl.ds(0, 33)
    own_copy = pltpu.make_async_copy(send_ref.at[me, used], recv_ref.at[me, used], own_sem)
    own_copy.start()

    def post(d):
        other = lax.rem(me + d * 37, devices)

        @pl.when(d < devices)
        def _():
            pltpu.make_async_remote_copy(
                src_ref=send_ref.at[other, used],
                dst_ref=recv_ref.at[me, used],
                send_sem=wall_send,
                recv_sem=wall_recv,
                device_id=(other // ny, lax.rem(other, ny)),
                device_id_type=pl.DeviceIdType.MESH,
            ).start()

    def settle():
        for sends, receives, copy in halos:
            pl.when(receives)(copy.wait_recv)

    near_compute(post, settle, ext_ref, out_ref, side_out, *scratch)
    for sends, receives, copy in halos:
        pl.when(sends)(copy.wait_send)
    own_copy.wait()
    everyone = recv_ref.at[pl.ds(0, devices - 1), used]
    pltpu.make_async_copy(everyone, everyone, wall_send).wait()
    pltpu.make_async_copy(everyone, everyone, wall_recv).wait()


def near_and_exchange(devices, counts_t, fluid_state, wall_blocks, readers_t, targets_t):
    walls = wall_blocks.shape[0]
    vmem = pl.BlockSpec(memory_space=pltpu.VMEM)
    anywhere = pl.BlockSpec(memory_space=pl.ANY)
    hbm = pl.BlockSpec(memory_space=pltpu.HBM)
    return pl.pallas_call(
        lambda *refs: exchange_kernel(devices, *refs),
        out_shape=(
            jax.ShapeDtypeStruct((CA, PAIRS, 8, 128), F32),
            jax.ShapeDtypeStruct((CA, PAIRS, 16, 128), F32),
            jax.ShapeDtypeStruct((CA * CB, 2, 64, 128), BF16),
            jax.ShapeDtypeStruct((devices, 40, 128), F32),
        ),
        in_specs=[hbm] * 5,
        out_specs=[vmem, vmem, vmem, anywhere],
        scratch_shapes=[
            pltpu.SMEM(counts_t.shape, jnp.int32),
            pltpu.VMEM(fluid_state.shape, F32),
            pltpu.VMEM(wall_blocks.shape, F32),
            pltpu.VMEM(readers_t.shape, jnp.int32),
            pltpu.VMEM(targets_t.shape, jnp.int32),
            pltpu.VMEM((devices, 40, 128), F32),
            pltpu.VMEM((devices * SLOTS // 2, 2 * walls), BF16),
            pltpu.VMEM((2 * walls, 384), BF16),
            pltpu.VMEM((18, 6, 16, 128), F32),
            pltpu.VMEM((8, 128), F32),
            pltpu.VMEM((18, 6, 3, 64, 128), BF16),
            pltpu.VMEM((18, 6, 128, 128), BF16),
            pltpu.VMEM((18, PAIRS, 64, 128), BF16),
            pltpu.VMEM((18, 6, 8, 128), F32),
        ]
        + [
            pltpu.VMEM((576, 256), F32),
            pltpu.VMEM((3, 2, 256, 128), BF16),
            pltpu.VMEM((3, 2, 128, 128), BF16),
        ]
        * 2
        + [
            pltpu.SemaphoreType.DMA((5,)),
            pltpu.SemaphoreType.DMA,
            pltpu.SemaphoreType.DMA,
            pltpu.SemaphoreType.DMA,
            pltpu.SemaphoreType.DMA((8,)),
            pltpu.SemaphoreType.DMA((8,)),
        ],
        compiler_params=pltpu.CompilerParams(
            vmem_limit_bytes=26 << 20, collective_id=0, has_side_effects=True
        ),
        name="near_and_exchange",
    )(
        *[
            pltpu.with_memory_space_constraint(array, pltpu.HBM)
            for array in (counts_t, fluid_state, wall_blocks, readers_t, targets_t)
        ],
    )


UNROLL = 32


def wall_kernel(
    recv_ref,
    rec_ref,
    near_ref,
    side_ref,
    rates_ref,
    dens_ref,
    acc_ref,
    turn_ref,
    cells_ref,
    list_ref,
    sems,
):
    turn_ref[...] = recv_ref[:, 32, :].T[0:16].astype(jnp.int32)
    spread = pltpu.make_async_copy(turn_ref, cells_ref, sems.at[0])
    spread.start()
    spread.wait()
    lane1 = iota((1, 128), 1)
    left1 = lane1 < 64
    row8 = iota((8, 128), 0)
    left8 = iota((8, 128), 1) < 64
    zero8 = jnp.zeros((8, 128), F32)
    zero16 = jnp.zeros((16, 128), BF16)

    def listing(src, m):
        for q in range(SLOTS // 2):
            list_ref[m + q] = src * (SLOTS // 2) + q
        return m + (cells_ref[SLOTS, src] + 1) // 2

    def clear(a, m):
        for n in range(CB):
            acc_ref[0, a * CB + n] = zero8
            acc_ref[1, a * CB + n] = zero8
        for n in range(recv_ref.shape[0] // CA):
            m = listing(a * (recv_ref.shape[0] // CA) + n, m)
        return m

    live = lax.fori_loop(0, CA, clear, 0)
    for q in range(UNROLL):
        list_ref[live + q] = 0

    center = jnp.where(row8 == 2, 2.0, jnp.where(row8 < 2, 0.5, 0.0))

    def block(k, carry):
        ids, tiles, squares = [], [], []
        for u in range(UNROLL):
            at = k * UNROLL + u
            pair = list_ref[at]
            src = pair // (SLOTS // 2)
            q = pair - src * (SLOTS // 2)
            ids.append((cells_ref[2 * q, src], cells_ref[2 * q + 1, src]))
            tile = recv_ref[src, pl.ds(pl.multiple_of(q * 8, 8), 8), :]
            tiles.append(jnp.where(at < live, tile, 0.0))
        for u in range(0, UNROLL, 2):
            stacks = []
            for tile in tiles[u : u + 2]:
                c = tile - center
                sq = c * c
                norm = sq[0:1] + sq[1:2] + sq[2:3]
                rows = jnp.where(
                    row8 < 3, c, jnp.where(row8 == 3, norm, jnp.where(row8 == 4, 1.0, 0.0))
                )
                stacks += groups(*split3(rows), LEFT_ORDER) + [zero16]
            turned = jnp.concatenate(stacks, axis=0).T
            for side in range(2):
                right = jnp.concatenate(
                    [side_ref[ids[u][side], 0], side_ref[ids[u + 1][side], 1]], axis=0
                )
                squares.append(
                    jnp.dot(
                        turned[64 * side : 64 * side + 64], right, preferred_element_type=F32
                    )
                )
        weights = []
        for q2 in squares:
            q2 = jnp.maximum(q2, 1e-20)
            t = q2 * lax.rsqrt(q2)
            shell = jnp.maximum(1.0 - t, 0.0)
            shell = shell * shell
            weights.append(jnp.concatenate(split2(shell * shell * (4.0 * t + 1.0)), axis=0))
        outs = []
        for u in range(0, UNROLL, 2):
            rolled = [pltpu.roll(tile, 64, 1) for tile in tiles[u : u + 2]]
            for side in range(2):
                lines = []
                for tile, turn in zip(tiles[u : u + 2], rolled):
                    twice = jnp.where(left8, turn, tile) if side else jnp.where(left8, tile, turn)
                    high = twice.astype(BF16).astype(F32)
                    lines.append(jnp.concatenate([high, twice - high], axis=0).astype(BF16))
                outs.append(
                    jnp.dot(
                        jnp.concatenate(lines, axis=0),
                        weights[u + side],
                        preferred_element_type=F32,
                    )
                )
        for u in range(0, UNROLL, 2):
            for side in range(2):
                got = outs[u + side]
                for n in range(2):
                    cell = ids[u + n][side]
                    acc_ref[n, cell] = acc_ref[n, cell] + (
                        got[16 * n : 16 * n + 8] + got[16 * n + 8 : 16 * n + 16]
                    )
        return carry

    lax.fori_loop(0, (live + UNROLL - 1) // UNROLL, block, 0)

    def finish(a, carry):
        for p in range(PAIRS):
            one, two = a * CB + 2 * p, a * CB + 2 * p + 1
            total = jnp.where(
                left8,
                acc_ref[0, one] + pltpu.roll(acc_ref[1, one], 64, 1),
                pltpu.roll(acc_ref[0, two], 64, 1) + acc_ref[1, two],
            )
            tile = rec_ref[a, p]
            near = near_ref[a, p]
            h, sound = tile[10:11], tile[12:13]
            scale = KERN_W / (h * h * h)
            push = WALL_PUSH * sound * sound * scale
            heat = WALL_HEAT * scale * (total[7:8] - tile[11:12] * total[6:7])
            r = [near[1 + n : 2 + n] + push * total[3 + n : 4 + n] for n in range(3)]
            r.append(near[4:5] + heat)
            t = [pltpu.roll(line, 64, 1) for line in r]
            for v in range(2):
                lo, hi = 2 * v, 2 * v + 1
                span = slice(v * 128, (v + 1) * 128)
                rates_ref[a, 2 * p : 2 * p + 1, span] = jnp.where(left1, r[lo], t[hi])
                rates_ref[a, 2 * p + 1 : 2 * p + 2, span] = jnp.where(left1, t[lo], r[hi])
            dens_ref[a, p : p + 1, :] = near[0:1]
        return carry

    lax.fori_loop(0, CA, finish, 0)


def wall_terms(recv, records, near, sides):
    return pl.pallas_call(
        wall_kernel,
        out_shape=(
            jax.ShapeDtypeStruct((CA, CB, 256), F32),
            jax.ShapeDtypeStruct((CA, PAIRS, 128), F32),
        ),
        in_specs=[pl.BlockSpec(memory_space=pltpu.VMEM)] * 4,
        out_specs=[pl.BlockSpec(memory_space=pltpu.VMEM)] * 2,
        scratch_shapes=[
            pltpu.VMEM((2, CA * CB, 8, 128), F32),
            pltpu.VMEM((16, recv.shape[0]), jnp.int32),
            pltpu.SMEM((16, recv.shape[0]), jnp.int32),
            pltpu.SMEM((recv.shape[0] * SLOTS // 2 + UNROLL + 8,), jnp.int32),
            pltpu.SemaphoreType.DMA((1,)),
        ],
        compiler_params=pltpu.CompilerParams(vmem_limit_bytes=10 << 20),
        name="wall_terms",
    )(recv, records, near, sides)


def local(fluid_state, cell_counts, wall_blocks, readers, targets):
    devices = lax.axis_size("gx") * lax.axis_size("gy")
    near, records, sides, recv = near_and_exchange(
        devices, cell_counts.T, fluid_state, wall_blocks, readers.T, targets.T
    )
    rates, density = wall_terms(recv, records, near, sides)
    return (rates, density.reshape(CA, CB * 64))


def solution(mesh):
    placed = (
        P("gx", "gy", None),
        P("gx", "gy"),
        P(("gx", "gy"), None),
        P(("gx", "gy"), None),
        P(("gx", "gy"), None),
    )
    return jax.shard_map(
        local,
        mesh=mesh,
        in_specs=placed,
        out_specs=(P("gx", "gy", None), P("gx", "gy")),
        check_vma=False,
    )
```

```python
import math

import jax
import jax.numpy as jnp
from jax import lax
from jax.experimental import pallas as pl
from jax.experimental.pallas import tpu as pltpu
from jax.sharding import PartitionSpec as P

CA = 16
CB = 8
PAIRS = 4
SLOTS = 8
SENDS = 1
STEP_SENDS = 2
KERN_W = 21.0 / (16.0 * math.pi)
KERN_F = 105.0 / (16.0 * math.pi)
KAPPA = 0.02
WALL_PUSH = 0.03
WALL_HEAT = 0.02
EPS_R = 0.01
F32 = jnp.float32
BF16 = jnp.bfloat16


def iota(shape, axis):
    return lax.broadcasted_iota(jnp.int32, shape, axis)


def split2(value):
    high = value.astype(BF16)
    low = (value - high.astype(F32)).astype(BF16)
    return high, low


def split3(value):
    high = value.astype(BF16).astype(F32)
    rest = value - high
    middle = rest.astype(BF16).astype(F32)
    return high, middle, rest - middle


def pack_records(counts_ref, fluid_ref, out_ref, greet):
    lane = iota((8, 128), 1)
    left = lane < 64
    slot = lane - jnp.where(left, 0, 64)

    def row(a, carry):
        comps = []
        for v in range(6):
            x = fluid_ref[a, :, v * 128 : (v + 1) * 128]
            turned = pltpu.roll(x, 64, 1)
            comps.append(jnp.where(left, x, pltpu.roll(turned, 7, 0)))
            comps.append(jnp.where(left, turned, pltpu.roll(x, 7, 0)))
        density, smooth, sound = comps[7], comps[8], comps[9]
        inverse = 1.0 / density
        d2 = density * density
        d4 = d2 * d2
        pressure = sound * sound / 7.0 * (d4 * d2 * density - 1.0)
        fields = comps[:6] + [
            comps[6],
            pressure * inverse * inverse,
            comps[10] * inverse,
            inverse,
            smooth,
            comps[11],
            sound,
        ]
        for p in range(PAIRS):
            count = jnp.where(left[:1], counts_ref[2 * p, a], counts_ref[2 * p + 1, a])
            for c, field in enumerate(fields):
                line = field[2 * p : 2 * p + 1]
                if c == 6:
                    line = jnp.where(slot[:1] < count, line, 0.0)
                out_ref[a, p, c : c + 1, :] = line
            out_ref[a, p, 13:16, :] = jnp.zeros((3, 128), F32)
        for n in range(SLOTS):
            greet(a * SLOTS + n + 1)
        return carry

    lax.fori_loop(0, CA, row, 0)


def route_walls(devices, wall_ref, readers_ref, targets_ref, out_ref, sel_ref, rhs_ref):
    rows = wall_ref.shape[0]
    lane = iota((rows, 128), 1)
    left = lane < 64
    later = (iota((rows, rows), 0) < iota((rows, rows), 1)).astype(BF16)
    device = iota((devices, rows), 0)
    before = jnp.zeros((devices, 1), F32)
    slots = []
    cells = jnp.zeros((devices, 128), F32)
    slot_row = iota((128, rows), 0).astype(F32)
    for r in range(2):
        reader = readers_ref[r : r + 1, :]
        hot = (device == reader).astype(F32)
        earlier = jnp.dot(hot.astype(BF16), later, preferred_element_type=F32) + before
        position = jnp.sum(hot * earlier, axis=0, keepdims=True)
        before = before + jnp.sum(hot, axis=1, keepdims=True)
        slots.append(reader * SLOTS + position.astype(jnp.int32))
        named = jnp.where(slot_row == position, targets_ref[r : r + 1, :].astype(F32), 0.0)
        named = jnp.where(slot_row == SLOTS, 1.0, named)
        cells = cells + lax.dot_general(
            hot.astype(BF16),
            named.astype(BF16),
            (((1,), (1,)), ((), ())),
            preferred_element_type=F32,
        )
    chunk = devices * SLOTS // 2
    pair = iota((chunk, rows), 0) * 2
    for half in range(2):
        chosen = (pair + half == slots[0]) | (pair + half == slots[1])
        sel_ref[:, half * rows : (half + 1) * rows] = jnp.where(chosen, 1.0, 0.0).astype(BF16)
    gamma = wall_ref[:, 384:512]
    gamma = jnp.where(left, gamma, pltpu.roll(gamma, 64, 1))
    for v in range(4):
        x = wall_ref[:, v * 128 : (v + 1) * 128]
        if v == 1:
            x = jnp.where(left, x, x * gamma)
        elif v == 2:
            x = x * gamma
        elif v == 3:
            x = jnp.where(left, x, x * gamma)
        turned = pltpu.roll(x, 64, 1)
        for odd in range(2):
            even_half = jnp.where(left, turned if odd else x, 0.0)
            odd_half = jnp.where(left, 0.0, x if odd else turned)
            for part, (e, o) in enumerate(zip(split3(even_half), split3(odd_half))):
                rhs_ref[0:rows, part * 128 : (part + 1) * 128] = e.astype(BF16)
                rhs_ref[rows : 2 * rows, part * 128 : (part + 1) * 128] = o.astype(BF16)
            got = jnp.dot(sel_ref[...], rhs_ref[...], preferred_element_type=F32)
            got = got[:, 0:128] + got[:, 128:256] + got[:, 256:384]
            got = got.reshape(devices, SLOTS // 2, 128)
            for q in range(SLOTS // 2):
                out_ref[:, q * 8 + 2 * v + odd, :] = got[:, q, :]
    out_ref[:, 32, :] = cells


def stack_rows(row8, rows):
    out = jnp.broadcast_to(rows[0], row8.shape)
    for n in range(1, len(rows)):
        out = jnp.where(row8 == n, rows[n], out)
    return out


def groups(high, middle, low, order):
    parts = {"h": high, "m": middle, "l": low}
    return [
        jnp.concatenate([parts[pair[0]], parts[pair[1]]], axis=0).astype(BF16) for pair in order
    ]


LEFT_ORDER = ("hh", "mh", "ml")
RIGHT_ORDER = ("hm", "hl", "mh")


def near_compute(
    post, settle, ext_ref, out_ref, side_out, mean_ref, feat_ref, turn_ref, side_ref, geo_ref, sd0, mid0, mix0, sd1, mid1, mix1
):
    left1 = iota((1, 128), 1) < 64
    left8 = iota((8, 128), 1) < 64
    left16 = iota((16, 128), 1) < 64
    row8 = iota((8, 128), 0)
    zero8 = jnp.zeros((8, 128), F32)
    zero16 = jnp.zeros((16, 128), BF16)
    own = jnp.where(left1, -1.0, 0.0)
    for n, c in enumerate((3, 4, 5, 11)):
        mean_ref[n : n + 1, :] = jnp.broadcast_to(
            jnp.mean(ext_ref[CA // 2, 2, c : c + 1, :], axis=1, keepdims=True), (1, 128)
        )
    mean = {c: mean_ref.at[n : n + 1, :] for n, c in enumerate((3, 4, 5, 11))}

    def prepare(a, p):
        row = lambda c: ext_ref[a, p, c : c + 1, :]
        level = lambda c: row(c) - mean[c][...]
        x = row(0) - 0.5
        y = row(1) + own
        z = row(2) - 2.0
        u, v, w, mass = level(3), level(4), level(5), row(6) * (-32.0 * KERN_F)
        pres, visc, inv, h, heat = row(7), row(8), row(9), row(10), level(11)
        one = jnp.ones_like(x)
        head = [one, pres, u, one, pres, v]
        v0 = mass * stack_rows(row8, head + [w, z])
        place = jnp.where(row8 < 3, x, jnp.where(row8 < 6, y, z))
        v1 = mass * stack_rows(row8, head + [pres, w]) * place
        v2 = mass * jnp.where(row8 < 5, inv, visc)
        v2 = v2 * stack_rows(row8, [one, u, v, w, heat, one, u, v])
        v3 = jnp.where(row8 == 0, mass * visc * w, 0.0)
        fa = jnp.concatenate([v0, v1], axis=0)
        fb = jnp.concatenate([v2, v3], axis=0)
        turned = [pltpu.roll(t, 64, 1) for t in (v0, v1, v2, v3)]
        ta = jnp.concatenate(turned[:2], axis=0)
        tb = jnp.concatenate(turned[2:], axis=0)
        for variant in ((2,) if p == 0 else (1,) if p == 5 else (0, 1, 2)):
            if variant == 0:
                va, vb = fa, fb
            elif variant == 1:
                va, vb = jnp.where(left16, fa, ta), jnp.where(left16, fb, tb)
            else:
                va, vb = jnp.where(left16, ta, fa), jnp.where(left16, tb, fb)
            ha, la = split2(va)
            hb, lb = split2(vb)
            feat_ref[a, p, variant, 0:16, :] = ha
            feat_ref[a, p, variant, 16:32, :] = la
            feat_ref[a, p, variant, 32:48, :] = hb
            feat_ref[a, p, variant, 48:64, :] = lb
        norm = x * x + y * y + z * z
        tile = stack_rows(row8, [x, y, z, one, norm, h, one, jnp.zeros_like(x)])
        geo_ref[a, p] = stack_rows(row8, [x, y, z, norm, h, jnp.zeros_like(x)])
        half = jnp.concatenate(groups(*split3(tile), LEFT_ORDER) + [zero16], axis=0)
        turn_ref[a, p] = jnp.concatenate([half, half], axis=0).T

    def prepare_row(a, carry):
        for p in range(PAIRS):
            prepare(a + 1, p + 1)
        for n in range(SENDS):
            post(a * SENDS + n + 1)
        return carry

    lax.fori_loop(0, CA, prepare_row, 0)
    settle()

    def prepare_columns(a, carry):
        for p in (0, PAIRS + 1):
            prepare(a + 1, p)
        return carry

    lax.fori_loop(0, CA, prepare_columns, 0)
    for p in range(PAIRS + 2):
        prepare(0, p)
        prepare(CA + 1, p)

    def sides(a, carry):
        for p in range(PAIRS):
            keep = iota((64, 128), 1) < 64
            side_ref[a, p] = jnp.where(
                keep,
                turn_ref[a, p, 64:128, :].astype(F32),
                turn_ref[a, p + 2, 0:64, :].astype(F32),
            ).astype(BF16)
        return carry

    lax.fori_loop(0, 18, sides, 0)

    row16 = iota((16, 128), 0)
    lane16 = iota((16, 128), 1)

    def scalars(s, wide, diagonal):
        s = jnp.maximum(s, 1e-20)
        w2 = wide * wide
        e = s + (0.25 * EPS_R) * w2
        w4 = w2 * w2
        den = w4 * w4 * e
        shell = jnp.maximum(wide - s * lax.rsqrt(s), 0.0)
        base = shell * shell * shell / den
        plain = base * e
        if diagonal is not None:
            plain = jnp.where(diagonal, 0.0, plain)
        return split2(plain), split2(base * s)

    y_shift = jnp.where(left1, -2.0, 2.0)
    geo_mask = jnp.where(row8 < 3, -2.0, 0.0)
    halves = lambda parts: (
        groups(*[jnp.where(left8, t, 0.0) for t in parts], RIGHT_ORDER)
        + [zero16]
        + groups(*[jnp.where(left8, 0.0, t) for t in parts], RIGHT_ORDER)
        + [zero16]
    )

    def distances(k, sd_ref):
        a = k // PAIRS
        p = k - a * PAIRS
        geo = lambda c: geo_ref[a + 1, p + 1, c : c + 1, :]
        x, y, norm, h = geo(0), geo(1), geo(3), geo(4)
        flat = geo_ref[a + 1, p + 1] * geo_mask
        wide_parts = split3(jnp.where(row8 == 5, 1.0, jnp.where(row8 == 6, h, 0.0)))
        wide_mid = jnp.concatenate(groups(*wide_parts, RIGHT_ORDER) + [zero16], axis=0)
        wide_mix = jnp.concatenate(halves(wide_parts), axis=0)
        for sx in (-1, 0, 1):
            r = a + 1 + sx
            at = (sx + 1) * 192
            n = norm - (2.0 * sx) * x + float(sx * sx) if sx else norm
            base = flat + jnp.where(row8 == 0, 2.0 * sx, jnp.where(row8 == 4, 1.0, 0.0))
            tile = jnp.where(row8 == 3, n, base)
            right = jnp.concatenate(groups(*split3(tile), RIGHT_ORDER) + [zero16], axis=0)
            sd_ref[at : at + 128, :] = jnp.dot(
                turn_ref[r, p + 1][:, 0:64],
                jnp.concatenate([right, wide_mid], axis=1),
                preferred_element_type=F32,
            )
            nm = n - 2.0 * y_shift * y + 4.0
            tile = jnp.where(row8 == 3, nm, base + jnp.where(row8 == 1, 2.0 * y_shift, 0.0))
            right = jnp.concatenate(halves(split3(tile)), axis=0)
            sd_ref[at + 128 : at + 192, :] = jnp.dot(
                side_ref[r, p],
                jnp.concatenate([right, wide_mix], axis=1),
                preferred_element_type=F32,
            )

    def weigh(sd_ref, mid_ref, mix_ref):
        for t in range(3):
            for c in range(12):
                at = t * 192 + c * 16
                diagonal = (row16 + c * 16 == lane16) if t == 1 and c < 8 else None
                (ah, al), (bh, bl) = scalars(
                    sd_ref[at : at + 16, 0:128], sd_ref[at : at + 16, 128:256], diagonal
                )
                if c < 8:
                    lo, step, ref = c * 16, 128, mid_ref
                else:
                    lo, step, ref = (c - 8) * 16, 64, mix_ref
                ref[t, 0, lo : lo + 16, :] = ah
                ref[t, 0, step + lo : step + lo + 16, :] = al
                ref[t, 1, lo : lo + 16, :] = bh
                ref[t, 1, step + lo : step + lo + 16, :] = bl

    def gather(k, mid_ref, mix_ref):
        a = k // PAIRS
        p = k - a * PAIRS
        sums = [zero8 for _ in range(4)]
        for sx in (-1, 0, 1):
            r = a + 1 + sx
            mid = feat_ref[r, p + 1, 0]
            fa = jnp.concatenate([mid[0:32], mid[0:32]], axis=1)
            fb = jnp.concatenate([mid[32:64], mid[32:64]], axis=1)
            ga = jnp.dot(fa, mid_ref[sx + 1, 0], preferred_element_type=F32)
            gb = jnp.dot(fb, mid_ref[sx + 1, 1], preferred_element_type=F32)
            side_l = feat_ref[r, p, 2]
            side_r = feat_ref[r, p + 2, 1]
            xa = jnp.dot(
                jnp.concatenate([side_l[0:32], side_r[0:32]], axis=0),
                mix_ref[sx + 1, 0],
                preferred_element_type=F32,
            )
            xb = jnp.dot(
                jnp.concatenate([side_l[32:64], side_r[32:64]], axis=0),
                mix_ref[sx + 1, 1],
                preferred_element_type=F32,
            )
            ga = ga[0:16] + ga[16:32]
            gb = gb[0:16] + gb[16:32]
            xa = jnp.where(left16, xa[0:16] + xa[16:32], xa[32:48] + xa[48:64])
            xb = jnp.where(left16, xb[0:16] + xb[16:32], xb[32:48] + xb[48:64])
            by_x = jnp.where(row8 < 3, float(sx), 0.0)
            by_y = jnp.where((row8 >= 3) & (row8 < 6), y_shift, 0.0)
            sums[0] = sums[0] + (ga[0:8] + xa[0:8])
            sums[1] = sums[1] + (ga[8:16] + xa[8:16] + by_y * xa[0:8])
            if sx:
                sums[1] = sums[1] + by_x * (ga[0:8] + xa[0:8])
            sums[2] = sums[2] + (gb[0:8] + xb[0:8])
            sums[3] = sums[3] + (gb[8:16] + xb[8:16])
        v0, v1, v2, v3 = sums
        geo = lambda c: geo_ref[a + 1, p + 1, c : c + 1, :]
        x, y, z = geo(0), geo(1), geo(2)
        row = lambda c: ext_ref[a + 1, p + 1, c : c + 1, :]
        u, v, w = [row(c) - mean[c][...] for c in (3, 4, 5)]
        sm, smp = v0[0:1], v0[1:2]
        gx = x * sm - v1[0:1]
        gy = y * sm - v1[3:4]
        gz = z * sm - v0[7:8]
        density = (
            u * gx
            - (x * v0[2:3] - v1[2:3])
            + v * gy
            - (y * v0[5:6] - v1[5:6])
            + w * gz
            - (z * v0[6:7] - v1[7:8])
        )
        pi, visc, inv = row(7), row(8), row(9)
        smi, smv = v2[0:1], v2[5:6]
        ax = visc * (u * smi - v2[1:2]) + inv * (u * smv - v2[6:7])
        ay = visc * (v * smi - v2[2:3]) + inv * (v * smv - v2[7:8])
        az = visc * (w * smi - v2[3:4]) + inv * (w * smv - v3[0:1])
        ax = ax - (pi * gx + (x * smp - v1[1:2]))
        ay = ay - (pi * gy + (y * smp - v1[4:5]))
        az = az - (pi * gz + (z * smp - v1[6:7]))
        heat = (2.0 * KAPPA) * inv * ((row(11) - mean[11][...]) * smi - v2[4:5])
        for n, line in enumerate((density, ax, ay, az, heat)):
            out_ref[a, p, n : n + 1, :] = line

    def wall_side(k):
        a = k // PAIRS
        p = k - a * PAIRS
        row = lambda c: ext_ref[a + 1, p + 1, c : c + 1, :]
        x = row(0) - 0.5
        y = row(1) - 0.5
        z = row(2) - 2.0
        h = row(10)
        s = 0.25 / (h * h)
        norm = x * x + y * y + z * z
        rows = s * stack_rows(
            row8, [-2.0 * x, -2.0 * y, -2.0 * z, jnp.ones_like(x), norm, jnp.zeros_like(x)]
        )
        here, there = split3(rows), split3(pltpu.roll(rows, 64, 1))
        for n, side, parts in ((0, 0, here), (0, 1, there), (1, 0, there), (1, 1, here)):
            kept = [jnp.where(left8, 0.0, t) if side else jnp.where(left8, t, 0.0) for t in parts]
            side_out[2 * k + n, side] = jnp.concatenate(
                groups(*kept, RIGHT_ORDER) + [zero16], axis=0
            )

    last = CA * PAIRS - 1
    slots = ((sd0, mid0, mix0), (sd1, mid1, mix1))
    for _, mid_ref, mix_ref in slots:
        mid_ref[...] = jnp.zeros(mid_ref.shape, BF16)
        mix_ref[...] = jnp.zeros(mix_ref.shape, BF16)
    distances(0, sd0)

    def step(m, carry):
        for odd in range(2):
            k = 2 * m + odd
            sd_ref, mid_ref, mix_ref = slots[odd]
            sd_next, mid_last, mix_last = slots[1 - odd]
            post(CA * SENDS + k * STEP_SENDS + 1)
            gather(jnp.clip(k - 1, 0, last), mid_last, mix_last)
            distances(jnp.minimum(k + 1, last), sd_next)
            weigh(sd_ref, mid_ref, mix_ref)
            wall_side(jnp.minimum(k, last))
            post(CA * SENDS + k * STEP_SENDS + 2)
        return carry

    lax.fori_loop(0, CA * PAIRS // 2, step, 0)
    gather(last, mid1, mix1)


def exchange_kernel(
    devices,
    counts_hbm,
    fluid_hbm,
    wall_hbm,
    readers_hbm,
    targets_hbm,
    out_ref,
    rec_ref,
    side_out,
    recv_ref,
    counts_ref,
    fluid_ref,
    wall_ref,
    readers_ref,
    targets_ref,
    send_ref,
    sel_ref,
    rhs_ref,
    ext_ref,
    *rest,
):
    scratch, (load_sem, wall_send, wall_recv, own_sem, halo_send, halo_recv) = rest[:-6], rest[-6:]
    gx, gy = lax.axis_index("gx"), lax.axis_index("gy")
    nx, ny = lax.axis_size("gx"), lax.axis_size("gy")
    me = gx * ny + gy
    loads = [
        pltpu.make_async_copy(src, dst, load_sem.at[n])
        for n, (src, dst) in enumerate(
            [
                (readers_hbm, readers_ref),
                (targets_hbm, targets_ref),
                (wall_hbm, wall_ref),
                (fluid_hbm, fluid_ref),
                (counts_hbm, counts_ref),
            ]
        )
    ]
    for load in loads[::-1]:
        load.start()
    barrier = pltpu.get_barrier_semaphore()

    def greet(d):
        other = lax.rem(me + d, devices)

        @pl.when(d < devices)
        def _():
            pl.semaphore_signal(
                barrier,
                inc=1,
                device_id=(other // ny, lax.rem(other, ny)),
                device_id_type=pl.DeviceIdType.MESH,
            )

    blank = jnp.zeros((16, 128), F32)

    @pl.when(gx == 0)
    def _():
        for p in range(6):
            ext_ref[0, p] = blank

    @pl.when(gx == nx - 1)
    def _():
        for p in range(6):
            ext_ref[CA + 1, p] = blank

    @pl.when(gy == 0)
    def _():
        for a in range(CA + 2):
            ext_ref[a, 0] = blank

    @pl.when(gy == ny - 1)
    def _():
        for a in range(CA + 2):
            ext_ref[a, PAIRS + 1] = blank

    loads[3].wait()
    loads[4].wait()
    pack_records(counts_ref, fluid_ref, rec_ref, greet)
    for load in loads[:3]:
        load.wait()
    route_walls(devices, wall_ref, readers_ref, targets_ref, send_ref, sel_ref, rhs_ref)

    def keep(a, carry):
        for p in range(PAIRS):
            ext_ref[a + 1, p + 1] = rec_ref[a, p]
        return carry

    lax.fori_loop(0, CA, keep, 0)
    pl.semaphore_wait(barrier, devices - 1)

    rows = {-1: (0, CA + 1), 1: (CA - 1, 0)}
    cols = {-1: (0, PAIRS + 1), 1: (PAIRS - 1, 0)}
    halos = []
    for n, (dx, dy) in enumerate(
        [(0, 1), (0, -1), (1, 0), (-1, 0), (1, 1), (1, -1), (-1, 1), (-1, -1)]
    ):
        src_a, dst_a = rows[dx] if dx else (pl.ds(0, CA), pl.ds(1, CA))
        src_p, dst_p = cols[dy] if dy else (pl.ds(0, PAIRS), pl.ds(1, PAIRS))
        to_x, to_y = gx + dx, gy + dy
        sends = (to_x >= 0) & (to_x < nx) & (to_y >= 0) & (to_y < ny)
        from_x, from_y = gx - dx, gy - dy
        receives = (from_x >= 0) & (from_x < nx) & (from_y >= 0) & (from_y < ny)
        copy = pltpu.make_async_remote_copy(
            src_ref=rec_ref.at[src_a, src_p],
            dst_ref=ext_ref.at[dst_a, dst_p],
            send_sem=halo_send.at[n],
            recv_sem=halo_recv.at[n],
            device_id=(jnp.clip(to_x, 0, nx - 1), jnp.clip(to_y, 0, ny - 1)),
            device_id_type=pl.DeviceIdType.MESH,
        )
        halos.append((sends, receives, copy))
        pl.when(sends)(copy.start)

    used = pl.ds(0, 33)
    own_copy = pltpu.make_async_copy(send_ref.at[me, used], recv_ref.at[me, used], own_sem)
    own_copy.start()

    def post(d):
        other = lax.rem(me + d * 37, devices)

        @pl.when(d < devices)
        def _():
            pltpu.make_async_remote_copy(
                src_ref=send_ref.at[other, used],
                dst_ref=recv_ref.at[me, used],
                send_sem=wall_send,
                recv_sem=wall_recv,
                device_id=(other // ny, lax.rem(other, ny)),
                device_id_type=pl.DeviceIdType.MESH,
            ).start()

    def settle():
        for sends, receives, copy in halos:
            pl.when(receives)(copy.wait_recv)

    near_compute(post, settle, ext_ref, out_ref, side_out, *scratch)
    for sends, receives, copy in halos:
        pl.when(sends)(copy.wait_send)
    own_copy.wait()
    everyone = recv_ref.at[pl.ds(0, devices - 1), used]
    pltpu.make_async_copy(everyone, everyone, wall_send).wait()
    pltpu.make_async_copy(everyone, everyone, wall_recv).wait()


def near_and_exchange(devices, counts_t, fluid_state, wall_blocks, readers_t, targets_t):
    walls = wall_blocks.shape[0]
    vmem = pl.BlockSpec(memory_space=pltpu.VMEM)
    anywhere = pl.BlockSpec(memory_space=pl.ANY)
    hbm = pl.BlockSpec(memory_space=pltpu.HBM)
    return pl.pallas_call(
        lambda *refs: exchange_kernel(devices, *refs),
        out_shape=(
            jax.ShapeDtypeStruct((CA, PAIRS, 8, 128), F32),
            jax.ShapeDtypeStruct((CA, PAIRS, 16, 128), F32),
            jax.ShapeDtypeStruct((CA * CB, 2, 64, 128), BF16),
            jax.ShapeDtypeStruct((devices, 40, 128), F32),
        ),
        in_specs=[hbm] * 5,
        out_specs=[vmem, vmem, vmem, anywhere],
        scratch_shapes=[
            pltpu.SMEM(counts_t.shape, jnp.int32),
            pltpu.VMEM(fluid_state.shape, F32),
            pltpu.VMEM(wall_blocks.shape, F32),
            pltpu.VMEM(readers_t.shape, jnp.int32),
            pltpu.VMEM(targets_t.shape, jnp.int32),
            pltpu.VMEM((devices, 40, 128), F32),
            pltpu.VMEM((devices * SLOTS // 2, 2 * walls), BF16),
            pltpu.VMEM((2 * walls, 384), BF16),
            pltpu.VMEM((18, 6, 16, 128), F32),
            pltpu.VMEM((8, 128), F32),
            pltpu.VMEM((18, 6, 3, 64, 128), BF16),
            pltpu.VMEM((18, 6, 128, 128), BF16),
            pltpu.VMEM((18, PAIRS, 64, 128), BF16),
            pltpu.VMEM((18, 6, 8, 128), F32),
        ]
        + [
            pltpu.VMEM((576, 256), F32),
            pltpu.VMEM((3, 2, 256, 128), BF16),
            pltpu.VMEM((3, 2, 128, 128), BF16),
        ]
        * 2
        + [
            pltpu.SemaphoreType.DMA((5,)),
            pltpu.SemaphoreType.DMA,
            pltpu.SemaphoreType.DMA,
            pltpu.SemaphoreType.DMA,
            pltpu.SemaphoreType.DMA((8,)),
            pltpu.SemaphoreType.DMA((8,)),
        ],
        compiler_params=pltpu.CompilerParams(
            vmem_limit_bytes=26 << 20, collective_id=0, has_side_effects=True
        ),
        name="near_and_exchange",
    )(
        *[
            pltpu.with_memory_space_constraint(array, pltpu.HBM)
            for array in (counts_t, fluid_state, wall_blocks, readers_t, targets_t)
        ],
    )


UNROLL = 32


def wall_kernel(
    recv_ref,
    rec_ref,
    near_ref,
    side_ref,
    rates_ref,
    dens_ref,
    acc_ref,
    turn_ref,
    cells_ref,
    list_ref,
    sems,
):
    turn_ref[...] = recv_ref[:, 32, :].T[0:16].astype(jnp.int32)
    spread = pltpu.make_async_copy(turn_ref, cells_ref, sems.at[0])
    spread.start()
    spread.wait()
    lane1 = iota((1, 128), 1)
    left1 = lane1 < 64
    row8 = iota((8, 128), 0)
    left8 = iota((8, 128), 1) < 64
    zero8 = jnp.zeros((8, 128), F32)
    zero16 = jnp.zeros((16, 128), BF16)

    def listing(src, m):
        for q in range(SLOTS // 2):
            list_ref[m + q] = src * (SLOTS // 2) + q
        return m + (cells_ref[SLOTS, src] + 1) // 2

    def clear(a, m):
        for n in range(CB):
            acc_ref[0, a * CB + n] = zero8
            acc_ref[1, a * CB + n] = zero8
        for n in range(recv_ref.shape[0] // CA):
            m = listing(a * (recv_ref.shape[0] // CA) + n, m)
        return m

    live = lax.fori_loop(0, CA, clear, 0)
    for q in range(UNROLL):
        list_ref[live + q] = 0

    center = jnp.where(row8 == 2, 2.0, jnp.where(row8 < 2, 0.5, 0.0))

    def block(k, carry):
        ids, tiles, squares = [], [], []
        for u in range(UNROLL):
            at = k * UNROLL + u
            pair = list_ref[at]
            src = pair // (SLOTS // 2)
            q = pair - src * (SLOTS // 2)
            ids.append((cells_ref[2 * q, src], cells_ref[2 * q + 1, src]))
            tile = recv_ref[src, pl.ds(pl.multiple_of(q * 8, 8), 8), :]
            tiles.append(jnp.where(at < live, tile, 0.0))
        for u in range(0, UNROLL, 2):
            stacks = []
            for tile in tiles[u : u + 2]:
                c = tile - center
                sq = c * c
                norm = sq[0:1] + sq[1:2] + sq[2:3]
                rows = jnp.where(
                    row8 < 3, c, jnp.where(row8 == 3, norm, jnp.where(row8 == 4, 1.0, 0.0))
                )
                stacks += groups(*split3(rows), LEFT_ORDER) + [zero16]
            turned = jnp.concatenate(stacks, axis=0).T
            for side in range(2):
                right = jnp.concatenate(
                    [side_ref[ids[u][side], 0], side_ref[ids[u + 1][side], 1]], axis=0
                )
                squares.append(
                    jnp.dot(
                        turned[64 * side : 64 * side + 64], right, preferred_element_type=F32
                    )
                )
        weights = []
        for q2 in squares:
            q2 = jnp.maximum(q2, 1e-20)
            t = q2 * lax.rsqrt(q2)
            shell = jnp.maximum(1.0 - t, 0.0)
            shell = shell * shell
            weights.append(jnp.concatenate(split2(shell * shell * (4.0 * t + 1.0)), axis=0))
        outs = []
        for u in range(0, UNROLL, 2):
            rolled = [pltpu.roll(tile, 64, 1) for tile in tiles[u : u + 2]]
            for side in range(2):
                lines = []
                for tile, turn in zip(tiles[u : u + 2], rolled):
                    twice = jnp.where(left8, turn, tile) if side else jnp.where(left8, tile, turn)
                    high = twice.astype(BF16).astype(F32)
                    lines.append(jnp.concatenate([high, twice - high], axis=0).astype(BF16))
                outs.append(
                    jnp.dot(
                        jnp.concatenate(lines, axis=0),
                        weights[u + side],
                        preferred_element_type=F32,
                    )
                )
        for u in range(0, UNROLL, 2):
            for side in range(2):
                got = outs[u + side]
                for n in range(2):
                    cell = ids[u + n][side]
                    acc_ref[n, cell] = acc_ref[n, cell] + (
                        got[16 * n : 16 * n + 8] + got[16 * n + 8 : 16 * n + 16]
                    )
        return carry

    lax.fori_loop(0, (live + UNROLL - 1) // UNROLL, block, 0)

    def finish(a, carry):
        for p in range(PAIRS):
            one, two = a * CB + 2 * p, a * CB + 2 * p + 1
            total = jnp.where(
                left8,
                acc_ref[0, one] + pltpu.roll(acc_ref[1, one], 64, 1),
                pltpu.roll(acc_ref[0, two], 64, 1) + acc_ref[1, two],
            )
            tile = rec_ref[a, p]
            near = near_ref[a, p]
            h, sound = tile[10:11], tile[12:13]
            scale = KERN_W / (h * h * h)
            push = WALL_PUSH * sound * sound * scale
            heat = WALL_HEAT * scale * (total[7:8] - tile[11:12] * total[6:7])
            r = [near[1 + n : 2 + n] + push * total[3 + n : 4 + n] for n in range(3)]
            r.append(near[4:5] + heat)
            t = [pltpu.roll(line, 64, 1) for line in r]
            for v in range(2):
                lo, hi = 2 * v, 2 * v + 1
                span = slice(v * 128, (v + 1) * 128)
                rates_ref[a, 2 * p : 2 * p + 1, span] = jnp.where(left1, r[lo], t[hi])
                rates_ref[a, 2 * p + 1 : 2 * p + 2, span] = jnp.where(left1, t[lo], r[hi])
        return carry

    lax.fori_loop(0, CA, finish, 0)
    for p in range(PAIRS):
        dens_ref[:, p * 128 : (p + 1) * 128] = near_ref[:, p, 0, :]


def wall_terms(recv, records, near, sides):
    return pl.pallas_call(
        wall_kernel,
        out_shape=(
            jax.ShapeDtypeStruct((CA, CB, 256), F32),
            jax.ShapeDtypeStruct((CA, CB * 64), F32),
        ),
        in_specs=[pl.BlockSpec(memory_space=pltpu.VMEM)] * 4,
        out_specs=[pl.BlockSpec(memory_space=pltpu.VMEM)] * 2,
        scratch_shapes=[
            pltpu.VMEM((2, CA * CB, 8, 128), F32),
            pltpu.VMEM((16, recv.shape[0]), jnp.int32),
            pltpu.SMEM((16, recv.shape[0]), jnp.int32),
            pltpu.SMEM((recv.shape[0] * SLOTS // 2 + UNROLL + 8,), jnp.int32),
            pltpu.SemaphoreType.DMA((1,)),
        ],
        compiler_params=pltpu.CompilerParams(vmem_limit_bytes=10 << 20),
        name="wall_terms",
    )(recv, records, near, sides)


def local(fluid_state, cell_counts, wall_blocks, readers, targets):
    devices = lax.axis_size("gx") * lax.axis_size("gy")
    near, records, sides, recv = near_and_exchange(
        devices, cell_counts.T, fluid_state, wall_blocks, readers.T, targets.T
    )
    rates, density = wall_terms(recv, records, near, sides)
    return (rates, density)


def solution(mesh):
    placed = (
        P("gx", "gy", None),
        P("gx", "gy"),
        P(("gx", "gy"), None),
        P(("gx", "gy"), None),
        P(("gx", "gy"), None),
    )
    return jax.shard_map(
        local,
        mesh=mesh,
        in_specs=placed,
        out_specs=(P("gx", "gy", None), P("gx", "gy")),
        check_vma=False,
    )
```
